512 devices in a mesh: dom: 128 (over y, z, core), grp: 4 (over x).
Axes of the slice: x: 4, y: 8, z: 8, core: 2. Of those that a mesh axis runs over, the one named last changes fastest.
Arguments:
- right_side: float32 [512, 2, 80, 128], P(('dom', 'grp')), may hold values from -24 to 24
- absorption: float32 [512, 80, 128], P(('dom', 'grp')), may hold values from 0.5 to 4
- vertical: float32 [512, 2, 80, 128], P(('dom', 'grp')), may hold values from -1.5 to 0.3
- horizontal: float32 [512, 6, 80, 128], P(('dom', 'grp')), may hold values from -1 to 0.25
- neighbours: int32 [512, 6, 128], P(('dom', 'grp')), may hold values from 0 to 256, as said below
- send_index: int32 [512, 8, 16], P(('dom', 'grp')), may hold values from 0 to 127
- aggregate: int32 [512, 128], P(('dom', 'grp')), may hold values from 0 to 15, as said below
- weights: float32 [512, 80, 128], P(('dom', 'grp')), may hold values from 0.5 to 1.5
- coarse_vertical: float32 [512, 2, 80, 16], P(('dom', 'grp')), may hold values from -1.5 to 0.3
- coarse_horizontal: float32 [512, 6, 80, 16], P(('dom', 'grp')), may hold values from -1 to 0.25
- coarse_neighbours: int32 [512, 6, 16], P(('dom', 'grp')), may hold values from 0 to 144, as said below
Outputs:
- solution: float32 [512, 2, 80, 128], P(('dom', 'grp'))
The draws below stay inside these ranges and needn't reach their ends.
Inputs may be any that keep to these rules, and one draw needn't show every extreme that they name: `neighbours`: below 128 an entry names a column of the same partition (never the column itself); from 128 to 255 it names column i of ghost slot s as 128 + s * 16 + i; 256 is a padded slot that reads a zero cell. Each column has 3 to 6 live slots, the live ones first. `aggregate`: every coarse column of a partition has at least one fine column. `coarse_neighbours`: an entry (k + 4) * 16 + j names coarse column j of the partition k places away, k from -4 to 4, never the column itself; (9) * 16 is a padded slot that reads a zero cell. Each coarse column has 2 to 6 live slots, the live ones first.
All inputs are finite; a program needn't handle non-finite values.
Results may differ from the reference program's by a relative error of at most 0.0001.
Values sent between devices are 32-bit elements; how exact they have to be, the bound alone decides.
A program may use at most 64 MiB of HBM per device.

```python
import math
import jax
import jax.numpy as jnp
from jax import lax

LAYERS = 80
TRACERS = 2
C0 = 128
AGG = 8
G = 16
R = 4
NB = 6
NB1 = 6
CYCLES = 2
PRE = 2
POST = 2
CSWEEPS = 4
C1 = 16
PARTS_SIZE = 512


def draw_neighbours(key, part):
    keys = jax.random.split(jax.random.fold_in(key, 11), 4)
    shape = (PARTS_SIZE, NB, C0)
    column = lax.broadcasted_iota(jnp.int32, shape, 2)
    position = lax.broadcasted_iota(jnp.int32, shape, 1)
    counts = jax.random.randint(keys[0], (PARTS_SIZE, 1, C0), 3, NB + 1)
    counts = jnp.where(column == 0, 3, counts)
    remote = jax.random.randint(keys[1], shape, 0, 10) < 3
    local = (column + 1 + jax.random.randint(keys[2], shape, 0, C0 - 1)) % C0
    ghost = C0 + jax.random.randint(keys[3], shape, 0, 2 * R * G)
    chosen = jnp.where(remote, ghost, local)
    chosen = jnp.where(position < counts, chosen, C0 + 2 * R * G)
    chosen = jnp.where((column == 1) & (position == 0), 0, chosen)
    return chosen.astype(jnp.int32)


def draw_aggregate(key, part):
    coarse_count = C0 // AGG
    column = lax.broadcasted_iota(jnp.int32, (PARTS_SIZE, C0), 1)
    picked = jax.random.randint(jax.random.fold_in(key, 23), (PARTS_SIZE, C0), 0, coarse_count)
    return jnp.where(column < coarse_count, column, picked).astype(jnp.int32)


def draw_coarse_neighbours(key, part):
    coarse_count = C0 // AGG
    keys = jax.random.split(jax.random.fold_in(key, 37), 4)
    shape = (PARTS_SIZE, NB1, coarse_count)
    column = lax.broadcasted_iota(jnp.int32, shape, 2)
    position = lax.broadcasted_iota(jnp.int32, shape, 1)
    counts = jax.random.randint(keys[0], (PARTS_SIZE, 1, coarse_count), 2, NB1 + 1)
    counts = jnp.where(column == 0, 2, counts)
    distance = jax.random.randint(keys[1], shape, -R, R + 1)
    other = jax.random.randint(keys[2], shape, 0, coarse_count)
    beside = (column + 1 + jax.random.randint(keys[3], shape, 0, coarse_count - 1)) % coarse_count
    target = jnp.where(distance == 0, beside, other)
    chosen = (distance + R) * coarse_count + target
    chosen = jnp.where(position < counts, chosen, (2 * R + 1) * coarse_count)
    chosen = jnp.where((column == 1) & (position == 0), 0, chosen)
    return chosen.astype(jnp.int32)


def place_ends(entries, rng, least, largest):
    extent = entries.shape
    place = [jax.random.randint(jax.random.fold_in(rng, axis), (), 0, extent[axis]) for axis in range(len(extent))]
    entries = entries.at[tuple(place)].set(least)
    longest = extent.index(max(extent))
    place[longest] = (place[longest] + 1) % extent[longest]
    return entries.at[tuple(place)].set(largest)


def shard_levels(key, extent, cuts, smallest, high):
    loudness, own = 1.0, jax.random.fold_in(key, 6)
    for dim, blocks in cuts:
        steps = jnp.exp(jax.random.uniform(jax.random.fold_in(own, dim), (blocks,), jnp.float32, smallest / len(cuts), high / len(cuts)))
        loudness = loudness * jnp.repeat(steps, extent[dim] // blocks).reshape([-1 if axis == dim else 1 for axis in range(len(extent))])
    return loudness


def scatter_about(stream_key, dims, spread, most, cuts=(), held_as=jnp.bfloat16):
    entries = spread * jax.random.normal(stream_key, dims, jnp.float32)
    if cuts:
        entries = entries * shard_levels(stream_key, dims, cuts, -0.22, 0.18)
    return jnp.clip(entries, -most, most).astype(held_as)


def setup_inputs(seed: int = 0) -> dict:
    key_of = jax.random.split(jax.random.key(seed), 12)
    return {
        "right_side": scatter_about(key_of[0], (PARTS_SIZE, TRACERS, LAYERS, C0), 4.0, 24.0, ((0, 512),), jnp.float32),
        "absorption": jnp.clip(jnp.exp(math.log(4.0) - 2.0794415 * jax.random.uniform(key_of[1], (PARTS_SIZE, LAYERS, C0), jnp.float32) ** shard_levels(key_of[1], (PARTS_SIZE, LAYERS, C0), ((0, 512),), -0.2, 0.2)), 0.5, 4.0),
        "vertical": jnp.clip(-1.5 + 1.8 * jax.random.uniform(key_of[2], (PARTS_SIZE, 2, LAYERS, C0), jnp.float32) ** shard_levels(key_of[2], (PARTS_SIZE, 2, LAYERS, C0), ((0, 512),), -0.2, 0.2), -1.5, 0.3),
        "horizontal": jnp.clip(-1.0 + 1.25 * jax.random.uniform(key_of[3], (PARTS_SIZE, NB, LAYERS, C0), jnp.float32) ** shard_levels(key_of[3], (PARTS_SIZE, NB, LAYERS, C0), ((0, 512),), -0.2, 0.2), -1.0, 0.25),
        "neighbours": draw_neighbours(jax.random.fold_in(key_of[11], 71), 0),
        "send_index": place_ends(jax.random.randint(key_of[5], (PARTS_SIZE, 2 * R, G), 0, C0), jax.random.fold_in(key_of[5], 1), 0, C0 - 1).astype(jnp.int32),
        "aggregate": draw_aggregate(jax.random.fold_in(key_of[11], 71), 0),
        "weights": jnp.clip(0.5 + 1.0 * jax.random.uniform(key_of[7], (PARTS_SIZE, LAYERS, C0), jnp.float32) ** shard_levels(key_of[7], (PARTS_SIZE, LAYERS, C0), ((0, 512),), -0.2, 0.2), 0.5, 1.5),
        "coarse_vertical": jnp.clip(-1.5 + 1.8 * jax.random.uniform(key_of[8], (PARTS_SIZE, 2, LAYERS, C1), jnp.float32) ** shard_levels(key_of[8], (PARTS_SIZE, 2, LAYERS, C1), ((0, 512),), -0.2, 0.2), -1.5, 0.3),
        "coarse_horizontal": jnp.clip(-1.0 + 1.25 * jax.random.uniform(key_of[9], (PARTS_SIZE, NB1, LAYERS, C1), jnp.float32) ** shard_levels(key_of[9], (PARTS_SIZE, NB1, LAYERS, C1), ((0, 512),), -0.2, 0.2), -1.0, 0.25),
        "coarse_neighbours": draw_coarse_neighbours(jax.random.fold_in(key_of[11], 71), 0),
    }


OMEGA = 0.8


def part_shift(values, amount):
    if amount == 0:
        return values
    if amount > 0:
        return jnp.concatenate([jnp.zeros_like(values[:amount]), values[:-amount]], 0)
    return jnp.concatenate([values[-amount:], jnp.zeros_like(values[:-amount])], 0)


def layer_pair(tracer_field):
    zero_rim = jnp.zeros_like(tracer_field[:, :, :1])
    lower_layer = jnp.concatenate([zero_rim, tracer_field[:, :, :-1]], 2)
    upper_layer = jnp.concatenate([tracer_field[:, :, 1:], zero_rim], 2)
    return lower_layer, upper_layer


def apply_rows(tracer_field, extended, diagonal, vertical, horizontal, neighbours):
    lower_layer, upper_layer = layer_pair(tracer_field)
    totals = diagonal[:, None] * tracer_field + vertical[:, 0][:, None] * lower_layer + vertical[:, 1][:, None] * upper_layer
    target = tracer_field.shape
    for branch in range(neighbours.shape[1]):
        index_map = jnp.broadcast_to(neighbours[:, branch][:, None, None, :], target)
        totals = totals + horizontal[:, branch][:, None] * jnp.take_along_axis(extended, index_map, axis=3)
    return totals


def fine_extended(tracer_field, send_index):
    reach = send_index.shape[1] // 2
    offsets = list(range(1, reach + 1)) + [-distance for distance in range(1, reach + 1)]
    blocks = [tracer_field]
    for position, offset in enumerate(offsets):
        source = part_shift(tracer_field, offset)
        chosen = part_shift(send_index[:, position], offset)
        index_map = jnp.broadcast_to(chosen[:, None, None, :], source.shape[:3] + chosen.shape[1:])
        blocks.append(jnp.take_along_axis(source, index_map, axis=3))
    blocks.append(jnp.zeros_like(tracer_field[:, :, :, :1]))
    return jnp.concatenate(blocks, 3)


def coarse_extended(coarse_field, reach):
    blocks = [part_shift(coarse_field, -distance) for distance in range(-reach, reach + 1)]
    blocks.append(jnp.zeros_like(coarse_field[:, :, :, :1]))
    return jnp.concatenate(blocks, 3)


def reference(right_side, absorption, vertical, horizontal, neighbours, send_index, aggregate, weights, coarse_vertical, coarse_horizontal, coarse_neighbours):
    diagonal = absorption + jnp.abs(vertical[:, 0]) + jnp.abs(vertical[:, 1]) + jnp.sum(jnp.abs(horizontal), axis=1)
    coarse_diagonal = 0.5 + jnp.abs(coarse_vertical[:, 0]) + jnp.abs(coarse_vertical[:, 1]) + jnp.sum(jnp.abs(coarse_horizontal), axis=1)
    coarse_count = coarse_neighbours.shape[2]
    one_hot = (aggregate[:, :, None] == jnp.arange(coarse_count, dtype=jnp.int32)[None, None, :]).astype(jnp.float32)

    def fine_apply(tracer_field):
        return apply_rows(tracer_field, fine_extended(tracer_field, send_index), diagonal, vertical, horizontal, neighbours)

    def smooth(tracer_field):
        return tracer_field + OMEGA * (right_side - fine_apply(tracer_field)) / diagonal[:, None]

    solution = jnp.zeros_like(right_side)
    for cycle_index in range(CYCLES):
        for sweep_index in range(PRE):
            solution = smooth(solution)
        residual = right_side - fine_apply(solution)
        coarse_source = jnp.einsum('ptlc,pca->ptla', residual * weights[:, None], one_hot, precision=lax.Precision.HIGHEST)
        correction = OMEGA * coarse_source / coarse_diagonal[:, None]
        for sweep_index in range(CSWEEPS - 1):
            coarse_image = apply_rows(correction, coarse_extended(correction, R), coarse_diagonal, coarse_vertical, coarse_horizontal, coarse_neighbours)
            correction = correction + OMEGA * (coarse_source - coarse_image) / coarse_diagonal[:, None]
        solution = solution + jnp.einsum('ptla,pca->ptlc', correction, one_hot, precision=lax.Precision.HIGHEST) * weights[:, None]
        for sweep_index in range(POST):
            solution = smooth(solution)
    return solution
```

```python
import functools

import jax
import jax.numpy as jnp
from jax import lax
from jax.experimental import pallas as pl
from jax.experimental.pallas import tpu as pltpu
from jax.sharding import PartitionSpec as P

CYCLES = 2
PRE = 2
POST = 2
CSWEEPS = 4

OMEGA = 0.8
HIGHEST = lax.Precision.HIGHEST
MESH = pl.DeviceIdType.MESH
LANES = 128


def mm(a, b):
    return jnp.dot(a, b, precision=HIGHEST, preferred_element_type=jnp.float32)


def vcycle_kernel(
    n_parts,
    n_grp,
    reach,
    width,
    rhs_ref,
    diag_ref,
    v0_ref,
    v1_ref,
    h_ref,
    w_ref,
    mt_ref,
    st_ref,
    at_ref,
    a_ref,
    mct_ref,
    cdiag_ref,
    cv0_ref,
    cv1_ref,
    ch_ref,
    out_ref,
    ext,
    sendbuf,
    cext,
    send_sem,
    recv_sem,
    csend_sem,
    crecv_sem,
):
    me = lax.axis_index("dom") * n_grp + lax.axis_index("grp")
    offsets = list(range(1, reach + 1)) + [-d for d in range(1, reach + 1)]
    columns = mt_ref.shape[1] // 2
    c1 = cdiag_ref.shape[0]
    n_slots = len(offsets)

    def valid(q):
        return jnp.logical_and(q >= 0, q < n_parts)

    def device(q):
        return (lax.div(q, n_grp), lax.rem(q, n_grp))

    ext[...] = jnp.zeros_like(ext)
    cext[...] = jnp.zeros_like(cext)

    barrier = pltpu.get_barrier_semaphore()
    for d in offsets:
        @pl.when(valid(me + d))
        def _():
            pl.semaphore_signal(barrier, 1, device_id=device(me + d), device_id_type=MESH)
    peers = sum(valid(me + d).astype(jnp.int32) for d in offsets)
    pl.semaphore_wait(barrier, peers)

    lane = lax.broadcasted_iota(jnp.int32, (8, LANES), 1)
    probe = pltpu.roll(lane, 1, 1)
    expected = jnp.where(lane == 0, LANES - 1, lane - 1)
    forward = (probe == expected)[0:1, :]

    def shifted(x):
        a = pltpu.roll(x, 1, 1)
        b = pltpu.roll(x, LANES - 1, 1)
        lower = jnp.where(forward, a, b)
        upper = jnp.where(forward, b, a)
        return lower, upper

    diag = diag_ref[...]
    v0 = v0_ref[...]
    v1 = v1_ref[...]
    w = w_ref[...]
    cdiag = cdiag_ref[...]
    cv0 = cv0_ref[...]
    cv1 = cv1_ref[...]
    rhs = rhs_ref[...]

    def halves(x):
        return [x[:, t * LANES:(t + 1) * LANES] for t in range(x.shape[1] // LANES)]

    def fine_copy(slot, s):
        rows = pl.ds(s * width, width)
        return pltpu.make_async_remote_copy(
            src_ref=sendbuf.at[rows],
            dst_ref=ext.at[slot, pl.ds(columns + s * width, width)],
            send_sem=send_sem.at[s],
            recv_sem=recv_sem.at[slot, s],
            device_id=device(me + offsets[s]),
            device_id_type=MESH,
        )

    fine_round = [0]

    def fine_apply(field):
        slot = fine_round[0] % 2
        fine_round[0] += 1
        sendbuf[...] = mm(st_ref[...], field)
        for s in range(n_slots):
            @pl.when(valid(me + offsets[s]))
            def _():
                fine_copy(slot, s).start()
        ext[slot, pl.ds(0, columns), :] = field
        for s in range(n_slots):
            @pl.when(valid(me + offsets[s]))
            def _():
                fine_copy(slot, s).wait_send()

            @pl.when(valid(me - offsets[s]))
            def _():
                fine_copy(slot, s).wait_recv()
        gathered = mm(mt_ref[...], ext[slot])
        totals = []
        for t, part in enumerate(halves(field)):
            lower, upper = shifted(part)
            total = diag * part + v0 * lower + v1 * upper
            for n in range(h_ref.shape[0]):
                total = total + h_ref[n] * gathered[n * columns:(n + 1) * columns, t * LANES:(t + 1) * LANES]
            totals.append(total)
        return jnp.concatenate(totals, 1)

    def coarse_copy(slot, k):
        d = offsets[k]
        return pltpu.make_async_remote_copy(
            src_ref=cext.at[slot, pl.ds(reach * c1, c1)],
            dst_ref=cext.at[slot, pl.ds((reach - d) * c1, c1)],
            send_sem=csend_sem.at[k],
            recv_sem=crecv_sem.at[slot, k],
            device_id=device(me + d),
            device_id_type=MESH,
        )

    coarse_round = [0]

    def coarse_apply(corr):
        slot = coarse_round[0] % 2
        coarse_round[0] += 1
        cext[slot, pl.ds(reach * c1, c1), :] = corr
        for k in range(n_slots):
            @pl.when(valid(me + offsets[k]))
            def _():
                coarse_copy(slot, k).start()
        for k in range(n_slots):
            @pl.when(valid(me + offsets[k]))
            def _():
                coarse_copy(slot, k).wait_send()

            @pl.when(valid(me - offsets[k]))
            def _():
                coarse_copy(slot, k).wait_recv()
        gathered = mm(mct_ref[...], cext[slot])
        totals = []
        for t, part in enumerate(halves(corr)):
            lower, upper = shifted(part)
            total = cdiag * part + cv0 * lower + cv1 * upper
            for n in range(ch_ref.shape[0]):
                total = total + ch_ref[n] * gathered[n * c1:(n + 1) * c1, t * LANES:(t + 1) * LANES]
            totals.append(total)
        return jnp.concatenate(totals, 1)

    def per_half(x, coeff, op):
        return jnp.concatenate([op(part, coeff) for part in halves(x)], 1)

    solution = per_half(OMEGA * rhs, diag, lambda x, c: x / c)
    for cycle_index in range(CYCLES):
        for sweep_index in range(PRE):
            if cycle_index == 0 and sweep_index == 0:
                continue
            step = OMEGA * (rhs - fine_apply(solution))
            solution = solution + per_half(step, diag, lambda x, c: x / c)
        residual = rhs - fine_apply(solution)
        weighted = per_half(residual, w, lambda x, c: x * c)
        coarse_source = mm(at_ref[...], weighted)
        correction = per_half(OMEGA * coarse_source, cdiag, lambda x, c: x / c)
        for coarse_sweep_index in range(CSWEEPS - 1):
            step = OMEGA * (coarse_source - coarse_apply(correction))
            correction = correction + per_half(step, cdiag, lambda x, c: x / c)
        lifted = mm(a_ref[...], correction)
        solution = solution + per_half(lifted, w, lambda x, c: x * c)
        for sweep_index in range(POST):
            step = OMEGA * (rhs - fine_apply(solution))
            solution = solution + per_half(step, diag, lambda x, c: x / c)
    out_ref[...] = solution


def to_lanes(x, fill=0.0):
    layers = x.shape[-2]
    moved = jnp.moveaxis(x, -1, 0)
    pad = [(0, 0)] * (moved.ndim - 1) + [(0, LANES - layers)]
    padded = jnp.pad(moved, pad, constant_values=fill)
    return padded.reshape(padded.shape[0], -1)


def body(
    right_side,
    absorption,
    vertical,
    horizontal,
    neighbours,
    send_index,
    aggregate,
    weights,
    coarse_vertical,
    coarse_horizontal,
    coarse_neighbours,
    *,
    n_parts,
    n_grp,
):
    rhs = right_side[0]
    vertical_rows = vertical[0]
    horizontal_rows = horizontal[0]
    tracers, layers, columns = rhs.shape
    diagonal = (
        absorption[0]
        + jnp.abs(vertical_rows[0])
        + jnp.abs(vertical_rows[1])
        + jnp.sum(jnp.abs(horizontal_rows), axis=0)
    )
    cvert = coarse_vertical[0]
    chor = coarse_horizontal[0]
    coarse_diagonal = (
        0.5 + jnp.abs(cvert[0]) + jnp.abs(cvert[1]) + jnp.sum(jnp.abs(chor), axis=0)
    )
    layer = lax.broadcasted_iota(jnp.int32, (layers, 1), 0)
    v0 = jnp.where(layer == 0, 0.0, vertical_rows[0])
    v1 = jnp.where(layer == layers - 1, 0.0, vertical_rows[1])
    cv0 = jnp.where(layer == 0, 0.0, cvert[0])
    cv1 = jnp.where(layer == layers - 1, 0.0, cvert[1])

    reach = send_index.shape[1] // 2
    width = send_index.shape[2]
    c1 = coarse_neighbours.shape[2]
    nb = neighbours[0]
    n_nb = nb.shape[0]
    ext_rows = columns + 2 * reach * width
    mt = (nb.reshape(-1)[:, None] == jnp.arange(ext_rows, dtype=jnp.int32)[None, :]).astype(jnp.float32)
    st = (send_index[0].reshape(-1)[:, None] == jnp.arange(columns, dtype=jnp.int32)[None, :]).astype(jnp.float32)
    at = (aggregate[0][None, :] == jnp.arange(c1, dtype=jnp.int32)[:, None]).astype(jnp.float32)
    a = at.T
    coarse_rows = (2 * reach + 1) * c1
    mct = (coarse_neighbours[0].reshape(-1)[:, None] == jnp.arange(coarse_rows, dtype=jnp.int32)[None, :]).astype(jnp.float32)

    args = (
        to_lanes(rhs),
        to_lanes(diagonal, 1.0),
        to_lanes(v0),
        to_lanes(v1),
        jnp.stack([to_lanes(horizontal_rows[n]) for n in range(horizontal_rows.shape[0])]),
        to_lanes(weights[0]),
        mt,
        st,
        at,
        a,
        mct,
        to_lanes(coarse_diagonal, 1.0),
        to_lanes(cv0),
        to_lanes(cv1),
        jnp.stack([to_lanes(chor[n]) for n in range(chor.shape[0])]),
    )
    n_slots = 2 * reach
    out = pl.pallas_call(
        functools.partial(vcycle_kernel, n_parts, n_grp, reach, width),
        out_shape=jax.ShapeDtypeStruct((columns, tracers * LANES), jnp.float32),
        in_specs=[pl.BlockSpec(memory_space=pltpu.VMEM)] * len(args),
        out_specs=pl.BlockSpec(memory_space=pltpu.VMEM),
        scratch_shapes=[
            pltpu.VMEM((2, ext_rows, tracers * LANES), jnp.float32),
            pltpu.VMEM((n_slots * width, tracers * LANES), jnp.float32),
            pltpu.VMEM((2, coarse_rows, tracers * LANES), jnp.float32),
            pltpu.SemaphoreType.DMA((n_slots,)),
            pltpu.SemaphoreType.DMA((2, n_slots)),
            pltpu.SemaphoreType.DMA((n_slots,)),
            pltpu.SemaphoreType.DMA((2, n_slots)),
        ],
        compiler_params=pltpu.CompilerParams(collective_id=0, has_side_effects=True),
    )(*args)
    result = out.reshape(columns, tracers, LANES)[:, :, :layers]
    return jnp.transpose(result, (1, 2, 0))[None]


def solution(mesh):
    placed = (
        P(("dom", "grp"), None, None, None),
        P(("dom", "grp"), None, None),
        P(("dom", "grp"), None, None, None),
        P(("dom", "grp"), None, None, None),
        P(("dom", "grp"), None, None),
        P(("dom", "grp"), None, None),
        P(("dom", "grp"), None),
        P(("dom", "grp"), None, None),
        P(("dom", "grp"), None, None, None),
        P(("dom", "grp"), None, None, None),
        P(("dom", "grp"), None, None),
    )
    n_grp = mesh.shape["grp"]
    n_parts = mesh.shape["dom"] * n_grp
    return jax.shard_map(
        functools.partial(body, n_parts=n_parts, n_grp=n_grp),
        mesh=mesh,
        in_specs=placed,
        out_specs=P(("dom", "grp"), None, None, None),
        check_vma=False,
    )
```

```python
import functools

import jax
import jax.numpy as jnp
from jax import lax
from jax.experimental import pallas as pl
from jax.experimental.pallas import tpu as pltpu
from jax.sharding import PartitionSpec as P

CYCLES = 2
PRE = 2
POST = 2
CSWEEPS = 4

OMEGA = 0.8
HIGHEST = lax.Precision.HIGHEST
MESH = pl.DeviceIdType.MESH
LANES = 128
F32 = jnp.float32


def mm(a, b):
    return jnp.dot(a, b, precision=HIGHEST, preferred_element_type=F32)


def vcycle_kernel(
    n_parts,
    n_grp,
    reach,
    width,
    rhs_hbm,
    absorption_hbm,
    vertical_hbm,
    horizontal_hbm,
    weights_hbm,
    nb_hbm,
    si_hbm,
    agg_hbm,
    cnb_hbm,
    cprep_hbm,
    out_hbm,
    rhs_v,
    absorption_v,
    vertical_v,
    horizontal_v,
    weights_v,
    nb_v,
    si_v,
    agg_v,
    cnb_v,
    cprep_v,
    out_v,
    load_sem,
    mt_s,
    ghost,
    sendbuf,
    cext,
    send_sem,
    recv_sem,
    csend_sem,
    crecv_sem,
):
    me = lax.axis_index("dom") * n_grp + lax.axis_index("grp")
    offsets = list(range(1, reach + 1)) + [-d for d in range(1, reach + 1)]
    n_slots = len(offsets)
    tracers, layers, columns = rhs_v.shape[1:]
    n_nb = nb_v.shape[0]
    c1 = cprep_v.shape[1]
    n_ch = cprep_v.shape[0] - 3
    halo = n_slots * width

    def valid(q):
        return jnp.logical_and(q >= 0, q < n_parts)

    def device(q):
        return (lax.div(q, n_grp), lax.rem(q, n_grp))

    loads = [
        pltpu.make_async_copy(src, dst, load_sem.at[i])
        for i, (src, dst) in enumerate(
            [
                (rhs_hbm, rhs_v),
                (absorption_hbm, absorption_v),
                (vertical_hbm, vertical_v),
                (horizontal_hbm, horizontal_v),
                (weights_hbm, weights_v),
                (nb_hbm, nb_v),
                (si_hbm, si_v),
                (agg_hbm, agg_v),
                (cnb_hbm, cnb_v),
                (cprep_hbm, cprep_v),
            ]
        )
    ]
    for copy in loads:
        copy.start()

    ghost[...] = jnp.zeros_like(ghost)
    cext[...] = jnp.zeros_like(cext)

    barrier = pltpu.get_barrier_semaphore()
    for d in offsets:
        @pl.when(valid(me + d))
        def _():
            pl.semaphore_signal(barrier, 1, device_id=device(me + d), device_id_type=MESH)
    peers = sum(valid(me + d).astype(jnp.int32) for d in offsets)
    pl.semaphore_wait(barrier, peers)

    for copy in loads:
        copy.wait()

    lane = lax.broadcasted_iota(jnp.int32, (8, LANES), 1)
    probe = pltpu.roll(lane, 1, 1)
    expected = jnp.where(lane == 0, LANES - 1, lane - 1)
    forward = (probe == expected)[0:1, :]
    layer_lane = lax.broadcasted_iota(jnp.int32, (1, LANES), 1)
    live = layer_lane < layers

    def shifted(x):
        a = pltpu.roll(x, 1, 1)
        b = pltpu.roll(x, LANES - 1, 1)
        lower = jnp.where(forward, a, b)
        upper = jnp.where(forward, b, a)
        return lower, upper

    pad_rows = jnp.zeros((LANES - layers, columns), F32)

    def to_cols(slab):
        return jnp.transpose(jnp.concatenate([slab, pad_rows], 0))

    ab = absorption_v[0]
    vr0 = vertical_v[0, 0]
    vr1 = vertical_v[0, 1]
    diag_rows = ab + jnp.abs(vr0) + jnp.abs(vr1)
    hsum = jnp.abs(horizontal_v[0, 0])
    for n in range(1, horizontal_v.shape[1]):
        hsum = hsum + jnp.abs(horizontal_v[0, n])
    diag_rows = diag_rows + hsum
    diag = jnp.where(live, to_cols(diag_rows), 1.0)
    v0 = jnp.where(layer_lane == 0, 0.0, to_cols(vr0))
    v1 = jnp.where(layer_lane == layers - 1, 0.0, to_cols(vr1))
    h = [to_cols(horizontal_v[0, n]) for n in range(horizontal_v.shape[1])]
    w = to_cols(weights_v[0])
    rhs = jnp.concatenate([to_cols(rhs_v[0, t]) for t in range(tracers)], 1)

    ext_rows = columns + halo
    k_iota = lax.broadcasted_iota(jnp.int32, (ext_rows, columns), 0)
    for n in range(n_nb):
        chosen = (k_iota == nb_v[n:n + 1, :]).astype(F32)
        mt_s[pl.ds(n * columns, columns), :] = jnp.transpose(chosen)
    st = jnp.transpose((lax.broadcasted_iota(jnp.int32, (columns, halo), 0) == si_v[...]).astype(F32))
    at = (lax.broadcasted_iota(jnp.int32, (c1, columns), 0) == agg_v[...]).astype(F32)
    a_full = jnp.transpose((lax.broadcasted_iota(jnp.int32, (LANES, columns), 0) == agg_v[...]).astype(F32))
    a = a_full[:, :c1]
    coarse_rows = cext.shape[1]
    n_crow = n_ch * c1
    mct = jnp.transpose(
        (lax.broadcasted_iota(jnp.int32, (coarse_rows, cnb_v.shape[1]), 0) == cnb_v[...]).astype(F32)
    )[:n_crow]

    cdiag = cprep_v[0]
    cv0 = cprep_v[1]
    cv1 = cprep_v[2]

    def halves(x):
        return [x[:, t * LANES:(t + 1) * LANES] for t in range(x.shape[1] // LANES)]

    def fine_copy(slot, s):
        rows = pl.ds(s * width, width)
        return pltpu.make_async_remote_copy(
            src_ref=sendbuf.at[rows],
            dst_ref=ghost.at[slot, rows],
            send_sem=send_sem.at[s],
            recv_sem=recv_sem.at[slot, s],
            device_id=device(me + offsets[s]),
            device_id_type=MESH,
        )

    fine_round = [0]

    def fine_apply(field):
        slot = fine_round[0] % 2
        fine_round[0] += 1
        sendbuf[...] = mm(st, field)
        for s in range(n_slots):
            @pl.when(valid(me + offsets[s]))
            def _():
                fine_copy(slot, s).start()
        local = mm(mt_s[:, pl.ds(0, columns)], field)
        bases = []
        for part in halves(field):
            lower, upper = shifted(part)
            bases.append(diag * part + v0 * lower + v1 * upper)
        for s in range(n_slots):
            @pl.when(valid(me + offsets[s]))
            def _():
                fine_copy(slot, s).wait_send()

            @pl.when(valid(me - offsets[s]))
            def _():
                fine_copy(slot, s).wait_recv()
        gathered = local + mm(mt_s[:, pl.ds(columns, halo)], ghost[slot])
        totals = []
        for t, total in enumerate(bases):
            for n in range(n_nb):
                total = total + h[n] * gathered[n * columns:(n + 1) * columns, t * LANES:(t + 1) * LANES]
            totals.append(total)
        return jnp.concatenate(totals, 1)

    def coarse_copy(slot, k):
        d = offsets[k]
        return pltpu.make_async_remote_copy(
            src_ref=cext.at[slot, pl.ds(reach * c1, c1)],
            dst_ref=cext.at[slot, pl.ds((reach - d) * c1, c1)],
            send_sem=csend_sem.at[k],
            recv_sem=crecv_sem.at[slot, k],
            device_id=device(me + d),
            device_id_type=MESH,
        )

    coarse_round = [0]

    def coarse_apply(corr):
        slot = coarse_round[0] % 2
        coarse_round[0] += 1
        cext[slot, pl.ds(reach * c1, c1), :] = corr
        for k in range(n_slots):
            @pl.when(valid(me + offsets[k]))
            def _():
                coarse_copy(slot, k).start()
        bases = []
        for part in halves(corr):
            lower, upper = shifted(part)
            bases.append(cdiag * part + cv0 * lower + cv1 * upper)
        for k in range(n_slots):
            @pl.when(valid(me + offsets[k]))
            def _():
                coarse_copy(slot, k).wait_send()

            @pl.when(valid(me - offsets[k]))
            def _():
                coarse_copy(slot, k).wait_recv()
        gathered = mm(mct, cext[slot])
        totals = []
        for t, total in enumerate(bases):
            for n in range(n_ch):
                total = total + cprep_v[3 + n] * gathered[n * c1:(n + 1) * c1, t * LANES:(t + 1) * LANES]
            totals.append(total)
        return jnp.concatenate(totals, 1)

    def per_half(x, coeff, op):
        return jnp.concatenate([op(part, coeff) for part in halves(x)], 1)

    solution = per_half(OMEGA * rhs, diag, lambda x, c: x / c)
    for cycle_index in range(CYCLES):
        for sweep_index in range(PRE):
            if cycle_index == 0 and sweep_index == 0:
                continue
            step = OMEGA * (rhs - fine_apply(solution))
            solution = solution + per_half(step, diag, lambda x, c: x / c)
        residual = rhs - fine_apply(solution)
        weighted = per_half(residual, w, lambda x, c: x * c)
        coarse_source = mm(at, weighted)
        correction = per_half(OMEGA * coarse_source, cdiag, lambda x, c: x / c)
        for coarse_sweep_index in range(CSWEEPS - 1):
            step = OMEGA * (coarse_source - coarse_apply(correction))
            correction = correction + per_half(step, cdiag, lambda x, c: x / c)
        lifted = mm(a, correction)
        solution = solution + per_half(lifted, w, lambda x, c: x * c)
        for sweep_index in range(POST):
            step = OMEGA * (rhs - fine_apply(solution))
            solution = solution + per_half(step, diag, lambda x, c: x / c)
    for t, part in enumerate(halves(solution)):
        out_v[0, t] = jnp.transpose(part)[:layers]
    store = pltpu.make_async_copy(out_v, out_hbm, load_sem.at[len(loads)])
    store.start()
    store.wait()


def body(
    right_side,
    absorption,
    vertical,
    horizontal,
    neighbours,
    send_index,
    aggregate,
    weights,
    coarse_vertical,
    coarse_horizontal,
    coarse_neighbours,
    *,
    n_parts,
    n_grp,
):
    _, tracers, layers, columns = right_side.shape
    reach = send_index.shape[1] // 2
    width = send_index.shape[2]
    c1 = coarse_neighbours.shape[2]
    n_slots = 2 * reach

    cvert = coarse_vertical[0]
    chor = coarse_horizontal[0]
    coarse_diagonal = (
        0.5 + jnp.abs(cvert[0]) + jnp.abs(cvert[1]) + jnp.sum(jnp.abs(chor), axis=0)
    )
    layer = lax.broadcasted_iota(jnp.int32, (layers, 1), 0)
    cv0 = jnp.where(layer == 0, 0.0, cvert[0])
    cv1 = jnp.where(layer == layers - 1, 0.0, cvert[1])
    stacked = jnp.concatenate([coarse_diagonal[None], cv0[None], cv1[None], chor], 0)
    fill = jnp.concatenate(
        [
            jnp.ones((1, c1, LANES - layers), F32),
            jnp.zeros((2 + chor.shape[0], c1, LANES - layers), F32),
        ],
        0,
    )
    cprep = jnp.concatenate([jnp.transpose(stacked, (0, 2, 1)), fill], 2)

    si = send_index.reshape(1, n_slots * width)
    n_crow = coarse_neighbours.shape[1] * c1
    cnb = jnp.pad(
        coarse_neighbours.reshape(1, n_crow), ((0, 0), (0, LANES - n_crow)), constant_values=-1
    )

    args = (right_side, absorption, vertical, horizontal, weights, neighbours[0], si, aggregate, cnb, cprep)
    ext_rows = columns + n_slots * width
    coarse_rows = ext_rows
    scratch = [pltpu.VMEM(x.shape, x.dtype) for x in args] + [
        pltpu.VMEM(right_side.shape, F32),
        pltpu.SemaphoreType.DMA((len(args) + 1,)),
        pltpu.VMEM((neighbours.shape[1] * columns, ext_rows), F32),
        pltpu.VMEM((2, n_slots * width, tracers * LANES), F32),
        pltpu.VMEM((n_slots * width, tracers * LANES), F32),
        pltpu.VMEM((2, coarse_rows, tracers * LANES), F32),
        pltpu.SemaphoreType.DMA((n_slots,)),
        pltpu.SemaphoreType.DMA((2, n_slots)),
        pltpu.SemaphoreType.DMA((n_slots,)),
        pltpu.SemaphoreType.DMA((2, n_slots)),
    ]
    return pl.pallas_call(
        functools.partial(vcycle_kernel, n_parts, n_grp, reach, width),
        out_shape=jax.ShapeDtypeStruct(right_side.shape, F32),
        in_specs=[pl.BlockSpec(memory_space=pl.ANY)] * len(args),
        out_specs=pl.BlockSpec(memory_space=pl.ANY),
        scratch_shapes=scratch,
        compiler_params=pltpu.CompilerParams(collective_id=0, has_side_effects=True),
    )(*args)


def solution(mesh):
    placed = (
        P(("dom", "grp"), None, None, None),
        P(("dom", "grp"), None, None),
        P(("dom", "grp"), None, None, None),
        P(("dom", "grp"), None, None, None),
        P(("dom", "grp"), None, None),
        P(("dom", "grp"), None, None),
        P(("dom", "grp"), None),
        P(("dom", "grp"), None, None),
        P(("dom", "grp"), None, None, None),
        P(("dom", "grp"), None, None, None),
        P(("dom", "grp"), None, None),
    )
    n_grp = mesh.shape["grp"]
    n_parts = mesh.shape["dom"] * n_grp
    return jax.shard_map(
        functools.partial(body, n_parts=n_parts, n_grp=n_grp),
        mesh=mesh,
        in_specs=placed,
        out_specs=P(("dom", "grp"), None, None, None),
        check_vma=False,
    )
```

```python
import functools

import jax
import jax.numpy as jnp
from jax import lax
from jax.experimental import pallas as pl
from jax.experimental.pallas import tpu as pltpu
from jax.sharding import PartitionSpec as P

CYCLES = 2
PRE = 2
POST = 2
CSWEEPS = 4

OMEGA = 0.8
HIGHEST = lax.Precision.HIGHEST
MESH = pl.DeviceIdType.MESH
LANES = 128
F32 = jnp.float32
BF16 = jnp.bfloat16


def mm(a, b):
    return jnp.dot(a, b, precision=HIGHEST, preferred_element_type=F32)


def select(onehot, x):
    hi = x.astype(BF16)
    rest = x - hi.astype(F32)
    mid = rest.astype(BF16)
    lo = (rest - mid.astype(F32)).astype(BF16)
    part = lambda y: jnp.dot(onehot, y, preferred_element_type=F32)
    return (part(hi) + part(mid)) + part(lo)


def vcycle_kernel(
    n_parts,
    n_grp,
    reach,
    width,
    rhs_hbm,
    absorption_hbm,
    vertical_hbm,
    horizontal_hbm,
    weights_hbm,
    nb_hbm,
    si_hbm,
    agg_hbm,
    cnb_hbm,
    cprep_hbm,
    out_hbm,
    rhs_v,
    absorption_v,
    vertical_v,
    horizontal_v,
    weights_v,
    nb_v,
    si_v,
    agg_v,
    cnb_v,
    cprep_v,
    out_v,
    load_sem,
    mt_s,
    ghost,
    sendbuf,
    cext,
    send_sem,
    recv_sem,
    csend_sem,
    crecv_sem,
):
    me = lax.axis_index("dom") * n_grp + lax.axis_index("grp")
    offsets = list(range(1, reach + 1)) + [-d for d in range(1, reach + 1)]
    n_slots = len(offsets)
    tracers, layers, columns = rhs_v.shape[1:]
    n_nb = nb_v.shape[0]
    c1 = cprep_v.shape[1]
    n_ch = cprep_v.shape[0] - 3
    halo = n_slots * width

    def valid(q):
        return jnp.logical_and(q >= 0, q < n_parts)

    def device(q):
        return (lax.div(q, n_grp), lax.rem(q, n_grp))

    loads = [
        pltpu.make_async_copy(src, dst, load_sem.at[i])
        for i, (src, dst) in enumerate(
            [
                (rhs_hbm, rhs_v),
                (absorption_hbm, absorption_v),
                (vertical_hbm, vertical_v),
                (horizontal_hbm, horizontal_v),
                (weights_hbm, weights_v),
                (nb_hbm, nb_v),
                (si_hbm, si_v),
                (agg_hbm, agg_v),
                (cnb_hbm, cnb_v),
                (cprep_hbm, cprep_v),
            ]
        )
    ]
    for copy in loads:
        copy.start()

    ghost[...] = jnp.zeros_like(ghost)
    cext[...] = jnp.zeros_like(cext)

    barrier = pltpu.get_barrier_semaphore()
    for d in offsets:
        @pl.when(valid(me + d))
        def _():
            pl.semaphore_signal(barrier, 1, device_id=device(me + d), device_id_type=MESH)
    peers = sum(valid(me + d).astype(jnp.int32) for d in offsets)
    pl.semaphore_wait(barrier, peers)

    for copy in loads:
        copy.wait()

    lane = lax.broadcasted_iota(jnp.int32, (8, LANES), 1)
    probe = pltpu.roll(lane, 1, 1)
    expected = jnp.where(lane == 0, LANES - 1, lane - 1)
    forward = (probe == expected)[0:1, :]
    layer_lane = lax.broadcasted_iota(jnp.int32, (1, LANES), 1)
    live = layer_lane < layers

    def shifted(x):
        a = pltpu.roll(x, 1, 1)
        b = pltpu.roll(x, LANES - 1, 1)
        lower = jnp.where(forward, a, b)
        upper = jnp.where(forward, b, a)
        return lower, upper

    pad_rows = jnp.zeros((LANES - layers, columns), F32)

    def to_cols(slab):
        return jnp.transpose(jnp.concatenate([slab, pad_rows], 0))

    ab = absorption_v[0]
    vr0 = vertical_v[0, 0]
    vr1 = vertical_v[0, 1]
    diag_rows = ab + jnp.abs(vr0) + jnp.abs(vr1)
    hsum = jnp.abs(horizontal_v[0, 0])
    for n in range(1, horizontal_v.shape[1]):
        hsum = hsum + jnp.abs(horizontal_v[0, n])
    diag_rows = diag_rows + hsum
    diag = jnp.where(live, to_cols(diag_rows), 1.0)
    v0 = jnp.where(layer_lane == 0, 0.0, to_cols(vr0))
    v1 = jnp.where(layer_lane == layers - 1, 0.0, to_cols(vr1))
    h = [to_cols(horizontal_v[0, n]) for n in range(horizontal_v.shape[1])]
    w = to_cols(weights_v[0])
    rhs = jnp.concatenate([to_cols(rhs_v[0, t]) for t in range(tracers)], 1)

    ext_rows = columns + halo
    k_iota = lax.broadcasted_iota(jnp.int32, (ext_rows, columns), 0)
    for n in range(n_nb):
        chosen = (k_iota == nb_v[n:n + 1, :]).astype(F32)
        mt_s[pl.ds(n * columns, columns), :] = jnp.transpose(chosen).astype(BF16)
    st = jnp.transpose((lax.broadcasted_iota(jnp.int32, (columns, halo), 0) == si_v[...]).astype(F32)).astype(BF16)
    at = (lax.broadcasted_iota(jnp.int32, (c1, columns), 0) == agg_v[...]).astype(F32)
    a_full = jnp.transpose((lax.broadcasted_iota(jnp.int32, (LANES, columns), 0) == agg_v[...]).astype(F32))
    a = a_full[:, :c1]
    coarse_rows = cext.shape[1]
    n_crow = n_ch * c1
    mct = jnp.transpose(
        (lax.broadcasted_iota(jnp.int32, (coarse_rows, cnb_v.shape[1]), 0) == cnb_v[...]).astype(F32)
    )[:n_crow].astype(BF16)

    cdiag = cprep_v[0]
    cv0 = cprep_v[1]
    cv1 = cprep_v[2]

    def halves(x):
        return [x[:, t * LANES:(t + 1) * LANES] for t in range(x.shape[1] // LANES)]

    def fine_copy(slot, s):
        rows = pl.ds(s * width, width)
        return pltpu.make_async_remote_copy(
            src_ref=sendbuf.at[rows],
            dst_ref=ghost.at[slot, rows],
            send_sem=send_sem.at[s],
            recv_sem=recv_sem.at[slot, s],
            device_id=device(me + offsets[s]),
            device_id_type=MESH,
        )

    fine_round = [0]

    def fine_apply(field):
        slot = fine_round[0] % 2
        fine_round[0] += 1
        sendbuf[...] = select(st, field)
        for s in range(n_slots):
            @pl.when(valid(me + offsets[s]))
            def _():
                fine_copy(slot, s).start()
        local = select(mt_s[:, pl.ds(0, columns)], field)
        bases = []
        for part in halves(field):
            lower, upper = shifted(part)
            bases.append(diag * part + v0 * lower + v1 * upper)
        for s in range(n_slots):
            @pl.when(valid(me + offsets[s]))
            def _():
                fine_copy(slot, s).wait_send()

            @pl.when(valid(me - offsets[s]))
            def _():
                fine_copy(slot, s).wait_recv()
        gathered = local + select(mt_s[:, pl.ds(columns, halo)], ghost[slot])
        totals = []
        for t, total in enumerate(bases):
            for n in range(n_nb):
                total = total + h[n] * gathered[n * columns:(n + 1) * columns, t * LANES:(t + 1) * LANES]
            totals.append(total)
        return jnp.concatenate(totals, 1)

    def coarse_copy(slot, k):
        d = offsets[k]
        return pltpu.make_async_remote_copy(
            src_ref=cext.at[slot, pl.ds(reach * c1, c1)],
            dst_ref=cext.at[slot, pl.ds((reach - d) * c1, c1)],
            send_sem=csend_sem.at[k],
            recv_sem=crecv_sem.at[slot, k],
            device_id=device(me + d),
            device_id_type=MESH,
        )

    coarse_round = [0]

    def coarse_apply(corr):
        slot = coarse_round[0] % 2
        coarse_round[0] += 1
        cext[slot, pl.ds(reach * c1, c1), :] = corr
        for k in range(n_slots):
            @pl.when(valid(me + offsets[k]))
            def _():
                coarse_copy(slot, k).start()
        bases = []
        for part in halves(corr):
            lower, upper = shifted(part)
            bases.append(cdiag * part + cv0 * lower + cv1 * upper)
        for k in range(n_slots):
            @pl.when(valid(me + offsets[k]))
            def _():
                coarse_copy(slot, k).wait_send()

            @pl.when(valid(me - offsets[k]))
            def _():
                coarse_copy(slot, k).wait_recv()
        gathered = select(mct, cext[slot])
        totals = []
        for t, total in enumerate(bases):
            for n in range(n_ch):
                total = total + cprep_v[3 + n] * gathered[n * c1:(n + 1) * c1, t * LANES:(t + 1) * LANES]
            totals.append(total)
        return jnp.concatenate(totals, 1)

    def per_half(x, coeff, op):
        return jnp.concatenate([op(part, coeff) for part in halves(x)], 1)

    solution = per_half(OMEGA * rhs, diag, lambda x, c: x / c)
    for cycle_index in range(CYCLES):
        for sweep_index in range(PRE):
            if cycle_index == 0 and sweep_index == 0:
                continue
            step = OMEGA * (rhs - fine_apply(solution))
            solution = solution + per_half(step, diag, lambda x, c: x / c)
        residual = rhs - fine_apply(solution)
        weighted = per_half(residual, w, lambda x, c: x * c)
        coarse_source = mm(at, weighted)
        correction = per_half(OMEGA * coarse_source, cdiag, lambda x, c: x / c)
        for coarse_sweep_index in range(CSWEEPS - 1):
            step = OMEGA * (coarse_source - coarse_apply(correction))
            correction = correction + per_half(step, cdiag, lambda x, c: x / c)
        lifted = mm(a, correction)
        solution = solution + per_half(lifted, w, lambda x, c: x * c)
        for sweep_index in range(POST):
            step = OMEGA * (rhs - fine_apply(solution))
            solution = solution + per_half(step, diag, lambda x, c: x / c)
    for t, part in enumerate(halves(solution)):
        out_v[0, t] = jnp.transpose(part)[:layers]
    store = pltpu.make_async_copy(out_v, out_hbm, load_sem.at[len(loads)])
    store.start()
    store.wait()


def body(
    right_side,
    absorption,
    vertical,
    horizontal,
    neighbours,
    send_index,
    aggregate,
    weights,
    coarse_vertical,
    coarse_horizontal,
    coarse_neighbours,
    *,
    n_parts,
    n_grp,
):
    _, tracers, layers, columns = right_side.shape
    reach = send_index.shape[1] // 2
    width = send_index.shape[2]
    c1 = coarse_neighbours.shape[2]
    n_slots = 2 * reach

    cvert = coarse_vertical[0]
    chor = coarse_horizontal[0]
    coarse_diagonal = (
        0.5 + jnp.abs(cvert[0]) + jnp.abs(cvert[1]) + jnp.sum(jnp.abs(chor), axis=0)
    )
    layer = lax.broadcasted_iota(jnp.int32, (layers, 1), 0)
    cv0 = jnp.where(layer == 0, 0.0, cvert[0])
    cv1 = jnp.where(layer == layers - 1, 0.0, cvert[1])
    stacked = jnp.concatenate([coarse_diagonal[None], cv0[None], cv1[None], chor], 0)
    fill = jnp.concatenate(
        [
            jnp.ones((1, c1, LANES - layers), F32),
            jnp.zeros((2 + chor.shape[0], c1, LANES - layers), F32),
        ],
        0,
    )
    cprep = jnp.concatenate([jnp.transpose(stacked, (0, 2, 1)), fill], 2)

    si = send_index.reshape(1, n_slots * width)
    n_crow = coarse_neighbours.shape[1] * c1
    cnb = jnp.pad(
        coarse_neighbours.reshape(1, n_crow), ((0, 0), (0, LANES - n_crow)), constant_values=-1
    )

    args = (right_side, absorption, vertical, horizontal, weights, neighbours[0], si, aggregate, cnb, cprep)
    ext_rows = columns + n_slots * width
    coarse_rows = ext_rows
    scratch = [pltpu.VMEM(x.shape, x.dtype) for x in args] + [
        pltpu.VMEM(right_side.shape, F32),
        pltpu.SemaphoreType.DMA((len(args) + 1,)),
        pltpu.VMEM((neighbours.shape[1] * columns, ext_rows), BF16),
        pltpu.VMEM((2, n_slots * width, tracers * LANES), F32),
        pltpu.VMEM((n_slots * width, tracers * LANES), F32),
        pltpu.VMEM((2, coarse_rows, tracers * LANES), F32),
        pltpu.SemaphoreType.DMA((n_slots,)),
        pltpu.SemaphoreType.DMA((2, n_slots)),
        pltpu.SemaphoreType.DMA((n_slots,)),
        pltpu.SemaphoreType.DMA((2, n_slots)),
    ]
    return pl.pallas_call(
        functools.partial(vcycle_kernel, n_parts, n_grp, reach, width),
        out_shape=jax.ShapeDtypeStruct(right_side.shape, F32),
        in_specs=[pl.BlockSpec(memory_space=pl.ANY)] * len(args),
        out_specs=pl.BlockSpec(memory_space=pl.ANY),
        scratch_shapes=scratch,
        compiler_params=pltpu.CompilerParams(collective_id=0, has_side_effects=True),
    )(*args)


def solution(mesh):
    placed = (
        P(("dom", "grp"), None, None, None),
        P(("dom", "grp"), None, None),
        P(("dom", "grp"), None, None, None),
        P(("dom", "grp"), None, None, None),
        P(("dom", "grp"), None, None),
        P(("dom", "grp"), None, None),
        P(("dom", "grp"), None),
        P(("dom", "grp"), None, None),
        P(("dom", "grp"), None, None, None),
        P(("dom", "grp"), None, None, None),
        P(("dom", "grp"), None, None),
    )
    n_grp = mesh.shape["grp"]
    n_parts = mesh.shape["dom"] * n_grp
    return jax.shard_map(
        functools.partial(body, n_parts=n_parts, n_grp=n_grp),
        mesh=mesh,
        in_specs=placed,
        out_specs=P(("dom", "grp"), None, None, None),
        check_vma=False,
    )
```

```python
import functools

import jax
import jax.numpy as jnp
from jax import lax
from jax.experimental import pallas as pl
from jax.experimental.pallas import tpu as pltpu
from jax.sharding import PartitionSpec as P

CYCLES = 2
PRE = 2
POST = 2
CSWEEPS = 4

OMEGA = 0.8
HIGHEST = lax.Precision.HIGHEST
MESH = pl.DeviceIdType.MESH
LANES = 128
F32 = jnp.float32
BF16 = jnp.bfloat16


def mm(a, b):
    return jnp.dot(a, b, precision=HIGHEST, preferred_element_type=F32)


def select(onehot, x):
    hi = x.astype(BF16)
    rest = x - hi.astype(F32)
    mid = rest.astype(BF16)
    lo = (rest - mid.astype(F32)).astype(BF16)
    part = lambda y: jnp.dot(onehot, y, preferred_element_type=F32)
    return (part(hi) + part(mid)) + part(lo)


def vcycle_kernel(
    n_parts,
    n_grp,
    reach,
    width,
    rhs_hbm,
    absorption_hbm,
    vertical_hbm,
    horizontal_hbm,
    weights_hbm,
    nb_hbm,
    si_hbm,
    agg_hbm,
    cnb_hbm,
    cprep_hbm,
    out_hbm,
    rhs_v,
    absorption_v,
    vertical_v,
    horizontal_v,
    weights_v,
    nb_v,
    si_v,
    agg_v,
    cnb_v,
    cprep_v,
    out_v,
    load_sem,
    mt_s,
    ghost,
    sendbuf,
    cext,
    send_sem,
    recv_sem,
    csend_sem,
    crecv_sem,
):
    me = lax.axis_index("dom") * n_grp + lax.axis_index("grp")
    offsets = list(range(1, reach + 1)) + [-d for d in range(1, reach + 1)]
    n_slots = len(offsets)
    tracers, layers, columns = rhs_v.shape[1:]
    n_nb = nb_v.shape[0]
    c1 = cprep_v.shape[1]
    n_ch = cprep_v.shape[0] - 3
    halo = n_slots * width

    def valid(q):
        return jnp.logical_and(q >= 0, q < n_parts)

    def device(q):
        return (lax.div(q, n_grp), lax.rem(q, n_grp))

    loads = [
        pltpu.make_async_copy(src, dst, load_sem.at[i])
        for i, (src, dst) in enumerate(
            [
                (rhs_hbm, rhs_v),
                (absorption_hbm, absorption_v),
                (vertical_hbm, vertical_v),
                (horizontal_hbm, horizontal_v),
                (weights_hbm, weights_v),
                (nb_hbm, nb_v),
                (si_hbm, si_v),
                (agg_hbm, agg_v),
                (cnb_hbm, cnb_v),
                (cprep_hbm, cprep_v),
            ]
        )
    ]
    for copy in loads:
        copy.start()

    ghost[...] = jnp.zeros_like(ghost)
    cext[...] = jnp.zeros_like(cext)

    barrier = pltpu.get_barrier_semaphore()
    for d in offsets:
        @pl.when(valid(me + d))
        def _():
            pl.semaphore_signal(barrier, 1, device_id=device(me + d), device_id_type=MESH)
    for copy in loads:
        copy.wait()

    lane = lax.broadcasted_iota(jnp.int32, (8, LANES), 1)
    probe = pltpu.roll(lane, 1, 1)
    expected = jnp.where(lane == 0, LANES - 1, lane - 1)
    forward = (probe == expected)[0:1, :]
    layer_lane = lax.broadcasted_iota(jnp.int32, (1, LANES), 1)
    live = layer_lane < layers

    def shifted(x):
        a = pltpu.roll(x, 1, 1)
        b = pltpu.roll(x, LANES - 1, 1)
        lower = jnp.where(forward, a, b)
        upper = jnp.where(forward, b, a)
        return lower, upper

    pad_rows = jnp.zeros((LANES - layers, columns), F32)

    def to_cols(slab):
        return jnp.transpose(jnp.concatenate([slab, pad_rows], 0))

    ab = absorption_v[0]
    vr0 = vertical_v[0, 0]
    vr1 = vertical_v[0, 1]
    diag_rows = ab + jnp.abs(vr0) + jnp.abs(vr1)
    hsum = jnp.abs(horizontal_v[0, 0])
    for n in range(1, horizontal_v.shape[1]):
        hsum = hsum + jnp.abs(horizontal_v[0, n])
    diag_rows = diag_rows + hsum
    diag = jnp.where(live, to_cols(diag_rows), 1.0)
    v0 = jnp.where(layer_lane == 0, 0.0, to_cols(vr0))
    v1 = jnp.where(layer_lane == layers - 1, 0.0, to_cols(vr1))
    h = [to_cols(horizontal_v[0, n]) for n in range(horizontal_v.shape[1])]
    w = to_cols(weights_v[0])
    rhs = jnp.concatenate([to_cols(rhs_v[0, t]) for t in range(tracers)], 1)

    ext_rows = columns + halo
    k_iota = lax.broadcasted_iota(jnp.int32, (ext_rows, columns), 0)
    for n in range(n_nb):
        chosen = (k_iota == nb_v[n:n + 1, :]).astype(F32)
        mt_s[pl.ds(n * columns, columns), :] = jnp.transpose(chosen).astype(BF16)
    st = jnp.transpose((lax.broadcasted_iota(jnp.int32, (columns, halo), 0) == si_v[...]).astype(F32)).astype(BF16)
    at = (lax.broadcasted_iota(jnp.int32, (c1, columns), 0) == agg_v[...]).astype(F32)
    a_full = jnp.transpose((lax.broadcasted_iota(jnp.int32, (LANES, columns), 0) == agg_v[...]).astype(F32))
    a = a_full[:, :c1]
    coarse_rows = cext.shape[1]
    n_crow = n_ch * c1
    mct = jnp.transpose(
        (lax.broadcasted_iota(jnp.int32, (coarse_rows, cnb_v.shape[1]), 0) == cnb_v[...]).astype(F32)
    )[:n_crow].astype(BF16)

    cdiag = cprep_v[0]
    cv0 = cprep_v[1]
    cv1 = cprep_v[2]

    def halves(x):
        return [x[:, t * LANES:(t + 1) * LANES] for t in range(x.shape[1] // LANES)]

    def fine_copy(slot, s):
        rows = pl.ds(s * width, width)
        return pltpu.make_async_remote_copy(
            src_ref=sendbuf.at[rows],
            dst_ref=ghost.at[slot, rows],
            send_sem=send_sem.at[s],
            recv_sem=recv_sem.at[slot, s],
            device_id=device(me + offsets[s]),
            device_id_type=MESH,
        )

    fine_round = [0]
    pending = {"fine": None, "coarse": None}

    def finish_sends(kind, copy_of):
        slot = pending[kind]
        if slot is None:
            return
        pending[kind] = None
        for s in range(n_slots):
            @pl.when(valid(me + offsets[s]))
            def _():
                copy_of(slot, s).wait_send()

    def fine_apply(field):
        slot = fine_round[0] % 2
        fine_round[0] += 1
        finish_sends("fine", fine_copy)
        sendbuf[...] = select(st, field)
        for s in range(n_slots):
            @pl.when(valid(me + offsets[s]))
            def _():
                fine_copy(slot, s).start()
        local = select(mt_s[:, pl.ds(0, columns)], field)
        bases = []
        for part in halves(field):
            lower, upper = shifted(part)
            bases.append(diag * part + v0 * lower + v1 * upper)
        pending["fine"] = slot
        for s in range(n_slots):
            @pl.when(valid(me - offsets[s]))
            def _():
                fine_copy(slot, s).wait_recv()
        gathered = local + select(mt_s[:, pl.ds(columns, halo)], ghost[slot])
        totals = []
        for t, total in enumerate(bases):
            for n in range(n_nb):
                total = total + h[n] * gathered[n * columns:(n + 1) * columns, t * LANES:(t + 1) * LANES]
            totals.append(total)
        return jnp.concatenate(totals, 1)

    def coarse_copy(slot, k):
        d = offsets[k]
        return pltpu.make_async_remote_copy(
            src_ref=cext.at[slot, pl.ds(reach * c1, c1)],
            dst_ref=cext.at[slot, pl.ds((reach - d) * c1, c1)],
            send_sem=csend_sem.at[k],
            recv_sem=crecv_sem.at[slot, k],
            device_id=device(me + d),
            device_id_type=MESH,
        )

    coarse_round = [0]

    def coarse_apply(corr):
        slot = coarse_round[0] % 2
        coarse_round[0] += 1
        finish_sends("coarse", coarse_copy)
        cext[slot, pl.ds(reach * c1, c1), :] = corr
        for k in range(n_slots):
            @pl.when(valid(me + offsets[k]))
            def _():
                coarse_copy(slot, k).start()
        bases = []
        for part in halves(corr):
            lower, upper = shifted(part)
            bases.append(cdiag * part + cv0 * lower + cv1 * upper)
        pending["coarse"] = slot
        for k in range(n_slots):
            @pl.when(valid(me - offsets[k]))
            def _():
                coarse_copy(slot, k).wait_recv()
        gathered = select(mct, cext[slot])
        totals = []
        for t, total in enumerate(bases):
            for n in range(n_ch):
                total = total + cprep_v[3 + n] * gathered[n * c1:(n + 1) * c1, t * LANES:(t + 1) * LANES]
            totals.append(total)
        return jnp.concatenate(totals, 1)

    peers = sum(valid(me + d).astype(jnp.int32) for d in offsets)
    pl.semaphore_wait(barrier, peers)

    def per_half(x, coeff, op):
        return jnp.concatenate([op(part, coeff) for part in halves(x)], 1)

    solution = per_half(OMEGA * rhs, diag, lambda x, c: x / c)
    for cycle_index in range(CYCLES):
        for sweep_index in range(PRE):
            if cycle_index == 0 and sweep_index == 0:
                continue
            step = OMEGA * (rhs - fine_apply(solution))
            solution = solution + per_half(step, diag, lambda x, c: x / c)
        residual = rhs - fine_apply(solution)
        weighted = per_half(residual, w, lambda x, c: x * c)
        coarse_source = mm(at, weighted)
        correction = per_half(OMEGA * coarse_source, cdiag, lambda x, c: x / c)
        for coarse_sweep_index in range(CSWEEPS - 1):
            step = OMEGA * (coarse_source - coarse_apply(correction))
            correction = correction + per_half(step, cdiag, lambda x, c: x / c)
        lifted = mm(a, correction)
        solution = solution + per_half(lifted, w, lambda x, c: x * c)
        for sweep_index in range(POST):
            step = OMEGA * (rhs - fine_apply(solution))
            solution = solution + per_half(step, diag, lambda x, c: x / c)
    finish_sends("fine", fine_copy)
    finish_sends("coarse", coarse_copy)
    for t, part in enumerate(halves(solution)):
        out_v[0, t] = jnp.transpose(part)[:layers]
    store = pltpu.make_async_copy(out_v, out_hbm, load_sem.at[len(loads)])
    store.start()
    store.wait()


def body(
    right_side,
    absorption,
    vertical,
    horizontal,
    neighbours,
    send_index,
    aggregate,
    weights,
    coarse_vertical,
    coarse_horizontal,
    coarse_neighbours,
    *,
    n_parts,
    n_grp,
):
    _, tracers, layers, columns = right_side.shape
    reach = send_index.shape[1] // 2
    width = send_index.shape[2]
    c1 = coarse_neighbours.shape[2]
    n_slots = 2 * reach

    cvert = coarse_vertical[0]
    chor = coarse_horizontal[0]
    coarse_diagonal = (
        0.5 + jnp.abs(cvert[0]) + jnp.abs(cvert[1]) + jnp.sum(jnp.abs(chor), axis=0)
    )
    layer = lax.broadcasted_iota(jnp.int32, (layers, 1), 0)
    cv0 = jnp.where(layer == 0, 0.0, cvert[0])
    cv1 = jnp.where(layer == layers - 1, 0.0, cvert[1])
    stacked = jnp.concatenate([coarse_diagonal[None], cv0[None], cv1[None], chor], 0)
    fill = jnp.concatenate(
        [
            jnp.ones((1, c1, LANES - layers), F32),
            jnp.zeros((2 + chor.shape[0], c1, LANES - layers), F32),
        ],
        0,
    )
    cprep = jnp.concatenate([jnp.transpose(stacked, (0, 2, 1)), fill], 2)

    si = send_index.reshape(1, n_slots * width)
    n_crow = coarse_neighbours.shape[1] * c1
    cnb = jnp.pad(
        coarse_neighbours.reshape(1, n_crow), ((0, 0), (0, LANES - n_crow)), constant_values=-1
    )

    args = (right_side, absorption, vertical, horizontal, weights, neighbours[0], si, aggregate, cnb, cprep)
    ext_rows = columns + n_slots * width
    coarse_rows = ext_rows
    scratch = [pltpu.VMEM(x.shape, x.dtype) for x in args] + [
        pltpu.VMEM(right_side.shape, F32),
        pltpu.SemaphoreType.DMA((len(args) + 1,)),
        pltpu.VMEM((neighbours.shape[1] * columns, ext_rows), BF16),
        pltpu.VMEM((2, n_slots * width, tracers * LANES), F32),
        pltpu.VMEM((n_slots * width, tracers * LANES), F32),
        pltpu.VMEM((2, coarse_rows, tracers * LANES), F32),
        pltpu.SemaphoreType.DMA((n_slots,)),
        pltpu.SemaphoreType.DMA((2, n_slots)),
        pltpu.SemaphoreType.DMA((n_slots,)),
        pltpu.SemaphoreType.DMA((2, n_slots)),
    ]
    return pl.pallas_call(
        functools.partial(vcycle_kernel, n_parts, n_grp, reach, width),
        out_shape=jax.ShapeDtypeStruct(right_side.shape, F32),
        in_specs=[pl.BlockSpec(memory_space=pl.ANY)] * len(args),
        out_specs=pl.BlockSpec(memory_space=pl.ANY),
        scratch_shapes=scratch,
        compiler_params=pltpu.CompilerParams(collective_id=0, has_side_effects=True),
    )(*args)


def solution(mesh):
    placed = (
        P(("dom", "grp"), None, None, None),
        P(("dom", "grp"), None, None),
        P(("dom", "grp"), None, None, None),
        P(("dom", "grp"), None, None, None),
        P(("dom", "grp"), None, None),
        P(("dom", "grp"), None, None),
        P(("dom", "grp"), None),
        P(("dom", "grp"), None, None),
        P(("dom", "grp"), None, None, None),
        P(("dom", "grp"), None, None, None),
        P(("dom", "grp"), None, None),
    )
    n_grp = mesh.shape["grp"]
    n_parts = mesh.shape["dom"] * n_grp
    return jax.shard_map(
        functools.partial(body, n_parts=n_parts, n_grp=n_grp),
        mesh=mesh,
        in_specs=placed,
        out_specs=P(("dom", "grp"), None, None, None),
        check_vma=False,
    )
```

```python
import functools

import jax
import jax.numpy as jnp
from jax import lax
from jax.experimental import pallas as pl
from jax.experimental.pallas import tpu as pltpu
from jax.sharding import PartitionSpec as P

CYCLES = 2
PRE = 2
POST = 2
CSWEEPS = 4

OMEGA = 0.8
HIGHEST = lax.Precision.HIGHEST
MESH = pl.DeviceIdType.MESH
LANES = 128
F32 = jnp.float32
BF16 = jnp.bfloat16


def mm(a, b):
    return jnp.dot(a, b, precision=HIGHEST, preferred_element_type=F32)


def select(onehot, x):
    hi = x.astype(BF16)
    lo = (x - hi.astype(F32)).astype(BF16)
    part = lambda y: jnp.dot(onehot, y, preferred_element_type=F32)
    return part(hi) + part(lo)


def vcycle_kernel(
    n_parts,
    n_grp,
    reach,
    width,
    rhs_hbm,
    absorption_hbm,
    vertical_hbm,
    horizontal_hbm,
    weights_hbm,
    nb_hbm,
    si_hbm,
    agg_hbm,
    cnb_hbm,
    cprep_hbm,
    out_hbm,
    rhs_v,
    absorption_v,
    vertical_v,
    horizontal_v,
    weights_v,
    nb_v,
    si_v,
    agg_v,
    cnb_v,
    cprep_v,
    out_v,
    load_sem,
    mt_s,
    ghost,
    sendbuf,
    cext,
    send_sem,
    recv_sem,
    csend_sem,
    crecv_sem,
):
    me = lax.axis_index("dom") * n_grp + lax.axis_index("grp")
    offsets = list(range(1, reach + 1)) + [-d for d in range(1, reach + 1)]
    n_slots = len(offsets)
    tracers, layers, columns = rhs_v.shape[1:]
    n_nb = nb_v.shape[0]
    c1 = cprep_v.shape[1]
    n_ch = cprep_v.shape[0] - 3
    halo = n_slots * width

    def valid(q):
        return jnp.logical_and(q >= 0, q < n_parts)

    def device(q):
        return (lax.div(q, n_grp), lax.rem(q, n_grp))

    loads = [
        pltpu.make_async_copy(src, dst, load_sem.at[i])
        for i, (src, dst) in enumerate(
            [
                (rhs_hbm, rhs_v),
                (absorption_hbm, absorption_v),
                (vertical_hbm, vertical_v),
                (horizontal_hbm, horizontal_v),
                (weights_hbm, weights_v),
                (nb_hbm, nb_v),
                (si_hbm, si_v),
                (agg_hbm, agg_v),
                (cnb_hbm, cnb_v),
                (cprep_hbm, cprep_v),
            ]
        )
    ]
    for copy in loads:
        copy.start()

    ghost[...] = jnp.zeros_like(ghost)
    cext[...] = jnp.zeros_like(cext)

    barrier = pltpu.get_barrier_semaphore()
    for d in offsets:
        @pl.when(valid(me + d))
        def _():
            pl.semaphore_signal(barrier, 1, device_id=device(me + d), device_id_type=MESH)
    for copy in loads:
        copy.wait()

    lane = lax.broadcasted_iota(jnp.int32, (8, LANES), 1)
    probe = pltpu.roll(lane, 1, 1)
    expected = jnp.where(lane == 0, LANES - 1, lane - 1)
    forward = (probe == expected)[0:1, :]
    layer_lane = lax.broadcasted_iota(jnp.int32, (1, LANES), 1)
    live = layer_lane < layers

    def shifted(x):
        a = pltpu.roll(x, 1, 1)
        b = pltpu.roll(x, LANES - 1, 1)
        lower = jnp.where(forward, a, b)
        upper = jnp.where(forward, b, a)
        return lower, upper

    pad_rows = jnp.zeros((LANES - layers, columns), F32)

    def to_cols(slab):
        return jnp.transpose(jnp.concatenate([slab, pad_rows], 0))

    ab = absorption_v[0]
    vr0 = vertical_v[0, 0]
    vr1 = vertical_v[0, 1]
    diag_rows = ab + jnp.abs(vr0) + jnp.abs(vr1)
    hsum = jnp.abs(horizontal_v[0, 0])
    for n in range(1, horizontal_v.shape[1]):
        hsum = hsum + jnp.abs(horizontal_v[0, n])
    diag_rows = diag_rows + hsum
    diag = jnp.where(live, to_cols(diag_rows), 1.0)
    v0 = jnp.where(layer_lane == 0, 0.0, to_cols(vr0))
    v1 = jnp.where(layer_lane == layers - 1, 0.0, to_cols(vr1))
    h = [to_cols(horizontal_v[0, n]) for n in range(horizontal_v.shape[1])]
    w = to_cols(weights_v[0])
    rhs = jnp.concatenate([to_cols(rhs_v[0, t]) for t in range(tracers)], 1)

    ext_rows = columns + halo
    k_iota = lax.broadcasted_iota(jnp.int32, (ext_rows, columns), 0)
    for n in range(n_nb):
        chosen = (k_iota == nb_v[n:n + 1, :]).astype(F32)
        mt_s[pl.ds(n * columns, columns), :] = jnp.transpose(chosen).astype(BF16)
    st = jnp.transpose((lax.broadcasted_iota(jnp.int32, (columns, halo), 0) == si_v[...]).astype(F32)).astype(BF16)
    at = (lax.broadcasted_iota(jnp.int32, (c1, columns), 0) == agg_v[...]).astype(F32)
    a_full = jnp.transpose((lax.broadcasted_iota(jnp.int32, (LANES, columns), 0) == agg_v[...]).astype(F32))
    a = a_full[:, :c1]
    coarse_rows = cext.shape[1]
    n_crow = n_ch * c1
    mct = jnp.transpose(
        (lax.broadcasted_iota(jnp.int32, (coarse_rows, cnb_v.shape[1]), 0) == cnb_v[...]).astype(F32)
    )[:n_crow].astype(BF16)

    inv_diag = 1.0 / diag
    cdiag = cprep_v[0]
    inv_cdiag = 1.0 / cdiag
    cv0 = cprep_v[1]
    cv1 = cprep_v[2]

    def halves(x):
        return [x[:, t * LANES:(t + 1) * LANES] for t in range(x.shape[1] // LANES)]

    def fine_copy(slot, s):
        rows = pl.ds(s * width, width)
        return pltpu.make_async_remote_copy(
            src_ref=sendbuf.at[rows],
            dst_ref=ghost.at[slot, rows],
            send_sem=send_sem.at[s],
            recv_sem=recv_sem.at[slot, s],
            device_id=device(me + offsets[s]),
            device_id_type=MESH,
        )

    fine_round = [0]
    pending = {"fine": None, "coarse": None}

    def finish_sends(kind, copy_of):
        slot = pending[kind]
        if slot is None:
            return
        pending[kind] = None
        for s in range(n_slots):
            @pl.when(valid(me + offsets[s]))
            def _():
                copy_of(slot, s).wait_send()

    def fine_apply(field):
        slot = fine_round[0] % 2
        fine_round[0] += 1
        finish_sends("fine", fine_copy)
        sendbuf[...] = select(st, field)
        for s in range(n_slots):
            @pl.when(valid(me + offsets[s]))
            def _():
                fine_copy(slot, s).start()
        local = select(mt_s[:, pl.ds(0, columns)], field)
        bases = []
        for t, part in enumerate(halves(field)):
            lower, upper = shifted(part)
            total = diag * part + v0 * lower + v1 * upper
            for n in range(n_nb):
                total = total + h[n] * local[n * columns:(n + 1) * columns, t * LANES:(t + 1) * LANES]
            bases.append(total)
        pending["fine"] = slot
        for s in range(n_slots):
            @pl.when(valid(me - offsets[s]))
            def _():
                fine_copy(slot, s).wait_recv()
        gathered = select(mt_s[:, pl.ds(columns, halo)], ghost[slot])
        totals = []
        for t, total in enumerate(bases):
            for n in range(n_nb):
                total = total + h[n] * gathered[n * columns:(n + 1) * columns, t * LANES:(t + 1) * LANES]
            totals.append(total)
        return jnp.concatenate(totals, 1)

    def coarse_copy(slot, k):
        d = offsets[k]
        return pltpu.make_async_remote_copy(
            src_ref=cext.at[slot, pl.ds(reach * c1, c1)],
            dst_ref=cext.at[slot, pl.ds((reach - d) * c1, c1)],
            send_sem=csend_sem.at[k],
            recv_sem=crecv_sem.at[slot, k],
            device_id=device(me + d),
            device_id_type=MESH,
        )

    coarse_round = [0]

    def coarse_apply(corr):
        slot = coarse_round[0] % 2
        coarse_round[0] += 1
        finish_sends("coarse", coarse_copy)
        cext[slot, pl.ds(reach * c1, c1), :] = corr
        for k in range(n_slots):
            @pl.when(valid(me + offsets[k]))
            def _():
                coarse_copy(slot, k).start()
        bases = []
        for part in halves(corr):
            lower, upper = shifted(part)
            bases.append(cdiag * part + cv0 * lower + cv1 * upper)
        pending["coarse"] = slot
        for k in range(n_slots):
            @pl.when(valid(me - offsets[k]))
            def _():
                coarse_copy(slot, k).wait_recv()
        gathered = select(mct, cext[slot])
        totals = []
        for t, total in enumerate(bases):
            for n in range(n_ch):
                total = total + cprep_v[3 + n] * gathered[n * c1:(n + 1) * c1, t * LANES:(t + 1) * LANES]
            totals.append(total)
        return jnp.concatenate(totals, 1)

    peers = sum(valid(me + d).astype(jnp.int32) for d in offsets)
    pl.semaphore_wait(barrier, peers)

    def per_half(x, coeff, op):
        return jnp.concatenate([op(part, coeff) for part in halves(x)], 1)

    solution = per_half(OMEGA * rhs, inv_diag, lambda x, c: x * c)
    for cycle_index in range(CYCLES):
        for sweep_index in range(PRE):
            if cycle_index == 0 and sweep_index == 0:
                continue
            step = OMEGA * (rhs - fine_apply(solution))
            solution = solution + per_half(step, inv_diag, lambda x, c: x * c)
        residual = rhs - fine_apply(solution)
        weighted = per_half(residual, w, lambda x, c: x * c)
        coarse_source = mm(at, weighted)
        correction = per_half(OMEGA * coarse_source, inv_cdiag, lambda x, c: x * c)
        for coarse_sweep_index in range(CSWEEPS - 1):
            step = OMEGA * (coarse_source - coarse_apply(correction))
            correction = correction + per_half(step, inv_cdiag, lambda x, c: x * c)
        lifted = mm(a, correction)
        solution = solution + per_half(lifted, w, lambda x, c: x * c)
        for sweep_index in range(POST):
            step = OMEGA * (rhs - fine_apply(solution))
            solution = solution + per_half(step, inv_diag, lambda x, c: x * c)
    finish_sends("fine", fine_copy)
    finish_sends("coarse", coarse_copy)
    for t, part in enumerate(halves(solution)):
        out_v[0, t] = jnp.transpose(part)[:layers]
    store = pltpu.make_async_copy(out_v, out_hbm, load_sem.at[len(loads)])
    store.start()
    store.wait()


def body(
    right_side,
    absorption,
    vertical,
    horizontal,
    neighbours,
    send_index,
    aggregate,
    weights,
    coarse_vertical,
    coarse_horizontal,
    coarse_neighbours,
    *,
    n_parts,
    n_grp,
):
    _, tracers, layers, columns = right_side.shape
    reach = send_index.shape[1] // 2
    width = send_index.shape[2]
    c1 = coarse_neighbours.shape[2]
    n_slots = 2 * reach

    cvert = coarse_vertical[0]
    chor = coarse_horizontal[0]
    coarse_diagonal = (
        0.5 + jnp.abs(cvert[0]) + jnp.abs(cvert[1]) + jnp.sum(jnp.abs(chor), axis=0)
    )
    layer = lax.broadcasted_iota(jnp.int32, (layers, 1), 0)
    cv0 = jnp.where(layer == 0, 0.0, cvert[0])
    cv1 = jnp.where(layer == layers - 1, 0.0, cvert[1])
    stacked = jnp.concatenate([coarse_diagonal[None], cv0[None], cv1[None], chor], 0)
    fill = jnp.concatenate(
        [
            jnp.ones((1, c1, LANES - layers), F32),
            jnp.zeros((2 + chor.shape[0], c1, LANES - layers), F32),
        ],
        0,
    )
    cprep = jnp.concatenate([jnp.transpose(stacked, (0, 2, 1)), fill], 2)

    si = send_index.reshape(1, n_slots * width)
    n_crow = coarse_neighbours.shape[1] * c1
    cnb = jnp.pad(
        coarse_neighbours.reshape(1, n_crow), ((0, 0), (0, LANES - n_crow)), constant_values=-1
    )

    args = (right_side, absorption, vertical, horizontal, weights, neighbours[0], si, aggregate, cnb, cprep)
    ext_rows = columns + n_slots * width
    coarse_rows = ext_rows
    scratch = [pltpu.VMEM(x.shape, x.dtype) for x in args] + [
        pltpu.VMEM(right_side.shape, F32),
        pltpu.SemaphoreType.DMA((len(args) + 1,)),
        pltpu.VMEM((neighbours.shape[1] * columns, ext_rows), BF16),
        pltpu.VMEM((2, n_slots * width, tracers * LANES), F32),
        pltpu.VMEM((n_slots * width, tracers * LANES), F32),
        pltpu.VMEM((2, coarse_rows, tracers * LANES), F32),
        pltpu.SemaphoreType.DMA((n_slots,)),
        pltpu.SemaphoreType.DMA((2, n_slots)),
        pltpu.SemaphoreType.DMA((n_slots,)),
        pltpu.SemaphoreType.DMA((2, n_slots)),
    ]
    return pl.pallas_call(
        functools.partial(vcycle_kernel, n_parts, n_grp, reach, width),
        out_shape=jax.ShapeDtypeStruct(right_side.shape, F32),
        in_specs=[pl.BlockSpec(memory_space=pl.ANY)] * len(args),
        out_specs=pl.BlockSpec(memory_space=pl.ANY),
        scratch_shapes=scratch,
        compiler_params=pltpu.CompilerParams(collective_id=0, has_side_effects=True),
    )(*args)


def solution(mesh):
    placed = (
        P(("dom", "grp"), None, None, None),
        P(("dom", "grp"), None, None),
        P(("dom", "grp"), None, None, None),
        P(("dom", "grp"), None, None, None),
        P(("dom", "grp"), None, None),
        P(("dom", "grp"), None, None),
        P(("dom", "grp"), None),
        P(("dom", "grp"), None, None),
        P(("dom", "grp"), None, None, None),
        P(("dom", "grp"), None, None, None),
        P(("dom", "grp"), None, None),
    )
    n_grp = mesh.shape["grp"]
    n_parts = mesh.shape["dom"] * n_grp
    return jax.shard_map(
        functools.partial(body, n_parts=n_parts, n_grp=n_grp),
        mesh=mesh,
        in_specs=placed,
        out_specs=P(("dom", "grp"), None, None, None),
        check_vma=False,
    )
```

```python
import functools

import jax
import jax.numpy as jnp
from jax import lax
from jax.experimental import pallas as pl
from jax.experimental.pallas import tpu as pltpu
from jax.sharding import PartitionSpec as P

CYCLES = 2
PRE = 2
POST = 2
CSWEEPS = 4

OMEGA = 0.8
HIGHEST = lax.Precision.HIGHEST
MESH = pl.DeviceIdType.MESH
LANES = 128
F32 = jnp.float32
BF16 = jnp.bfloat16


def mm(a, b):
    return jnp.dot(a, b, precision=HIGHEST, preferred_element_type=F32)


def select(onehot, x):
    hi = x.astype(BF16)
    lo = (x - hi.astype(F32)).astype(BF16)
    part = lambda y: jnp.dot(onehot, y, preferred_element_type=F32)
    return part(hi) + part(lo)


def vcycle_kernel(
    n_parts,
    n_grp,
    reach,
    width,
    rhs_hbm,
    absorption_hbm,
    vertical_hbm,
    horizontal_hbm,
    weights_hbm,
    nb_hbm,
    si_hbm,
    agg_hbm,
    cnb_hbm,
    cprep_hbm,
    out_hbm,
    rhs_v,
    absorption_v,
    vertical_v,
    horizontal_v,
    weights_v,
    nb_v,
    si_v,
    agg_v,
    cnb_v,
    cprep_v,
    out_v,
    load_sem,
    mt_s,
    ghost,
    sendbuf,
    cext,
    send_sem,
    recv_sem,
    csend_sem,
    crecv_sem,
):
    me = lax.axis_index("dom") * n_grp + lax.axis_index("grp")
    offsets = list(range(1, reach + 1)) + [-d for d in range(1, reach + 1)]
    n_slots = len(offsets)
    by_distance = sorted(range(n_slots), key=lambda s: (abs(offsets[s]) != 2, abs(offsets[s]) == reach, abs(offsets[s]), offsets[s] < 0))
    tracers, layers, columns = rhs_v.shape[1:]
    n_nb = nb_v.shape[0]
    c1 = cprep_v.shape[1]
    n_ch = cprep_v.shape[0] - 3
    halo = n_slots * width

    def valid(q):
        return jnp.logical_and(q >= 0, q < n_parts)

    def device(q):
        return (lax.div(q, n_grp), lax.rem(q, n_grp))

    loads = [
        pltpu.make_async_copy(src, dst, load_sem.at[i])
        for i, (src, dst) in enumerate(
            [
                (rhs_hbm, rhs_v),
                (absorption_hbm, absorption_v),
                (vertical_hbm, vertical_v),
                (horizontal_hbm, horizontal_v),
                (weights_hbm, weights_v),
                (nb_hbm, nb_v),
                (si_hbm, si_v),
                (agg_hbm, agg_v),
                (cnb_hbm, cnb_v),
                (cprep_hbm, cprep_v),
            ]
        )
    ]
    for copy in loads:
        copy.start()

    ghost[...] = jnp.zeros_like(ghost)
    cext[...] = jnp.zeros_like(cext)

    barrier = pltpu.get_barrier_semaphore()
    for d in offsets:
        @pl.when(valid(me + d))
        def _():
            pl.semaphore_signal(barrier, 1, device_id=device(me + d), device_id_type=MESH)
    for copy in loads:
        copy.wait()

    lane = lax.broadcasted_iota(jnp.int32, (8, LANES), 1)
    probe = pltpu.roll(lane, 1, 1)
    expected = jnp.where(lane == 0, LANES - 1, lane - 1)
    forward = (probe == expected)[0:1, :]
    layer_lane = lax.broadcasted_iota(jnp.int32, (1, LANES), 1)
    live = layer_lane < layers

    def shifted(x):
        a = pltpu.roll(x, 1, 1)
        b = pltpu.roll(x, LANES - 1, 1)
        lower = jnp.where(forward, a, b)
        upper = jnp.where(forward, b, a)
        return lower, upper

    pad_rows = jnp.zeros((LANES - layers, columns), F32)

    def to_cols(slab):
        return jnp.transpose(jnp.concatenate([slab, pad_rows], 0))

    ab = absorption_v[0]
    vr0 = vertical_v[0, 0]
    vr1 = vertical_v[0, 1]
    diag_rows = ab + jnp.abs(vr0) + jnp.abs(vr1)
    hsum = jnp.abs(horizontal_v[0, 0])
    for n in range(1, horizontal_v.shape[1]):
        hsum = hsum + jnp.abs(horizontal_v[0, n])
    diag_rows = diag_rows + hsum
    diag = jnp.where(live, to_cols(diag_rows), 1.0)
    v0 = jnp.where(layer_lane == 0, 0.0, to_cols(vr0))
    v1 = jnp.where(layer_lane == layers - 1, 0.0, to_cols(vr1))
    h = [to_cols(horizontal_v[0, n]) for n in range(horizontal_v.shape[1])]
    w = to_cols(weights_v[0])
    rhs = jnp.concatenate([to_cols(rhs_v[0, t]) for t in range(tracers)], 1)

    ext_rows = columns + halo
    k_iota = lax.broadcasted_iota(jnp.int32, (ext_rows, columns), 0)
    for n in range(n_nb):
        chosen = (k_iota == nb_v[n:n + 1, :]).astype(F32)
        mt_s[pl.ds(n * columns, columns), :] = jnp.transpose(chosen).astype(BF16)
    st = jnp.transpose((lax.broadcasted_iota(jnp.int32, (columns, halo), 0) == si_v[...]).astype(F32)).astype(BF16)
    at = (lax.broadcasted_iota(jnp.int32, (c1, columns), 0) == agg_v[...]).astype(F32)
    a_full = jnp.transpose((lax.broadcasted_iota(jnp.int32, (LANES, columns), 0) == agg_v[...]).astype(F32))
    a = a_full[:, :c1]
    coarse_rows = cext.shape[1]
    n_crow = n_ch * c1
    mct = jnp.transpose(
        (lax.broadcasted_iota(jnp.int32, (coarse_rows, cnb_v.shape[1]), 0) == cnb_v[...]).astype(F32)
    )[:n_crow].astype(BF16)

    inv_diag = 1.0 / diag
    cdiag = cprep_v[0]
    inv_cdiag = 1.0 / cdiag
    cv0 = cprep_v[1]
    cv1 = cprep_v[2]

    def halves(x):
        return [x[:, t * LANES:(t + 1) * LANES] for t in range(x.shape[1] // LANES)]

    def fine_copy(slot, s):
        rows = pl.ds(s * width, width)
        return pltpu.make_async_remote_copy(
            src_ref=sendbuf.at[rows],
            dst_ref=ghost.at[slot, rows],
            send_sem=send_sem.at[s],
            recv_sem=recv_sem.at[slot, s],
            device_id=device(me + offsets[s]),
            device_id_type=MESH,
        )

    fine_round = [0]
    pending = {"fine": None, "coarse": None}

    def finish_sends(kind, copy_of):
        slot = pending[kind]
        if slot is None:
            return
        pending[kind] = None
        for s in range(n_slots):
            @pl.when(valid(me + offsets[s]))
            def _():
                copy_of(slot, s).wait_send()

    def fine_apply(field):
        slot = fine_round[0] % 2
        fine_round[0] += 1
        finish_sends("fine", fine_copy)
        sendbuf[...] = select(st, field)
        for s in by_distance:
            @pl.when(valid(me + offsets[s]))
            def _():
                fine_copy(slot, s).start()
        local = select(mt_s[:, pl.ds(0, columns)], field)
        bases = []
        for t, part in enumerate(halves(field)):
            lower, upper = shifted(part)
            total = diag * part + v0 * lower + v1 * upper
            for n in range(n_nb):
                total = total + h[n] * local[n * columns:(n + 1) * columns, t * LANES:(t + 1) * LANES]
            bases.append(total)
        pending["fine"] = slot
        for s in range(n_slots):
            @pl.when(valid(me - offsets[s]))
            def _():
                fine_copy(slot, s).wait_recv()
        gathered = select(mt_s[:, pl.ds(columns, halo)], ghost[slot])
        totals = []
        for t, total in enumerate(bases):
            for n in range(n_nb):
                total = total + h[n] * gathered[n * columns:(n + 1) * columns, t * LANES:(t + 1) * LANES]
            totals.append(total)
        return jnp.concatenate(totals, 1)

    def coarse_copy(slot, k):
        d = offsets[k]
        return pltpu.make_async_remote_copy(
            src_ref=cext.at[slot, pl.ds(reach * c1, c1)],
            dst_ref=cext.at[slot, pl.ds((reach - d) * c1, c1)],
            send_sem=csend_sem.at[k],
            recv_sem=crecv_sem.at[slot, k],
            device_id=device(me + d),
            device_id_type=MESH,
        )

    coarse_round = [0]

    def coarse_apply(corr):
        slot = coarse_round[0] % 2
        coarse_round[0] += 1
        finish_sends("coarse", coarse_copy)
        cext[slot, pl.ds(reach * c1, c1), :] = corr
        for k in by_distance:
            @pl.when(valid(me + offsets[k]))
            def _():
                coarse_copy(slot, k).start()
        bases = []
        for part in halves(corr):
            lower, upper = shifted(part)
            bases.append(cdiag * part + cv0 * lower + cv1 * upper)
        pending["coarse"] = slot
        for k in range(n_slots):
            @pl.when(valid(me - offsets[k]))
            def _():
                coarse_copy(slot, k).wait_recv()
        gathered = select(mct, cext[slot])
        totals = []
        for t, total in enumerate(bases):
            for n in range(n_ch):
                total = total + cprep_v[3 + n] * gathered[n * c1:(n + 1) * c1, t * LANES:(t + 1) * LANES]
            totals.append(total)
        return jnp.concatenate(totals, 1)

    peers = sum(valid(me + d).astype(jnp.int32) for d in offsets)
    pl.semaphore_wait(barrier, peers)

    def per_half(x, coeff, op):
        return jnp.concatenate([op(part, coeff) for part in halves(x)], 1)

    solution = per_half(OMEGA * rhs, inv_diag, lambda x, c: x * c)
    for cycle_index in range(CYCLES):
        for sweep_index in range(PRE):
            if cycle_index == 0 and sweep_index == 0:
                continue
            step = OMEGA * (rhs - fine_apply(solution))
            solution = solution + per_half(step, inv_diag, lambda x, c: x * c)
        residual = rhs - fine_apply(solution)
        weighted = per_half(residual, w, lambda x, c: x * c)
        coarse_source = mm(at, weighted)
        correction = per_half(OMEGA * coarse_source, inv_cdiag, lambda x, c: x * c)
        for coarse_sweep_index in range(CSWEEPS - 1):
            step = OMEGA * (coarse_source - coarse_apply(correction))
            correction = correction + per_half(step, inv_cdiag, lambda x, c: x * c)
        lifted = mm(a, correction)
        solution = solution + per_half(lifted, w, lambda x, c: x * c)
        for sweep_index in range(POST):
            step = OMEGA * (rhs - fine_apply(solution))
            solution = solution + per_half(step, inv_diag, lambda x, c: x * c)
    finish_sends("fine", fine_copy)
    finish_sends("coarse", coarse_copy)
    for t, part in enumerate(halves(solution)):
        out_v[0, t] = jnp.transpose(part)[:layers]
    store = pltpu.make_async_copy(out_v, out_hbm, load_sem.at[len(loads)])
    store.start()
    store.wait()


def body(
    right_side,
    absorption,
    vertical,
    horizontal,
    neighbours,
    send_index,
    aggregate,
    weights,
    coarse_vertical,
    coarse_horizontal,
    coarse_neighbours,
    *,
    n_parts,
    n_grp,
):
    _, tracers, layers, columns = right_side.shape
    reach = send_index.shape[1] // 2
    width = send_index.shape[2]
    c1 = coarse_neighbours.shape[2]
    n_slots = 2 * reach

    cvert = coarse_vertical[0]
    chor = coarse_horizontal[0]
    coarse_diagonal = (
        0.5 + jnp.abs(cvert[0]) + jnp.abs(cvert[1]) + jnp.sum(jnp.abs(chor), axis=0)
    )
    layer = lax.broadcasted_iota(jnp.int32, (layers, 1), 0)
    cv0 = jnp.where(layer == 0, 0.0, cvert[0])
    cv1 = jnp.where(layer == layers - 1, 0.0, cvert[1])
    stacked = jnp.concatenate([coarse_diagonal[None], cv0[None], cv1[None], chor], 0)
    fill = jnp.concatenate(
        [
            jnp.ones((1, c1, LANES - layers), F32),
            jnp.zeros((2 + chor.shape[0], c1, LANES - layers), F32),
        ],
        0,
    )
    cprep = jnp.concatenate([jnp.transpose(stacked, (0, 2, 1)), fill], 2)

    si = send_index.reshape(1, n_slots * width)
    n_crow = coarse_neighbours.shape[1] * c1
    cnb = jnp.pad(
        coarse_neighbours.reshape(1, n_crow), ((0, 0), (0, LANES - n_crow)), constant_values=-1
    )

    args = (right_side, absorption, vertical, horizontal, weights, neighbours[0], si, aggregate, cnb, cprep)
    ext_rows = columns + n_slots * width
    coarse_rows = ext_rows
    scratch = [pltpu.VMEM(x.shape, x.dtype) for x in args] + [
        pltpu.VMEM(right_side.shape, F32),
        pltpu.SemaphoreType.DMA((len(args) + 1,)),
        pltpu.VMEM((neighbours.shape[1] * columns, ext_rows), BF16),
        pltpu.VMEM((2, n_slots * width, tracers * LANES), F32),
        pltpu.VMEM((n_slots * width, tracers * LANES), F32),
        pltpu.VMEM((2, coarse_rows, tracers * LANES), F32),
        pltpu.SemaphoreType.DMA((n_slots,)),
        pltpu.SemaphoreType.DMA((2, n_slots)),
        pltpu.SemaphoreType.DMA((n_slots,)),
        pltpu.SemaphoreType.DMA((2, n_slots)),
    ]
    return pl.pallas_call(
        functools.partial(vcycle_kernel, n_parts, n_grp, reach, width),
        out_shape=jax.ShapeDtypeStruct(right_side.shape, F32),
        in_specs=[pl.BlockSpec(memory_space=pl.ANY)] * len(args),
        out_specs=pl.BlockSpec(memory_space=pl.ANY),
        scratch_shapes=scratch,
        compiler_params=pltpu.CompilerParams(collective_id=0, has_side_effects=True),
    )(*args)


def solution(mesh):
    placed = (
        P(("dom", "grp"), None, None, None),
        P(("dom", "grp"), None, None),
        P(("dom", "grp"), None, None, None),
        P(("dom", "grp"), None, None, None),
        P(("dom", "grp"), None, None),
        P(("dom", "grp"), None, None),
        P(("dom", "grp"), None),
        P(("dom", "grp"), None, None),
        P(("dom", "grp"), None, None, None),
        P(("dom", "grp"), None, None, None),
        P(("dom", "grp"), None, None),
    )
    n_grp = mesh.shape["grp"]
    n_parts = mesh.shape["dom"] * n_grp
    return jax.shard_map(
        functools.partial(body, n_parts=n_parts, n_grp=n_grp),
        mesh=mesh,
        in_specs=placed,
        out_specs=P(("dom", "grp"), None, None, None),
        check_vma=False,
    )
```

```python
import functools

import jax
import jax.numpy as jnp
from jax import lax
from jax.experimental import pallas as pl
from jax.experimental.pallas import tpu as pltpu
from jax.sharding import PartitionSpec as P

CYCLES = 2
PRE = 2
POST = 2
CSWEEPS = 4

OMEGA = 0.8
HIGHEST = lax.Precision.HIGHEST
MESH = pl.DeviceIdType.MESH
LANES = 128
F32 = jnp.float32
BF16 = jnp.bfloat16


def mm(a, b):
    return jnp.dot(a, b, precision=HIGHEST, preferred_element_type=F32)


def select(onehot2, x):
    hi = x.astype(BF16)
    lo = (x - hi.astype(F32)).astype(BF16)
    return jnp.dot(onehot2, jnp.concatenate([hi, lo], 0), preferred_element_type=F32)


def doubled(onehot):
    return jnp.concatenate([onehot, onehot], 1)


def vcycle_kernel(
    n_parts,
    n_grp,
    reach,
    width,
    rhs_hbm,
    absorption_hbm,
    vertical_hbm,
    horizontal_hbm,
    weights_hbm,
    nb_hbm,
    si_hbm,
    agg_hbm,
    cnb_hbm,
    cprep_hbm,
    out_hbm,
    rhs_v,
    absorption_v,
    vertical_v,
    horizontal_v,
    weights_v,
    nb_v,
    si_v,
    agg_v,
    cnb_v,
    cprep_v,
    out_v,
    load_sem,
    mt_local,
    mt_ghost,
    ghost,
    sendbuf,
    cext,
    send_sem,
    recv_sem,
    csend_sem,
    crecv_sem,
):
    me = lax.axis_index("dom") * n_grp + lax.axis_index("grp")
    offsets = list(range(1, reach + 1)) + [-d for d in range(1, reach + 1)]
    n_slots = len(offsets)
    by_distance = sorted(range(n_slots), key=lambda s: (abs(offsets[s]) != 2, abs(offsets[s]) == reach, abs(offsets[s]), offsets[s] < 0))
    tracers, layers, columns = rhs_v.shape[1:]
    n_nb = nb_v.shape[0]
    c1 = cprep_v.shape[1]
    n_ch = cprep_v.shape[0] - 3
    halo = n_slots * width

    def valid(q):
        return jnp.logical_and(q >= 0, q < n_parts)

    def device(q):
        return (lax.div(q, n_grp), lax.rem(q, n_grp))

    loads = [
        pltpu.make_async_copy(src, dst, load_sem.at[i])
        for i, (src, dst) in enumerate(
            [
                (rhs_hbm, rhs_v),
                (absorption_hbm, absorption_v),
                (vertical_hbm, vertical_v),
                (horizontal_hbm, horizontal_v),
                (weights_hbm, weights_v),
                (nb_hbm, nb_v),
                (si_hbm, si_v),
                (agg_hbm, agg_v),
                (cnb_hbm, cnb_v),
                (cprep_hbm, cprep_v),
            ]
        )
    ]
    for copy in loads:
        copy.start()

    ghost[...] = jnp.zeros_like(ghost)
    cext[...] = jnp.zeros_like(cext)

    barrier = pltpu.get_barrier_semaphore()
    for d in offsets:
        @pl.when(valid(me + d))
        def _():
            pl.semaphore_signal(barrier, 1, device_id=device(me + d), device_id_type=MESH)
    for copy in loads:
        copy.wait()

    lane = lax.broadcasted_iota(jnp.int32, (8, LANES), 1)
    probe = pltpu.roll(lane, 1, 1)
    expected = jnp.where(lane == 0, LANES - 1, lane - 1)
    forward = (probe == expected)[0:1, :]
    layer_lane = lax.broadcasted_iota(jnp.int32, (1, LANES), 1)
    live = layer_lane < layers

    def shifted(x):
        a = pltpu.roll(x, 1, 1)
        b = pltpu.roll(x, LANES - 1, 1)
        lower = jnp.where(forward, a, b)
        upper = jnp.where(forward, b, a)
        return lower, upper

    pad_rows = jnp.zeros((LANES - layers, columns), F32)

    def to_cols(slab):
        return jnp.transpose(jnp.concatenate([slab, pad_rows], 0))

    ab = absorption_v[0]
    vr0 = vertical_v[0, 0]
    vr1 = vertical_v[0, 1]
    diag_rows = ab + jnp.abs(vr0) + jnp.abs(vr1)
    hsum = jnp.abs(horizontal_v[0, 0])
    for n in range(1, horizontal_v.shape[1]):
        hsum = hsum + jnp.abs(horizontal_v[0, n])
    diag_rows = diag_rows + hsum
    diag = jnp.where(live, to_cols(diag_rows), 1.0)
    v0 = jnp.where(layer_lane == 0, 0.0, to_cols(vr0))
    v1 = jnp.where(layer_lane == layers - 1, 0.0, to_cols(vr1))
    h = [to_cols(horizontal_v[0, n]) for n in range(horizontal_v.shape[1])]
    w = to_cols(weights_v[0])
    rhs = jnp.concatenate([to_cols(rhs_v[0, t]) for t in range(tracers)], 1)

    ext_rows = columns + halo
    k_iota = lax.broadcasted_iota(jnp.int32, (ext_rows, columns), 0)
    for n in range(n_nb):
        chosen = jnp.transpose((k_iota == nb_v[n:n + 1, :]).astype(F32)).astype(BF16)
        rows = pl.ds(n * columns, columns)
        mt_local[rows, :] = doubled(chosen[:, :columns])
        mt_ghost[rows, :] = doubled(chosen[:, columns:])
    st = doubled(jnp.transpose((lax.broadcasted_iota(jnp.int32, (columns, halo), 0) == si_v[...]).astype(F32)).astype(BF16))
    at = (lax.broadcasted_iota(jnp.int32, (c1, columns), 0) == agg_v[...]).astype(F32)
    a_full = jnp.transpose((lax.broadcasted_iota(jnp.int32, (LANES, columns), 0) == agg_v[...]).astype(F32))
    a = a_full[:, :c1]
    coarse_rows = cext.shape[1]
    n_crow = n_ch * c1
    mct = jnp.transpose(
        (lax.broadcasted_iota(jnp.int32, (coarse_rows, cnb_v.shape[1]), 0) == cnb_v[...]).astype(F32)
    )[:n_crow].astype(BF16)
    mct = doubled(mct)

    inv_diag = 1.0 / diag
    cdiag = cprep_v[0]
    inv_cdiag = 1.0 / cdiag
    cv0 = cprep_v[1]
    cv1 = cprep_v[2]

    def halves(x):
        return [x[:, t * LANES:(t + 1) * LANES] for t in range(x.shape[1] // LANES)]

    def fine_copy(slot, s):
        rows = pl.ds(s * width, width)
        return pltpu.make_async_remote_copy(
            src_ref=sendbuf.at[rows],
            dst_ref=ghost.at[slot, rows],
            send_sem=send_sem.at[s],
            recv_sem=recv_sem.at[slot, s],
            device_id=device(me + offsets[s]),
            device_id_type=MESH,
        )

    fine_round = [0]
    pending = {"fine": None, "coarse": None}

    def finish_sends(kind, copy_of):
        slot = pending[kind]
        if slot is None:
            return
        pending[kind] = None
        for s in range(n_slots):
            @pl.when(valid(me + offsets[s]))
            def _():
                copy_of(slot, s).wait_send()

    def fine_apply(field):
        slot = fine_round[0] % 2
        fine_round[0] += 1
        finish_sends("fine", fine_copy)
        sendbuf[...] = select(st, field)
        for s in by_distance:
            @pl.when(valid(me + offsets[s]))
            def _():
                fine_copy(slot, s).start()
        local = select(mt_local[...], field)
        bases = []
        for t, part in enumerate(halves(field)):
            lower, upper = shifted(part)
            total = diag * part + v0 * lower + v1 * upper
            for n in range(n_nb):
                total = total + h[n] * local[n * columns:(n + 1) * columns, t * LANES:(t + 1) * LANES]
            bases.append(total)
        pending["fine"] = slot
        for s in range(n_slots):
            @pl.when(valid(me - offsets[s]))
            def _():
                fine_copy(slot, s).wait_recv()
        gathered = select(mt_ghost[...], ghost[slot])
        totals = []
        for t, total in enumerate(bases):
            for n in range(n_nb):
                total = total + h[n] * gathered[n * columns:(n + 1) * columns, t * LANES:(t + 1) * LANES]
            totals.append(total)
        return jnp.concatenate(totals, 1)

    def coarse_copy(slot, k):
        d = offsets[k]
        return pltpu.make_async_remote_copy(
            src_ref=cext.at[slot, pl.ds(reach * c1, c1)],
            dst_ref=cext.at[slot, pl.ds((reach - d) * c1, c1)],
            send_sem=csend_sem.at[k],
            recv_sem=crecv_sem.at[slot, k],
            device_id=device(me + d),
            device_id_type=MESH,
        )

    coarse_round = [0]

    def coarse_apply(corr):
        slot = coarse_round[0] % 2
        coarse_round[0] += 1
        finish_sends("coarse", coarse_copy)
        cext[slot, pl.ds(reach * c1, c1), :] = corr
        for k in by_distance:
            @pl.when(valid(me + offsets[k]))
            def _():
                coarse_copy(slot, k).start()
        bases = []
        for part in halves(corr):
            lower, upper = shifted(part)
            bases.append(cdiag * part + cv0 * lower + cv1 * upper)
        pending["coarse"] = slot
        for k in range(n_slots):
            @pl.when(valid(me - offsets[k]))
            def _():
                coarse_copy(slot, k).wait_recv()
        gathered = select(mct, cext[slot])
        totals = []
        for t, total in enumerate(bases):
            for n in range(n_ch):
                total = total + cprep_v[3 + n] * gathered[n * c1:(n + 1) * c1, t * LANES:(t + 1) * LANES]
            totals.append(total)
        return jnp.concatenate(totals, 1)

    peers = sum(valid(me + d).astype(jnp.int32) for d in offsets)
    pl.semaphore_wait(barrier, peers)

    def per_half(x, coeff, op):
        return jnp.concatenate([op(part, coeff) for part in halves(x)], 1)

    solution = per_half(OMEGA * rhs, inv_diag, lambda x, c: x * c)
    for cycle_index in range(CYCLES):
        for sweep_index in range(PRE):
            if cycle_index == 0 and sweep_index == 0:
                continue
            step = OMEGA * (rhs - fine_apply(solution))
            solution = solution + per_half(step, inv_diag, lambda x, c: x * c)
        residual = rhs - fine_apply(solution)
        weighted = per_half(residual, w, lambda x, c: x * c)
        coarse_source = mm(at, weighted)
        correction = per_half(OMEGA * coarse_source, inv_cdiag, lambda x, c: x * c)
        for coarse_sweep_index in range(CSWEEPS - 1):
            step = OMEGA * (coarse_source - coarse_apply(correction))
            correction = correction + per_half(step, inv_cdiag, lambda x, c: x * c)
        lifted = mm(a, correction)
        solution = solution + per_half(lifted, w, lambda x, c: x * c)
        for sweep_index in range(POST):
            step = OMEGA * (rhs - fine_apply(solution))
            solution = solution + per_half(step, inv_diag, lambda x, c: x * c)
    finish_sends("fine", fine_copy)
    finish_sends("coarse", coarse_copy)
    for t, part in enumerate(halves(solution)):
        out_v[0, t] = jnp.transpose(part)[:layers]
    store = pltpu.make_async_copy(out_v, out_hbm, load_sem.at[len(loads)])
    store.start()
    store.wait()


def body(
    right_side,
    absorption,
    vertical,
    horizontal,
    neighbours,
    send_index,
    aggregate,
    weights,
    coarse_vertical,
    coarse_horizontal,
    coarse_neighbours,
    *,
    n_parts,
    n_grp,
):
    _, tracers, layers, columns = right_side.shape
    reach = send_index.shape[1] // 2
    width = send_index.shape[2]
    c1 = coarse_neighbours.shape[2]
    n_slots = 2 * reach

    cvert = coarse_vertical[0]
    chor = coarse_horizontal[0]
    coarse_diagonal = (
        0.5 + jnp.abs(cvert[0]) + jnp.abs(cvert[1]) + jnp.sum(jnp.abs(chor), axis=0)
    )
    layer = lax.broadcasted_iota(jnp.int32, (layers, 1), 0)
    cv0 = jnp.where(layer == 0, 0.0, cvert[0])
    cv1 = jnp.where(layer == layers - 1, 0.0, cvert[1])
    stacked = jnp.concatenate([coarse_diagonal[None], cv0[None], cv1[None], chor], 0)
    fill = jnp.concatenate(
        [
            jnp.ones((1, c1, LANES - layers), F32),
            jnp.zeros((2 + chor.shape[0], c1, LANES - layers), F32),
        ],
        0,
    )
    cprep = jnp.concatenate([jnp.transpose(stacked, (0, 2, 1)), fill], 2)

    si = send_index.reshape(1, n_slots * width)
    n_crow = coarse_neighbours.shape[1] * c1
    cnb = jnp.pad(
        coarse_neighbours.reshape(1, n_crow), ((0, 0), (0, LANES - n_crow)), constant_values=-1
    )

    args = (right_side, absorption, vertical, horizontal, weights, neighbours[0], si, aggregate, cnb, cprep)
    ext_rows = columns + n_slots * width
    coarse_rows = ext_rows
    scratch = [pltpu.VMEM(x.shape, x.dtype) for x in args] + [
        pltpu.VMEM(right_side.shape, F32),
        pltpu.SemaphoreType.DMA((len(args) + 1,)),
        pltpu.VMEM((neighbours.shape[1] * columns, 2 * columns), BF16),
        pltpu.VMEM((neighbours.shape[1] * columns, 2 * n_slots * width), BF16),
        pltpu.VMEM((2, n_slots * width, tracers * LANES), F32),
        pltpu.VMEM((n_slots * width, tracers * LANES), F32),
        pltpu.VMEM((2, coarse_rows, tracers * LANES), F32),
        pltpu.SemaphoreType.DMA((n_slots,)),
        pltpu.SemaphoreType.DMA((2, n_slots)),
        pltpu.SemaphoreType.DMA((n_slots,)),
        pltpu.SemaphoreType.DMA((2, n_slots)),
    ]
    return pl.pallas_call(
        functools.partial(vcycle_kernel, n_parts, n_grp, reach, width),
        out_shape=jax.ShapeDtypeStruct(right_side.shape, F32),
        in_specs=[pl.BlockSpec(memory_space=pl.ANY)] * len(args),
        out_specs=pl.BlockSpec(memory_space=pl.ANY),
        scratch_shapes=scratch,
        compiler_params=pltpu.CompilerParams(collective_id=0, has_side_effects=True),
    )(*args)


def solution(mesh):
    placed = (
        P(("dom", "grp"), None, None, None),
        P(("dom", "grp"), None, None),
        P(("dom", "grp"), None, None, None),
        P(("dom", "grp"), None, None, None),
        P(("dom", "grp"), None, None),
        P(("dom", "grp"), None, None),
        P(("dom", "grp"), None),
        P(("dom", "grp"), None, None),
        P(("dom", "grp"), None, None, None),
        P(("dom", "grp"), None, None, None),
        P(("dom", "grp"), None, None),
    )
    n_grp = mesh.shape["grp"]
    n_parts = mesh.shape["dom"] * n_grp
    return jax.shard_map(
        functools.partial(body, n_parts=n_parts, n_grp=n_grp),
        mesh=mesh,
        in_specs=placed,
        out_specs=P(("dom", "grp"), None, None, None),
        check_vma=False,
    )
```

```python
import functools

import jax
import jax.numpy as jnp
from jax import lax
from jax.experimental import pallas as pl
from jax.experimental.pallas import tpu as pltpu
from jax.sharding import PartitionSpec as P

CYCLES = 2
PRE = 2
POST = 2
CSWEEPS = 4

OMEGA = 0.8
HIGHEST = lax.Precision.HIGHEST
MESH = pl.DeviceIdType.MESH
LANES = 128
F32 = jnp.float32
BF16 = jnp.bfloat16


def mm(a, b):
    return jnp.dot(a, b, precision=HIGHEST, preferred_element_type=F32)


def select(onehot2, x):
    hi = x.astype(BF16)
    lo = (x - hi.astype(F32)).astype(BF16)
    return jnp.dot(onehot2, jnp.concatenate([hi, lo], 0), preferred_element_type=F32)


def doubled(onehot):
    return jnp.concatenate([onehot, onehot], 1)


def vcycle_kernel(
    n_parts,
    n_grp,
    reach,
    width,
    rhs_hbm,
    absorption_hbm,
    vertical_hbm,
    horizontal_hbm,
    weights_hbm,
    nb_hbm,
    si_hbm,
    agg_hbm,
    cnb_hbm,
    cvert_hbm,
    chor_hbm,
    out_hbm,
    rhs_v,
    absorption_v,
    vertical_v,
    horizontal_v,
    weights_v,
    nb_v,
    si_v,
    agg_v,
    cnb_v,
    cvert_v,
    chor_v,
    out_v,
    load_sem,
    mt_local,
    mt_ghost,
    ghost,
    sendbuf,
    cext,
    send_sem,
    recv_sem,
    csend_sem,
    crecv_sem,
):
    me = lax.axis_index("dom") * n_grp + lax.axis_index("grp")
    offsets = list(range(1, reach + 1)) + [-d for d in range(1, reach + 1)]
    n_slots = len(offsets)
    by_distance = sorted(range(n_slots), key=lambda s: (abs(offsets[s]) != 2, abs(offsets[s]) == reach, abs(offsets[s]), offsets[s] < 0))
    tracers, layers, columns = rhs_v.shape[1:]
    n_nb = nb_v.shape[0]
    c1 = cnb_v.shape[2]
    n_ch = chor_v.shape[1]
    halo = n_slots * width

    def valid(q):
        return jnp.logical_and(q >= 0, q < n_parts)

    def device(q):
        return (lax.div(q, n_grp), lax.rem(q, n_grp))

    loads = [
        pltpu.make_async_copy(src, dst, load_sem.at[i])
        for i, (src, dst) in enumerate(
            [
                (rhs_hbm, rhs_v),
                (absorption_hbm, absorption_v),
                (vertical_hbm, vertical_v),
                (horizontal_hbm, horizontal_v),
                (weights_hbm, weights_v),
                (nb_hbm, nb_v),
                (si_hbm, si_v),
                (agg_hbm, agg_v),
                (cnb_hbm, cnb_v),
                (cvert_hbm, cvert_v),
                (chor_hbm, chor_v),
            ]
        )
    ]
    for copy in loads:
        copy.start()

    ghost[...] = jnp.zeros_like(ghost)
    cext[...] = jnp.zeros_like(cext)

    barrier = pltpu.get_barrier_semaphore()
    for d in offsets:
        @pl.when(valid(me + d))
        def _():
            pl.semaphore_signal(barrier, 1, device_id=device(me + d), device_id_type=MESH)
    for copy in loads:
        copy.wait()

    lane = lax.broadcasted_iota(jnp.int32, (8, LANES), 1)
    probe = pltpu.roll(lane, 1, 1)
    expected = jnp.where(lane == 0, LANES - 1, lane - 1)
    forward = (probe == expected)[0:1, :]
    layer_lane = lax.broadcasted_iota(jnp.int32, (1, LANES), 1)
    live = layer_lane < layers

    def shifted(x):
        a = pltpu.roll(x, 1, 1)
        b = pltpu.roll(x, LANES - 1, 1)
        lower = jnp.where(forward, a, b)
        upper = jnp.where(forward, b, a)
        return lower, upper

    pad_rows = jnp.zeros((LANES - layers, columns), F32)

    def to_cols(slab):
        return jnp.transpose(jnp.concatenate([slab, pad_rows], 0))

    ab = absorption_v[0]
    vr0 = vertical_v[0, 0]
    vr1 = vertical_v[0, 1]
    diag_rows = ab + jnp.abs(vr0) + jnp.abs(vr1)
    hsum = jnp.abs(horizontal_v[0, 0])
    for n in range(1, horizontal_v.shape[1]):
        hsum = hsum + jnp.abs(horizontal_v[0, n])
    diag_rows = diag_rows + hsum
    diag = jnp.where(live, to_cols(diag_rows), 1.0)
    v0 = jnp.where(layer_lane == 0, 0.0, to_cols(vr0))
    v1 = jnp.where(layer_lane == layers - 1, 0.0, to_cols(vr1))
    h = [to_cols(horizontal_v[0, n]) for n in range(horizontal_v.shape[1])]
    w = to_cols(weights_v[0])
    rhs = jnp.concatenate([to_cols(rhs_v[0, t]) for t in range(tracers)], 1)

    ext_rows = columns + halo
    k_iota = lax.broadcasted_iota(jnp.int32, (ext_rows, columns), 0)
    for n in range(n_nb):
        chosen = jnp.transpose((k_iota == nb_v[n:n + 1, :]).astype(F32)).astype(BF16)
        rows = pl.ds(n * columns, columns)
        mt_local[rows, :] = doubled(chosen[:, :columns])
        mt_ghost[rows, :] = doubled(chosen[:, columns:])
    st_blocks = []
    for s in range(n_slots):
        block = (lax.broadcasted_iota(jnp.int32, (columns, width), 0) == si_v[0, s:s + 1, :]).astype(F32)
        st_blocks.append(jnp.transpose(block))
    st = doubled(jnp.concatenate(st_blocks, 0).astype(BF16))
    at = (lax.broadcasted_iota(jnp.int32, (c1, columns), 0) == agg_v[...]).astype(F32)
    a_full = jnp.transpose((lax.broadcasted_iota(jnp.int32, (LANES, columns), 0) == agg_v[...]).astype(F32))
    a = doubled(a_full[:, :c1].astype(BF16))
    coarse_rows = cext.shape[1]
    n_crow = n_ch * c1
    mct_blocks = []
    for n in range(n_ch):
        block = (lax.broadcasted_iota(jnp.int32, (coarse_rows, c1), 0) == cnb_v[0, n:n + 1, :]).astype(F32)
        mct_blocks.append(jnp.transpose(block))
    mct = doubled(jnp.concatenate(mct_blocks, 0).astype(BF16))

    coarse_pad = jnp.zeros((LANES - layers, c1), F32)

    def coarse_cols(slab):
        return jnp.transpose(jnp.concatenate([slab, coarse_pad], 0))

    cvr0 = cvert_v[0, 0]
    cvr1 = cvert_v[0, 1]
    cdiag_rows = 0.5 + jnp.abs(cvr0) + jnp.abs(cvr1)
    csum = jnp.abs(chor_v[0, 0])
    for n in range(1, n_ch):
        csum = csum + jnp.abs(chor_v[0, n])
    cdiag = jnp.where(live, coarse_cols(cdiag_rows + csum), 1.0)
    cv0 = jnp.where(layer_lane == 0, 0.0, coarse_cols(cvr0))
    cv1 = jnp.where(layer_lane == layers - 1, 0.0, coarse_cols(cvr1))
    ch = [coarse_cols(chor_v[0, n]) for n in range(n_ch)]
    inv_diag = 1.0 / diag
    inv_cdiag = 1.0 / cdiag

    def halves(x):
        return [x[:, t * LANES:(t + 1) * LANES] for t in range(x.shape[1] // LANES)]

    def fine_copy(slot, s):
        rows = pl.ds(s * width, width)
        return pltpu.make_async_remote_copy(
            src_ref=sendbuf.at[rows],
            dst_ref=ghost.at[slot, rows],
            send_sem=send_sem.at[s],
            recv_sem=recv_sem.at[slot, s],
            device_id=device(me + offsets[s]),
            device_id_type=MESH,
        )

    fine_round = [0]
    pending = {"fine": None, "coarse": None}

    def finish_sends(kind, copy_of):
        slot = pending[kind]
        if slot is None:
            return
        pending[kind] = None
        for s in range(n_slots):
            @pl.when(valid(me + offsets[s]))
            def _():
                copy_of(slot, s).wait_send()

    def fine_apply(field):
        slot = fine_round[0] % 2
        fine_round[0] += 1
        finish_sends("fine", fine_copy)
        sendbuf[...] = select(st, field)
        for s in by_distance:
            @pl.when(valid(me + offsets[s]))
            def _():
                fine_copy(slot, s).start()
        local = select(mt_local[...], field)
        bases = []
        for t, part in enumerate(halves(field)):
            lower, upper = shifted(part)
            total = diag * part + v0 * lower + v1 * upper
            for n in range(n_nb):
                total = total + h[n] * local[n * columns:(n + 1) * columns, t * LANES:(t + 1) * LANES]
            bases.append(total)
        pending["fine"] = slot
        for s in range(n_slots):
            @pl.when(valid(me - offsets[s]))
            def _():
                fine_copy(slot, s).wait_recv()
        gathered = select(mt_ghost[...], ghost[slot])
        totals = []
        for t, total in enumerate(bases):
            for n in range(n_nb):
                total = total + h[n] * gathered[n * columns:(n + 1) * columns, t * LANES:(t + 1) * LANES]
            totals.append(total)
        return jnp.concatenate(totals, 1)

    def coarse_copy(slot, k):
        d = offsets[k]
        return pltpu.make_async_remote_copy(
            src_ref=cext.at[slot, pl.ds(reach * c1, c1)],
            dst_ref=cext.at[slot, pl.ds((reach - d) * c1, c1)],
            send_sem=csend_sem.at[k],
            recv_sem=crecv_sem.at[slot, k],
            device_id=device(me + d),
            device_id_type=MESH,
        )

    coarse_round = [0]

    def coarse_apply(corr):
        slot = coarse_round[0] % 2
        coarse_round[0] += 1
        finish_sends("coarse", coarse_copy)
        cext[slot, pl.ds(reach * c1, c1), :] = corr
        for k in by_distance:
            @pl.when(valid(me + offsets[k]))
            def _():
                coarse_copy(slot, k).start()
        bases = []
        for part in halves(corr):
            lower, upper = shifted(part)
            bases.append(cdiag * part + cv0 * lower + cv1 * upper)
        pending["coarse"] = slot
        for k in range(n_slots):
            @pl.when(valid(me - offsets[k]))
            def _():
                coarse_copy(slot, k).wait_recv()
        gathered = select(mct, cext[slot])
        totals = []
        for t, total in enumerate(bases):
            for n in range(n_ch):
                total = total + ch[n] * gathered[n * c1:(n + 1) * c1, t * LANES:(t + 1) * LANES]
            totals.append(total)
        return jnp.concatenate(totals, 1)

    peers = sum(valid(me + d).astype(jnp.int32) for d in offsets)
    pl.semaphore_wait(barrier, peers)

    def per_half(x, coeff, op):
        return jnp.concatenate([op(part, coeff) for part in halves(x)], 1)

    solution = per_half(OMEGA * rhs, inv_diag, lambda x, c: x * c)
    for cycle_index in range(CYCLES):
        for sweep_index in range(PRE):
            if cycle_index == 0 and sweep_index == 0:
                continue
            step = OMEGA * (rhs - fine_apply(solution))
            solution = solution + per_half(step, inv_diag, lambda x, c: x * c)
        residual = rhs - fine_apply(solution)
        weighted = per_half(residual, w, lambda x, c: x * c)
        coarse_source = mm(at, weighted)
        correction = per_half(OMEGA * coarse_source, inv_cdiag, lambda x, c: x * c)
        for coarse_sweep_index in range(CSWEEPS - 1):
            step = OMEGA * (coarse_source - coarse_apply(correction))
            correction = correction + per_half(step, inv_cdiag, lambda x, c: x * c)
        lifted = select(a, correction)
        solution = solution + per_half(lifted, w, lambda x, c: x * c)
        for sweep_index in range(POST):
            step = OMEGA * (rhs - fine_apply(solution))
            solution = solution + per_half(step, inv_diag, lambda x, c: x * c)
    finish_sends("fine", fine_copy)
    finish_sends("coarse", coarse_copy)
    for t, part in enumerate(halves(solution)):
        out_v[0, t] = jnp.transpose(part)[:layers]
    store = pltpu.make_async_copy(out_v, out_hbm, load_sem.at[len(loads)])
    store.start()
    store.wait()


def body(
    right_side,
    absorption,
    vertical,
    horizontal,
    neighbours,
    send_index,
    aggregate,
    weights,
    coarse_vertical,
    coarse_horizontal,
    coarse_neighbours,
    *,
    n_parts,
    n_grp,
):
    _, tracers, layers, columns = right_side.shape
    reach = send_index.shape[1] // 2
    width = send_index.shape[2]
    c1 = coarse_neighbours.shape[2]
    n_slots = 2 * reach

    args = (right_side, absorption, vertical, horizontal, weights, neighbours[0], send_index, aggregate, coarse_neighbours, coarse_vertical, coarse_horizontal)
    ext_rows = columns + n_slots * width
    coarse_rows = ext_rows
    scratch = [pltpu.VMEM(x.shape, x.dtype) for x in args] + [
        pltpu.VMEM(right_side.shape, F32),
        pltpu.SemaphoreType.DMA((len(args) + 1,)),
        pltpu.VMEM((neighbours.shape[1] * columns, 2 * columns), BF16),
        pltpu.VMEM((neighbours.shape[1] * columns, 2 * n_slots * width), BF16),
        pltpu.VMEM((2, n_slots * width, tracers * LANES), F32),
        pltpu.VMEM((n_slots * width, tracers * LANES), F32),
        pltpu.VMEM((2, coarse_rows, tracers * LANES), F32),
        pltpu.SemaphoreType.DMA((n_slots,)),
        pltpu.SemaphoreType.DMA((2, n_slots)),
        pltpu.SemaphoreType.DMA((n_slots,)),
        pltpu.SemaphoreType.DMA((2, n_slots)),
    ]
    return pl.pallas_call(
        functools.partial(vcycle_kernel, n_parts, n_grp, reach, width),
        out_shape=jax.ShapeDtypeStruct(right_side.shape, F32),
        in_specs=[pl.BlockSpec(memory_space=pl.ANY)] * len(args),
        out_specs=pl.BlockSpec(memory_space=pl.ANY),
        scratch_shapes=scratch,
        compiler_params=pltpu.CompilerParams(collective_id=0, has_side_effects=True),
    )(*args)


def solution(mesh):
    placed = (
        P(("dom", "grp"), None, None, None),
        P(("dom", "grp"), None, None),
        P(("dom", "grp"), None, None, None),
        P(("dom", "grp"), None, None, None),
        P(("dom", "grp"), None, None),
        P(("dom", "grp"), None, None),
        P(("dom", "grp"), None),
        P(("dom", "grp"), None, None),
        P(("dom", "grp"), None, None, None),
        P(("dom", "grp"), None, None, None),
        P(("dom", "grp"), None, None),
    )
    n_grp = mesh.shape["grp"]
    n_parts = mesh.shape["dom"] * n_grp
    return jax.shard_map(
        functools.partial(body, n_parts=n_parts, n_grp=n_grp),
        mesh=mesh,
        in_specs=placed,
        out_specs=P(("dom", "grp"), None, None, None),
        check_vma=False,
    )
```

```python
import functools

import jax
import jax.numpy as jnp
from jax import lax
from jax.experimental import pallas as pl
from jax.experimental.pallas import tpu as pltpu
from jax.sharding import PartitionSpec as P

CYCLES = 2
PRE = 2
POST = 2
CSWEEPS = 4

OMEGA = 0.8
HIGHEST = lax.Precision.HIGHEST
MESH = pl.DeviceIdType.MESH
LANES = 128
F32 = jnp.float32
BF16 = jnp.bfloat16


def mm(a, b):
    return jnp.dot(a, b, precision=HIGHEST, preferred_element_type=F32)


def select(onehot2, x):
    hi = x.astype(BF16)
    lo = (x - hi.astype(F32)).astype(BF16)
    return jnp.dot(onehot2, jnp.concatenate([hi, lo], 0), preferred_element_type=F32)


def doubled(onehot):
    return jnp.concatenate([onehot, onehot], 1)


def vcycle_kernel(
    n_parts,
    n_grp,
    reach,
    width,
    rhs_hbm,
    absorption_hbm,
    vertical_hbm,
    horizontal_hbm,
    weights_hbm,
    nb_hbm,
    si_hbm,
    agg_hbm,
    cnb_hbm,
    cvert_hbm,
    chor_hbm,
    out_hbm,
    rhs_v,
    absorption_v,
    vertical_v,
    horizontal_v,
    weights_v,
    nb_v,
    si_v,
    agg_v,
    cnb_v,
    cvert_v,
    chor_v,
    out_v,
    load_sem,
    mt_local,
    mt_ghost,
    ghost,
    sendbuf,
    cext,
    send_sem,
    recv_sem,
    csend_sem,
    crecv_sem,
):
    me = lax.axis_index("dom") * n_grp + lax.axis_index("grp")
    offsets = list(range(1, reach + 1)) + [-d for d in range(1, reach + 1)]
    n_slots = len(offsets)
    by_distance = sorted(range(n_slots), key=lambda s: (abs(offsets[s]) != 2, abs(offsets[s]) == reach, abs(offsets[s]), offsets[s] < 0))
    tracers, layers, columns = rhs_v.shape[1:]
    n_nb = nb_v.shape[0]
    c1 = cnb_v.shape[2]
    n_ch = chor_v.shape[1]
    halo = n_slots * width

    def valid(q):
        return jnp.logical_and(q >= 0, q < n_parts)

    def device(q):
        return (lax.div(q, n_grp), lax.rem(q, n_grp))

    loads = [
        pltpu.make_async_copy(src, dst, load_sem.at[i])
        for i, (src, dst) in enumerate(
            [
                (rhs_hbm, rhs_v),
                (absorption_hbm, absorption_v),
                (vertical_hbm, vertical_v),
                (horizontal_hbm, horizontal_v),
                (weights_hbm, weights_v),
                (nb_hbm, nb_v),
                (si_hbm, si_v),
                (agg_hbm, agg_v),
                (cnb_hbm, cnb_v),
                (cvert_hbm, cvert_v),
                (chor_hbm, chor_v),
            ]
        )
    ]
    for copy in loads:
        copy.start()

    ghost[...] = jnp.zeros_like(ghost)
    cext[...] = jnp.zeros_like(cext)

    barrier = pltpu.get_barrier_semaphore()
    for d in offsets:
        @pl.when(valid(me + d))
        def _():
            pl.semaphore_signal(barrier, 1, device_id=device(me + d), device_id_type=MESH)
    for copy in loads:
        copy.wait()

    lane = lax.broadcasted_iota(jnp.int32, (8, LANES), 1)
    probe = pltpu.roll(lane, 1, 1)
    expected = jnp.where(lane == 0, LANES - 1, lane - 1)
    forward = (probe == expected)[0:1, :]
    layer_lane = lax.broadcasted_iota(jnp.int32, (1, LANES), 1)
    live = layer_lane < layers

    def shifted(x):
        a = pltpu.roll(x, 1, 1)
        b = pltpu.roll(x, LANES - 1, 1)
        lower = jnp.where(forward, a, b)
        upper = jnp.where(forward, b, a)
        return lower, upper

    pad_rows = jnp.zeros((LANES - layers, columns), F32)

    def to_cols(slab):
        return jnp.transpose(jnp.concatenate([slab, pad_rows], 0))

    ab = absorption_v[0]
    vr0 = vertical_v[0, 0]
    vr1 = vertical_v[0, 1]
    diag_rows = ab + jnp.abs(vr0) + jnp.abs(vr1)
    hsum = jnp.abs(horizontal_v[0, 0])
    for n in range(1, horizontal_v.shape[1]):
        hsum = hsum + jnp.abs(horizontal_v[0, n])
    diag_rows = diag_rows + hsum
    diag = jnp.where(live, to_cols(diag_rows), 1.0)
    v0 = jnp.where(layer_lane == 0, 0.0, to_cols(vr0))
    v1 = jnp.where(layer_lane == layers - 1, 0.0, to_cols(vr1))
    h = [to_cols(horizontal_v[0, n]) for n in range(horizontal_v.shape[1])]
    w = to_cols(weights_v[0])
    rhs = jnp.concatenate([to_cols(rhs_v[0, t]) for t in range(tracers)], 1)

    ext_rows = columns + halo
    k_iota = lax.broadcasted_iota(jnp.int32, (ext_rows, columns), 0)
    for n in range(n_nb):
        chosen = jnp.transpose((k_iota == nb_v[n]).astype(F32)).astype(BF16)
        rows = pl.ds(n * columns, columns)
        mt_local[rows, :] = doubled(chosen[:, :columns])
        mt_ghost[rows, :] = doubled(chosen[:, columns:])
    st_blocks = []
    for s in range(n_slots):
        block = (lax.broadcasted_iota(jnp.int32, (columns, width), 0) == si_v[0, s:s + 1, :]).astype(F32)
        st_blocks.append(jnp.transpose(block))
    st = doubled(jnp.concatenate(st_blocks, 0).astype(BF16))
    at = (lax.broadcasted_iota(jnp.int32, (c1, columns), 0) == agg_v[...]).astype(F32)
    a_full = jnp.transpose((lax.broadcasted_iota(jnp.int32, (LANES, columns), 0) == agg_v[...]).astype(F32))
    a = doubled(a_full[:, :c1].astype(BF16))
    coarse_rows = cext.shape[1]
    n_crow = n_ch * c1
    mct_blocks = []
    for n in range(n_ch):
        block = (lax.broadcasted_iota(jnp.int32, (coarse_rows, c1), 0) == cnb_v[n]).astype(F32)
        mct_blocks.append(jnp.transpose(block))
    mct = doubled(jnp.concatenate(mct_blocks, 0).astype(BF16))

    widen = (
        lax.broadcasted_iota(jnp.int32, (layers, LANES), 0) == lax.broadcasted_iota(jnp.int32, (layers, LANES), 1)
    ).astype(F32)

    def coarse_cols(slab):
        return mm(slab, widen)

    cvr0 = cvert_v[0, 0]
    cvr1 = cvert_v[0, 1]
    cdiag_rows = 0.5 + jnp.abs(cvr0) + jnp.abs(cvr1)
    csum = jnp.abs(chor_v[0, 0])
    for n in range(1, n_ch):
        csum = csum + jnp.abs(chor_v[0, n])
    cdiag = jnp.where(live, coarse_cols(cdiag_rows + csum), 1.0)
    cv0 = jnp.where(layer_lane == 0, 0.0, coarse_cols(cvr0))
    cv1 = jnp.where(layer_lane == layers - 1, 0.0, coarse_cols(cvr1))
    ch = [coarse_cols(chor_v[0, n]) for n in range(n_ch)]
    inv_diag = 1.0 / diag
    inv_cdiag = 1.0 / cdiag

    def halves(x):
        return [x[:, t * LANES:(t + 1) * LANES] for t in range(x.shape[1] // LANES)]

    def fine_copy(slot, s):
        rows = pl.ds(s * width, width)
        return pltpu.make_async_remote_copy(
            src_ref=sendbuf.at[rows],
            dst_ref=ghost.at[slot, rows],
            send_sem=send_sem.at[s],
            recv_sem=recv_sem.at[slot, s],
            device_id=device(me + offsets[s]),
            device_id_type=MESH,
        )

    fine_round = [0]
    pending = {"fine": None, "coarse": None}

    def finish_sends(kind, copy_of):
        slot = pending[kind]
        if slot is None:
            return
        pending[kind] = None
        for s in range(n_slots):
            @pl.when(valid(me + offsets[s]))
            def _():
                copy_of(slot, s).wait_send()

    def fine_apply(field):
        slot = fine_round[0] % 2
        fine_round[0] += 1
        finish_sends("fine", fine_copy)
        sendbuf[...] = select(st, field)
        for s in by_distance:
            @pl.when(valid(me + offsets[s]))
            def _():
                fine_copy(slot, s).start()
        local = select(mt_local[...], field)
        bases = []
        for t, part in enumerate(halves(field)):
            lower, upper = shifted(part)
            total = diag * part + v0 * lower + v1 * upper
            for n in range(n_nb):
                total = total + h[n] * local[n * columns:(n + 1) * columns, t * LANES:(t + 1) * LANES]
            bases.append(total)
        pending["fine"] = slot
        for s in range(n_slots):
            @pl.when(valid(me - offsets[s]))
            def _():
                fine_copy(slot, s).wait_recv()
        gathered = select(mt_ghost[...], ghost[slot])
        totals = []
        for t, total in enumerate(bases):
            for n in range(n_nb):
                total = total + h[n] * gathered[n * columns:(n + 1) * columns, t * LANES:(t + 1) * LANES]
            totals.append(total)
        return jnp.concatenate(totals, 1)

    def coarse_copy(slot, k):
        d = offsets[k]
        return pltpu.make_async_remote_copy(
            src_ref=cext.at[slot, pl.ds(reach * c1, c1)],
            dst_ref=cext.at[slot, pl.ds((reach - d) * c1, c1)],
            send_sem=csend_sem.at[k],
            recv_sem=crecv_sem.at[slot, k],
            device_id=device(me + d),
            device_id_type=MESH,
        )

    coarse_round = [0]

    def coarse_apply(corr):
        slot = coarse_round[0] % 2
        coarse_round[0] += 1
        finish_sends("coarse", coarse_copy)
        cext[slot, pl.ds(reach * c1, c1), :] = corr
        for k in by_distance:
            @pl.when(valid(me + offsets[k]))
            def _():
                coarse_copy(slot, k).start()
        bases = []
        for part in halves(corr):
            lower, upper = shifted(part)
            bases.append(cdiag * part + cv0 * lower + cv1 * upper)
        pending["coarse"] = slot
        for k in range(n_slots):
            @pl.when(valid(me - offsets[k]))
            def _():
                coarse_copy(slot, k).wait_recv()
        gathered = select(mct, cext[slot])
        totals = []
        for t, total in enumerate(bases):
            for n in range(n_ch):
                total = total + ch[n] * gathered[n * c1:(n + 1) * c1, t * LANES:(t + 1) * LANES]
            totals.append(total)
        return jnp.concatenate(totals, 1)

    peers = sum(valid(me + d).astype(jnp.int32) for d in offsets)
    pl.semaphore_wait(barrier, peers)

    def per_half(x, coeff, op):
        return jnp.concatenate([op(part, coeff) for part in halves(x)], 1)

    solution = per_half(OMEGA * rhs, inv_diag, lambda x, c: x * c)
    for cycle_index in range(CYCLES):
        for sweep_index in range(PRE):
            if cycle_index == 0 and sweep_index == 0:
                continue
            step = OMEGA * (rhs - fine_apply(solution))
            solution = solution + per_half(step, inv_diag, lambda x, c: x * c)
        residual = rhs - fine_apply(solution)
        weighted = per_half(residual, w, lambda x, c: x * c)
        coarse_source = mm(at, weighted)
        correction = per_half(OMEGA * coarse_source, inv_cdiag, lambda x, c: x * c)
        for coarse_sweep_index in range(CSWEEPS - 1):
            step = OMEGA * (coarse_source - coarse_apply(correction))
            correction = correction + per_half(step, inv_cdiag, lambda x, c: x * c)
        lifted = select(a, correction)
        solution = solution + per_half(lifted, w, lambda x, c: x * c)
        for sweep_index in range(POST):
            step = OMEGA * (rhs - fine_apply(solution))
            solution = solution + per_half(step, inv_diag, lambda x, c: x * c)
    finish_sends("fine", fine_copy)
    finish_sends("coarse", coarse_copy)
    for t, part in enumerate(halves(solution)):
        out_v[0, t] = jnp.transpose(part)[:layers]
    store = pltpu.make_async_copy(out_v, out_hbm, load_sem.at[len(loads)])
    store.start()
    store.wait()


def body(
    right_side,
    absorption,
    vertical,
    horizontal,
    neighbours,
    send_index,
    aggregate,
    weights,
    coarse_vertical,
    coarse_horizontal,
    coarse_neighbours,
    *,
    n_parts,
    n_grp,
):
    _, tracers, layers, columns = right_side.shape
    reach = send_index.shape[1] // 2
    width = send_index.shape[2]
    c1 = coarse_neighbours.shape[2]
    n_slots = 2 * reach

    args = (
        right_side,
        absorption,
        vertical,
        horizontal,
        weights,
        jnp.swapaxes(neighbours, 0, 1),
        send_index,
        aggregate,
        jnp.swapaxes(coarse_neighbours, 0, 1),
        jnp.swapaxes(coarse_vertical, 2, 3),
        jnp.swapaxes(coarse_horizontal, 2, 3),
    )
    ext_rows = columns + n_slots * width
    coarse_rows = ext_rows
    scratch = [pltpu.VMEM(x.shape, x.dtype) for x in args] + [
        pltpu.VMEM(right_side.shape, F32),
        pltpu.SemaphoreType.DMA((len(args) + 1,)),
        pltpu.VMEM((neighbours.shape[1] * columns, 2 * columns), BF16),
        pltpu.VMEM((neighbours.shape[1] * columns, 2 * n_slots * width), BF16),
        pltpu.VMEM((2, n_slots * width, tracers * LANES), F32),
        pltpu.VMEM((n_slots * width, tracers * LANES), F32),
        pltpu.VMEM((2, coarse_rows, tracers * LANES), F32),
        pltpu.SemaphoreType.DMA((n_slots,)),
        pltpu.SemaphoreType.DMA((2, n_slots)),
        pltpu.SemaphoreType.DMA((n_slots,)),
        pltpu.SemaphoreType.DMA((2, n_slots)),
    ]
    return pl.pallas_call(
        functools.partial(vcycle_kernel, n_parts, n_grp, reach, width),
        out_shape=jax.ShapeDtypeStruct(right_side.shape, F32),
        in_specs=[pl.BlockSpec(memory_space=pl.ANY)] * len(args),
        out_specs=pl.BlockSpec(memory_space=pl.ANY),
        scratch_shapes=scratch,
        compiler_params=pltpu.CompilerParams(collective_id=0, has_side_effects=True),
    )(*args)


def solution(mesh):
    placed = (
        P(("dom", "grp"), None, None, None),
        P(("dom", "grp"), None, None),
        P(("dom", "grp"), None, None, None),
        P(("dom", "grp"), None, None, None),
        P(("dom", "grp"), None, None),
        P(("dom", "grp"), None, None),
        P(("dom", "grp"), None),
        P(("dom", "grp"), None, None),
        P(("dom", "grp"), None, None, None),
        P(("dom", "grp"), None, None, None),
        P(("dom", "grp"), None, None),
    )
    n_grp = mesh.shape["grp"]
    n_parts = mesh.shape["dom"] * n_grp
    return jax.shard_map(
        functools.partial(body, n_parts=n_parts, n_grp=n_grp),
        mesh=mesh,
        in_specs=placed,
        out_specs=P(("dom", "grp"), None, None, None),
        check_vma=False,
    )
```

```python
import functools

import jax
import jax.numpy as jnp
from jax import lax
from jax.experimental import pallas as pl
from jax.experimental.pallas import tpu as pltpu
from jax.sharding import PartitionSpec as P

CYCLES = 2
PRE = 2
POST = 2
CSWEEPS = 4

OMEGA = 0.8
HIGHEST = lax.Precision.HIGHEST
MESH = pl.DeviceIdType.MESH
LANES = 128
F32 = jnp.float32
BF16 = jnp.bfloat16


def mm(a, b):
    return jnp.dot(a, b, precision=HIGHEST, preferred_element_type=F32)


def select(onehot2, x):
    hi = x.astype(BF16)
    lo = (x - hi.astype(F32)).astype(BF16)
    return jnp.dot(onehot2, jnp.concatenate([hi, lo], 0), preferred_element_type=F32)


def doubled(onehot):
    return jnp.concatenate([onehot, onehot], 1)


def vcycle_kernel(
    n_parts,
    n_grp,
    reach,
    width,
    rhs_hbm,
    absorption_hbm,
    vertical_hbm,
    horizontal_hbm,
    weights_hbm,
    nb_hbm,
    si_hbm,
    agg_hbm,
    cnb_hbm,
    cvert_hbm,
    chor_hbm,
    out_hbm,
    rhs_v,
    absorption_v,
    vertical_v,
    horizontal_v,
    weights_v,
    nb_v,
    si_v,
    agg_v,
    cnb_v,
    cvert_v,
    chor_v,
    out_v,
    load_sem,
    mt_local,
    mt_ghost,
    ghost,
    sendbuf,
    cext,
    send_sem,
    recv_sem,
    csend_sem,
    crecv_sem,
):
    me = lax.axis_index("dom") * n_grp + lax.axis_index("grp")
    offsets = list(range(1, reach + 1)) + [-d for d in range(1, reach + 1)]
    n_slots = len(offsets)
    by_distance = sorted(range(n_slots), key=lambda s: (abs(offsets[s]) != 2, abs(offsets[s]) == reach, abs(offsets[s]), offsets[s] < 0))
    tracers, layers, columns = rhs_v.shape[1:]
    n_nb = nb_v.shape[0]
    c1 = cnb_v.shape[2]
    n_ch = chor_v.shape[1]
    halo = n_slots * width

    def valid(q):
        return jnp.logical_and(q >= 0, q < n_parts)

    def device(q):
        return (lax.div(q, n_grp), lax.rem(q, n_grp))

    loads = [
        pltpu.make_async_copy(src, dst, load_sem.at[i])
        for i, (src, dst) in enumerate(
            [
                (rhs_hbm, rhs_v),
                (absorption_hbm, absorption_v),
                (vertical_hbm, vertical_v),
                (horizontal_hbm, horizontal_v),
                (weights_hbm, weights_v),
                (nb_hbm, nb_v),
                (si_hbm, si_v),
                (agg_hbm, agg_v),
                (cnb_hbm, cnb_v),
                (cvert_hbm, cvert_v),
                (chor_hbm, chor_v),
            ]
        )
    ]
    for copy in loads:
        copy.start()

    ghost[...] = jnp.zeros_like(ghost)
    cext[...] = jnp.zeros_like(cext)

    barrier = pltpu.get_barrier_semaphore()
    for d in offsets:
        @pl.when(valid(me + d))
        def _():
            pl.semaphore_signal(barrier, 1, device_id=device(me + d), device_id_type=MESH)
    for copy in loads:
        copy.wait()

    lane = lax.broadcasted_iota(jnp.int32, (8, LANES), 1)
    probe = pltpu.roll(lane, 1, 1)
    expected = jnp.where(lane == 0, LANES - 1, lane - 1)
    forward = (probe == expected)[0:1, :]
    layer_lane = lax.broadcasted_iota(jnp.int32, (1, LANES), 1)
    live = layer_lane < layers

    def shifted(x):
        a = pltpu.roll(x, 1, 1)
        b = pltpu.roll(x, LANES - 1, 1)
        lower = jnp.where(forward, a, b)
        upper = jnp.where(forward, b, a)
        return lower, upper

    pad_rows = jnp.zeros((LANES - layers, columns), F32)

    def to_cols(slab):
        return jnp.transpose(jnp.concatenate([slab, pad_rows], 0))

    ab = absorption_v[0]
    vr0 = vertical_v[0, 0]
    vr1 = vertical_v[0, 1]
    diag_rows = ab + jnp.abs(vr0) + jnp.abs(vr1)
    hsum = jnp.abs(horizontal_v[0, 0])
    for n in range(1, horizontal_v.shape[1]):
        hsum = hsum + jnp.abs(horizontal_v[0, n])
    diag_rows = diag_rows + hsum
    diag = jnp.where(live, to_cols(diag_rows), 1.0)
    inv_diag = 1.0 / diag
    rhs = jnp.concatenate([to_cols(rhs_v[0, t]) for t in range(tracers)], 1)
    st_blocks = []
    for s in range(n_slots):
        block = (lax.broadcasted_iota(jnp.int32, (columns, width), 0) == si_v[0, s:s + 1, :]).astype(F32)
        st_blocks.append(jnp.transpose(block))
    st = doubled(jnp.concatenate(st_blocks, 0).astype(BF16))
    ctx = {}

    def fine_setup():
        ctx["v0"] = jnp.where(layer_lane == 0, 0.0, to_cols(vr0))
        ctx["v1"] = jnp.where(layer_lane == layers - 1, 0.0, to_cols(vr1))
        ctx["h"] = [to_cols(horizontal_v[0, n]) for n in range(horizontal_v.shape[1])]
        k_iota = lax.broadcasted_iota(jnp.int32, (columns + halo, columns), 0)
        for n in range(n_nb):
            chosen = jnp.transpose((k_iota == nb_v[n]).astype(F32)).astype(BF16)
            rows = pl.ds(n * columns, columns)
            mt_local[rows, :] = doubled(chosen[:, :columns])
            mt_ghost[rows, :] = doubled(chosen[:, columns:])

    def coarse_setup():
        ctx["w"] = to_cols(weights_v[0])
        ctx["at"] = (lax.broadcasted_iota(jnp.int32, (c1, columns), 0) == agg_v[...]).astype(F32)
        a_full = jnp.transpose((lax.broadcasted_iota(jnp.int32, (LANES, columns), 0) == agg_v[...]).astype(F32))
        ctx["a"] = doubled(a_full[:, :c1].astype(BF16))
        coarse_rows = cext.shape[1]
        mct_blocks = []
        for n in range(n_ch):
            block = (lax.broadcasted_iota(jnp.int32, (coarse_rows, c1), 0) == cnb_v[n]).astype(F32)
            mct_blocks.append(jnp.transpose(block))
        ctx["mct"] = doubled(jnp.concatenate(mct_blocks, 0).astype(BF16))
        widen = (
            lax.broadcasted_iota(jnp.int32, (layers, LANES), 0) == lax.broadcasted_iota(jnp.int32, (layers, LANES), 1)
        ).astype(F32)

        def coarse_cols(slab):
            return mm(slab, widen)

        cvr0 = cvert_v[0, 0]
        cvr1 = cvert_v[0, 1]
        cdiag_rows = 0.5 + jnp.abs(cvr0) + jnp.abs(cvr1)
        csum = jnp.abs(chor_v[0, 0])
        for n in range(1, n_ch):
            csum = csum + jnp.abs(chor_v[0, n])
        cdiag = jnp.where(live, coarse_cols(cdiag_rows + csum), 1.0)
        ctx["cdiag"] = cdiag
        ctx["inv_cdiag"] = 1.0 / cdiag
        ctx["cv0"] = jnp.where(layer_lane == 0, 0.0, coarse_cols(cvr0))
        ctx["cv1"] = jnp.where(layer_lane == layers - 1, 0.0, coarse_cols(cvr1))
        ctx["ch"] = [coarse_cols(chor_v[0, n]) for n in range(n_ch)]

    setup_hooks = [fine_setup, coarse_setup]

    def halves(x):
        return [x[:, t * LANES:(t + 1) * LANES] for t in range(x.shape[1] // LANES)]

    def fine_copy(slot, s):
        rows = pl.ds(s * width, width)
        return pltpu.make_async_remote_copy(
            src_ref=sendbuf.at[rows],
            dst_ref=ghost.at[slot, rows],
            send_sem=send_sem.at[s],
            recv_sem=recv_sem.at[slot, s],
            device_id=device(me + offsets[s]),
            device_id_type=MESH,
        )

    fine_round = [0]
    pending = {"fine": None, "coarse": None}

    def finish_sends(kind, copy_of):
        slot = pending[kind]
        if slot is None:
            return
        pending[kind] = None
        for s in range(n_slots):
            @pl.when(valid(me + offsets[s]))
            def _():
                copy_of(slot, s).wait_send()

    def fine_apply(field):
        slot = fine_round[0] % 2
        fine_round[0] += 1
        finish_sends("fine", fine_copy)
        sendbuf[...] = select(st, field)
        for s in by_distance:
            @pl.when(valid(me + offsets[s]))
            def _():
                fine_copy(slot, s).start()
        if setup_hooks:
            setup_hooks.pop(0)()
        v0, v1, h = ctx["v0"], ctx["v1"], ctx["h"]
        local = select(mt_local[...], field)
        bases = []
        for t, part in enumerate(halves(field)):
            lower, upper = shifted(part)
            total = diag * part + v0 * lower + v1 * upper
            for n in range(n_nb):
                total = total + h[n] * local[n * columns:(n + 1) * columns, t * LANES:(t + 1) * LANES]
            bases.append(total)
        pending["fine"] = slot
        for s in range(n_slots):
            @pl.when(valid(me - offsets[s]))
            def _():
                fine_copy(slot, s).wait_recv()
        gathered = select(mt_ghost[...], ghost[slot])
        totals = []
        for t, total in enumerate(bases):
            for n in range(n_nb):
                total = total + h[n] * gathered[n * columns:(n + 1) * columns, t * LANES:(t + 1) * LANES]
            totals.append(total)
        return jnp.concatenate(totals, 1)

    def coarse_copy(slot, k):
        d = offsets[k]
        return pltpu.make_async_remote_copy(
            src_ref=cext.at[slot, pl.ds(reach * c1, c1)],
            dst_ref=cext.at[slot, pl.ds((reach - d) * c1, c1)],
            send_sem=csend_sem.at[k],
            recv_sem=crecv_sem.at[slot, k],
            device_id=device(me + d),
            device_id_type=MESH,
        )

    coarse_round = [0]

    def coarse_apply(corr):
        slot = coarse_round[0] % 2
        coarse_round[0] += 1
        finish_sends("coarse", coarse_copy)
        cext[slot, pl.ds(reach * c1, c1), :] = corr
        cdiag, cv0, cv1, ch, mct = ctx["cdiag"], ctx["cv0"], ctx["cv1"], ctx["ch"], ctx["mct"]
        for k in by_distance:
            @pl.when(valid(me + offsets[k]))
            def _():
                coarse_copy(slot, k).start()
        bases = []
        for part in halves(corr):
            lower, upper = shifted(part)
            bases.append(cdiag * part + cv0 * lower + cv1 * upper)
        pending["coarse"] = slot
        for k in range(n_slots):
            @pl.when(valid(me - offsets[k]))
            def _():
                coarse_copy(slot, k).wait_recv()
        gathered = select(mct, cext[slot])
        totals = []
        for t, total in enumerate(bases):
            for n in range(n_ch):
                total = total + ch[n] * gathered[n * c1:(n + 1) * c1, t * LANES:(t + 1) * LANES]
            totals.append(total)
        return jnp.concatenate(totals, 1)

    peers = sum(valid(me + d).astype(jnp.int32) for d in offsets)
    pl.semaphore_wait(barrier, peers)

    def per_half(x, coeff, op):
        return jnp.concatenate([op(part, coeff) for part in halves(x)], 1)

    solution = per_half(OMEGA * rhs, inv_diag, lambda x, c: x * c)
    for cycle_index in range(CYCLES):
        for sweep_index in range(PRE):
            if cycle_index == 0 and sweep_index == 0:
                continue
            step = OMEGA * (rhs - fine_apply(solution))
            solution = solution + per_half(step, inv_diag, lambda x, c: x * c)
        residual = rhs - fine_apply(solution)
        weighted = per_half(residual, ctx["w"], lambda x, c: x * c)
        coarse_source = mm(ctx["at"], weighted)
        correction = per_half(OMEGA * coarse_source, ctx["inv_cdiag"], lambda x, c: x * c)
        for coarse_sweep_index in range(CSWEEPS - 1):
            step = OMEGA * (coarse_source - coarse_apply(correction))
            correction = correction + per_half(step, ctx["inv_cdiag"], lambda x, c: x * c)
        lifted = select(ctx["a"], correction)
        solution = solution + per_half(lifted, ctx["w"], lambda x, c: x * c)
        for sweep_index in range(POST):
            step = OMEGA * (rhs - fine_apply(solution))
            solution = solution + per_half(step, inv_diag, lambda x, c: x * c)
    finish_sends("fine", fine_copy)
    finish_sends("coarse", coarse_copy)
    for t, part in enumerate(halves(solution)):
        out_v[0, t] = jnp.transpose(part)[:layers]
    store = pltpu.make_async_copy(out_v, out_hbm, load_sem.at[len(loads)])
    store.start()
    store.wait()


def body(
    right_side,
    absorption,
    vertical,
    horizontal,
    neighbours,
    send_index,
    aggregate,
    weights,
    coarse_vertical,
    coarse_horizontal,
    coarse_neighbours,
    *,
    n_parts,
    n_grp,
):
    _, tracers, layers, columns = right_side.shape
    reach = send_index.shape[1] // 2
    width = send_index.shape[2]
    c1 = coarse_neighbours.shape[2]
    n_slots = 2 * reach

    args = (
        right_side,
        absorption,
        vertical,
        horizontal,
        weights,
        jnp.swapaxes(neighbours, 0, 1),
        send_index,
        aggregate,
        jnp.swapaxes(coarse_neighbours, 0, 1),
        jnp.swapaxes(coarse_vertical, 2, 3),
        jnp.swapaxes(coarse_horizontal, 2, 3),
    )
    ext_rows = columns + n_slots * width
    coarse_rows = ext_rows
    scratch = [pltpu.VMEM(x.shape, x.dtype) for x in args] + [
        pltpu.VMEM(right_side.shape, F32),
        pltpu.SemaphoreType.DMA((len(args) + 1,)),
        pltpu.VMEM((neighbours.shape[1] * columns, 2 * columns), BF16),
        pltpu.VMEM((neighbours.shape[1] * columns, 2 * n_slots * width), BF16),
        pltpu.VMEM((2, n_slots * width, tracers * LANES), F32),
        pltpu.VMEM((n_slots * width, tracers * LANES), F32),
        pltpu.VMEM((2, coarse_rows, tracers * LANES), F32),
        pltpu.SemaphoreType.DMA((n_slots,)),
        pltpu.SemaphoreType.DMA((2, n_slots)),
        pltpu.SemaphoreType.DMA((n_slots,)),
        pltpu.SemaphoreType.DMA((2, n_slots)),
    ]
    return pl.pallas_call(
        functools.partial(vcycle_kernel, n_parts, n_grp, reach, width),
        out_shape=jax.ShapeDtypeStruct(right_side.shape, F32),
        in_specs=[pl.BlockSpec(memory_space=pl.ANY)] * len(args),
        out_specs=pl.BlockSpec(memory_space=pl.ANY),
        scratch_shapes=scratch,
        compiler_params=pltpu.CompilerParams(collective_id=0, has_side_effects=True),
    )(*args)


def solution(mesh):
    placed = (
        P(("dom", "grp"), None, None, None),
        P(("dom", "grp"), None, None),
        P(("dom", "grp"), None, None, None),
        P(("dom", "grp"), None, None, None),
        P(("dom", "grp"), None, None),
        P(("dom", "grp"), None, None),
        P(("dom", "grp"), None),
        P(("dom", "grp"), None, None),
        P(("dom", "grp"), None, None, None),
        P(("dom", "grp"), None, None, None),
        P(("dom", "grp"), None, None),
    )
    n_grp = mesh.shape["grp"]
    n_parts = mesh.shape["dom"] * n_grp
    return jax.shard_map(
        functools.partial(body, n_parts=n_parts, n_grp=n_grp),
        mesh=mesh,
        in_specs=placed,
        out_specs=P(("dom", "grp"), None, None, None),
        check_vma=False,
    )
```

```python
import functools

import jax
import jax.numpy as jnp
from jax import lax
from jax.experimental import pallas as pl
from jax.experimental.pallas import tpu as pltpu
from jax.sharding import PartitionSpec as P

CYCLES = 2
PRE = 2
POST = 2
CSWEEPS = 4

OMEGA = 0.8
HIGHEST = lax.Precision.HIGHEST
MESH = pl.DeviceIdType.MESH
LANES = 128
F32 = jnp.float32
BF16 = jnp.bfloat16


def mm(a, b):
    return jnp.dot(a, b, precision=HIGHEST, preferred_element_type=F32)


def select(onehot2, x):
    hi = x.astype(BF16)
    lo = (x - hi.astype(F32)).astype(BF16)
    return jnp.dot(onehot2, jnp.concatenate([hi, lo], 0), preferred_element_type=F32)


def doubled(onehot):
    return jnp.concatenate([onehot, onehot], 1)


def vcycle_kernel(
    n_parts,
    n_grp,
    reach,
    width,
    rhs_hbm,
    absorption_hbm,
    vertical_hbm,
    horizontal_hbm,
    weights_hbm,
    nb_hbm,
    si_hbm,
    agg_hbm,
    cnb_hbm,
    cvert_hbm,
    chor_hbm,
    out_hbm,
    rhs_v,
    absorption_v,
    vertical_v,
    horizontal_v,
    weights_v,
    nb_v,
    si_v,
    agg_v,
    cnb_v,
    cvert_v,
    chor_v,
    load_sem,
    mt_local,
    mt_ghost,
    ghost,
    sendbuf,
    cext,
    send_sem,
    recv_sem,
    csend_sem,
    crecv_sem,
):
    me = lax.axis_index("dom") * n_grp + lax.axis_index("grp")
    offsets = list(range(1, reach + 1)) + [-d for d in range(1, reach + 1)]
    n_slots = len(offsets)
    by_distance = sorted(range(n_slots), key=lambda s: (abs(offsets[s]) != 2, abs(offsets[s]) == reach, abs(offsets[s]), offsets[s] < 0))
    tracers, layers, columns = rhs_v.shape[1:]
    n_nb = nb_v.shape[0]
    c1 = cnb_v.shape[2]
    n_ch = chor_v.shape[1]
    halo = n_slots * width

    def valid(q):
        return jnp.logical_and(q >= 0, q < n_parts)

    def device(q):
        return (lax.div(q, n_grp), lax.rem(q, n_grp))

    loads = [
        pltpu.make_async_copy(src, dst, load_sem.at[i])
        for i, (src, dst) in enumerate(
            [
                (rhs_hbm, rhs_v),
                (absorption_hbm, absorption_v),
                (vertical_hbm, vertical_v),
                (horizontal_hbm, horizontal_v),
                (weights_hbm, weights_v),
                (nb_hbm, nb_v),
                (si_hbm, si_v),
                (agg_hbm, agg_v),
                (cnb_hbm, cnb_v),
                (cvert_hbm, cvert_v),
                (chor_hbm, chor_v),
            ]
        )
    ]
    for copy in loads:
        copy.start()

    ghost[...] = jnp.zeros_like(ghost)
    cext[...] = jnp.zeros_like(cext)

    barrier = pltpu.get_barrier_semaphore()
    for d in offsets:
        @pl.when(valid(me + d))
        def _():
            pl.semaphore_signal(barrier, 1, device_id=device(me + d), device_id_type=MESH)
    for copy in loads:
        copy.wait()

    lane = lax.broadcasted_iota(jnp.int32, (8, LANES), 1)
    probe = pltpu.roll(lane, 1, 1)
    expected = jnp.where(lane == 0, LANES - 1, lane - 1)
    forward = (probe == expected)[0:1, :]
    layer_lane = lax.broadcasted_iota(jnp.int32, (1, LANES), 1)
    live = layer_lane < layers

    def shifted(x):
        a = pltpu.roll(x, 1, 1)
        b = pltpu.roll(x, LANES - 1, 1)
        lower = jnp.where(forward, a, b)
        upper = jnp.where(forward, b, a)
        return lower, upper

    pad_rows = jnp.zeros((LANES - layers, columns), F32)

    def to_cols(slab):
        return jnp.transpose(jnp.concatenate([slab, pad_rows], 0))

    ab = absorption_v[0]
    vr0 = vertical_v[0, 0]
    vr1 = vertical_v[0, 1]
    diag_rows = ab + jnp.abs(vr0) + jnp.abs(vr1)
    hsum = jnp.abs(horizontal_v[0, 0])
    for n in range(1, horizontal_v.shape[1]):
        hsum = hsum + jnp.abs(horizontal_v[0, n])
    diag_rows = diag_rows + hsum
    diag = jnp.where(live, to_cols(diag_rows), 1.0)
    inv_diag = 1.0 / diag
    rhs = jnp.concatenate([to_cols(rhs_v[0, t]) for t in range(tracers)], 1)
    st_blocks = []
    for s in range(n_slots):
        block = (lax.broadcasted_iota(jnp.int32, (columns, width), 0) == si_v[0, s:s + 1, :]).astype(F32)
        st_blocks.append(jnp.transpose(block))
    st = doubled(jnp.concatenate(st_blocks, 0).astype(BF16))
    ctx = {}

    def fine_setup():
        ctx["v0"] = jnp.where(layer_lane == 0, 0.0, to_cols(vr0))
        ctx["v1"] = jnp.where(layer_lane == layers - 1, 0.0, to_cols(vr1))
        ctx["h"] = [to_cols(horizontal_v[0, n]) for n in range(horizontal_v.shape[1])]
        k_iota = lax.broadcasted_iota(jnp.int32, (columns + halo, columns), 0)
        for n in range(n_nb):
            chosen = jnp.transpose((k_iota == nb_v[n]).astype(F32)).astype(BF16)
            rows = pl.ds(n * columns, columns)
            mt_local[rows, :] = doubled(chosen[:, :columns])
            mt_ghost[rows, :] = doubled(chosen[:, columns:])

    def coarse_setup():
        ctx["w"] = to_cols(weights_v[0])
        ctx["at"] = (lax.broadcasted_iota(jnp.int32, (c1, columns), 0) == agg_v[...]).astype(F32)
        a_full = jnp.transpose((lax.broadcasted_iota(jnp.int32, (LANES, columns), 0) == agg_v[...]).astype(F32))
        ctx["a"] = doubled(a_full[:, :c1].astype(BF16))
        coarse_rows = cext.shape[1]
        mct_blocks = []
        for n in range(n_ch):
            block = (lax.broadcasted_iota(jnp.int32, (coarse_rows, c1), 0) == cnb_v[n]).astype(F32)
            mct_blocks.append(jnp.transpose(block))
        ctx["mct"] = doubled(jnp.concatenate(mct_blocks, 0).astype(BF16))
        widen = (
            lax.broadcasted_iota(jnp.int32, (layers, LANES), 0) == lax.broadcasted_iota(jnp.int32, (layers, LANES), 1)
        ).astype(F32)

        def coarse_cols(slab):
            return mm(slab, widen)

        cvr0 = cvert_v[0, 0]
        cvr1 = cvert_v[0, 1]
        cdiag_rows = 0.5 + jnp.abs(cvr0) + jnp.abs(cvr1)
        csum = jnp.abs(chor_v[0, 0])
        for n in range(1, n_ch):
            csum = csum + jnp.abs(chor_v[0, n])
        cdiag = jnp.where(live, coarse_cols(cdiag_rows + csum), 1.0)
        ctx["cdiag"] = cdiag
        ctx["inv_cdiag"] = 1.0 / cdiag
        ctx["cv0"] = jnp.where(layer_lane == 0, 0.0, coarse_cols(cvr0))
        ctx["cv1"] = jnp.where(layer_lane == layers - 1, 0.0, coarse_cols(cvr1))
        ctx["ch"] = [coarse_cols(chor_v[0, n]) for n in range(n_ch)]

    setup_hooks = [fine_setup, coarse_setup]

    def halves(x):
        return [x[:, t * LANES:(t + 1) * LANES] for t in range(x.shape[1] // LANES)]

    def fine_copy(slot, s):
        rows = pl.ds(s * width, width)
        return pltpu.make_async_remote_copy(
            src_ref=sendbuf.at[rows],
            dst_ref=ghost.at[slot, rows],
            send_sem=send_sem.at[s],
            recv_sem=recv_sem.at[slot, s],
            device_id=device(me + offsets[s]),
            device_id_type=MESH,
        )

    fine_round = [0]
    pending = {"fine": None, "coarse": None}

    def finish_sends(kind, copy_of):
        slot = pending[kind]
        if slot is None:
            return
        pending[kind] = None
        for s in range(n_slots):
            @pl.when(valid(me + offsets[s]))
            def _():
                copy_of(slot, s).wait_send()

    def fine_apply(field):
        slot = fine_round[0] % 2
        fine_round[0] += 1
        finish_sends("fine", fine_copy)
        sendbuf[...] = select(st, field)
        for s in by_distance:
            @pl.when(valid(me + offsets[s]))
            def _():
                fine_copy(slot, s).start()
        if setup_hooks:
            setup_hooks.pop(0)()
        v0, v1, h = ctx["v0"], ctx["v1"], ctx["h"]
        local = select(mt_local[...], field)
        bases = []
        for t, part in enumerate(halves(field)):
            lower, upper = shifted(part)
            total = diag * part + v0 * lower + v1 * upper
            for n in range(n_nb):
                total = total + h[n] * local[n * columns:(n + 1) * columns, t * LANES:(t + 1) * LANES]
            bases.append(total)
        pending["fine"] = slot
        for s in range(n_slots):
            @pl.when(valid(me - offsets[s]))
            def _():
                fine_copy(slot, s).wait_recv()
        gathered = select(mt_ghost[...], ghost[slot])
        totals = []
        for t, total in enumerate(bases):
            for n in range(n_nb):
                total = total + h[n] * gathered[n * columns:(n + 1) * columns, t * LANES:(t + 1) * LANES]
            totals.append(total)
        return jnp.concatenate(totals, 1)

    def coarse_copy(slot, k):
        d = offsets[k]
        return pltpu.make_async_remote_copy(
            src_ref=cext.at[slot, pl.ds(reach * c1, c1)],
            dst_ref=cext.at[slot, pl.ds((reach - d) * c1, c1)],
            send_sem=csend_sem.at[k],
            recv_sem=crecv_sem.at[slot, k],
            device_id=device(me + d),
            device_id_type=MESH,
        )

    coarse_round = [0]

    def coarse_apply(corr):
        slot = coarse_round[0] % 2
        coarse_round[0] += 1
        finish_sends("coarse", coarse_copy)
        cext[slot, pl.ds(reach * c1, c1), :] = corr
        cdiag, cv0, cv1, ch, mct = ctx["cdiag"], ctx["cv0"], ctx["cv1"], ctx["ch"], ctx["mct"]
        for k in by_distance:
            @pl.when(valid(me + offsets[k]))
            def _():
                coarse_copy(slot, k).start()
        bases = []
        for part in halves(corr):
            lower, upper = shifted(part)
            bases.append(cdiag * part + cv0 * lower + cv1 * upper)
        pending["coarse"] = slot
        for k in range(n_slots):
            @pl.when(valid(me - offsets[k]))
            def _():
                coarse_copy(slot, k).wait_recv()
        gathered = select(mct, cext[slot])
        totals = []
        for t, total in enumerate(bases):
            for n in range(n_ch):
                total = total + ch[n] * gathered[n * c1:(n + 1) * c1, t * LANES:(t + 1) * LANES]
            totals.append(total)
        return jnp.concatenate(totals, 1)

    peers = sum(valid(me + d).astype(jnp.int32) for d in offsets)
    pl.semaphore_wait(barrier, peers)

    def per_half(x, coeff, op):
        return jnp.concatenate([op(part, coeff) for part in halves(x)], 1)

    solution = per_half(OMEGA * rhs, inv_diag, lambda x, c: x * c)
    for cycle_index in range(CYCLES):
        for sweep_index in range(PRE):
            if cycle_index == 0 and sweep_index == 0:
                continue
            step = OMEGA * (rhs - fine_apply(solution))
            solution = solution + per_half(step, inv_diag, lambda x, c: x * c)
        residual = rhs - fine_apply(solution)
        weighted = per_half(residual, ctx["w"], lambda x, c: x * c)
        coarse_source = mm(ctx["at"], weighted)
        correction = per_half(OMEGA * coarse_source, ctx["inv_cdiag"], lambda x, c: x * c)
        for coarse_sweep_index in range(CSWEEPS - 1):
            step = OMEGA * (coarse_source - coarse_apply(correction))
            correction = correction + per_half(step, ctx["inv_cdiag"], lambda x, c: x * c)
        lifted = select(ctx["a"], correction)
        solution = solution + per_half(lifted, ctx["w"], lambda x, c: x * c)
        for sweep_index in range(POST):
            step = OMEGA * (rhs - fine_apply(solution))
            solution = solution + per_half(step, inv_diag, lambda x, c: x * c)
    finish_sends("fine", fine_copy)
    finish_sends("coarse", coarse_copy)
    out_hbm[...] = solution


def unpack_kernel(layers, cols_ref, out_ref):
    for t in range(out_ref.shape[1]):
        out_ref[0, t] = jnp.transpose(cols_ref[:, t * LANES:(t + 1) * LANES])[:layers]


def body(
    right_side,
    absorption,
    vertical,
    horizontal,
    neighbours,
    send_index,
    aggregate,
    weights,
    coarse_vertical,
    coarse_horizontal,
    coarse_neighbours,
    *,
    n_parts,
    n_grp,
):
    _, tracers, layers, columns = right_side.shape
    reach = send_index.shape[1] // 2
    width = send_index.shape[2]
    c1 = coarse_neighbours.shape[2]
    n_slots = 2 * reach

    args = (
        right_side,
        absorption,
        vertical,
        horizontal,
        weights,
        jnp.swapaxes(neighbours, 0, 1),
        send_index,
        aggregate,
        jnp.swapaxes(coarse_neighbours, 0, 1),
        jnp.swapaxes(coarse_vertical, 2, 3),
        jnp.swapaxes(coarse_horizontal, 2, 3),
    )
    ext_rows = columns + n_slots * width
    coarse_rows = ext_rows
    scratch = [pltpu.VMEM(x.shape, x.dtype) for x in args] + [
        pltpu.SemaphoreType.DMA((len(args),)),
        pltpu.VMEM((neighbours.shape[1] * columns, 2 * columns), BF16),
        pltpu.VMEM((neighbours.shape[1] * columns, 2 * n_slots * width), BF16),
        pltpu.VMEM((2, n_slots * width, tracers * LANES), F32),
        pltpu.VMEM((n_slots * width, tracers * LANES), F32),
        pltpu.VMEM((2, coarse_rows, tracers * LANES), F32),
        pltpu.SemaphoreType.DMA((n_slots,)),
        pltpu.SemaphoreType.DMA((2, n_slots)),
        pltpu.SemaphoreType.DMA((n_slots,)),
        pltpu.SemaphoreType.DMA((2, n_slots)),
    ]
    cols = pl.pallas_call(
        functools.partial(vcycle_kernel, n_parts, n_grp, reach, width),
        out_shape=jax.ShapeDtypeStruct((columns, tracers * LANES), F32),
        in_specs=[pl.BlockSpec(memory_space=pl.ANY)] * len(args),
        out_specs=pl.BlockSpec(memory_space=pltpu.VMEM),
        scratch_shapes=scratch,
        compiler_params=pltpu.CompilerParams(collective_id=0, has_side_effects=True),
    )(*args)
    return pl.pallas_call(
        functools.partial(unpack_kernel, layers),
        out_shape=jax.ShapeDtypeStruct(right_side.shape, F32),
        in_specs=[pl.BlockSpec(memory_space=pltpu.VMEM)],
        out_specs=pl.BlockSpec(memory_space=pltpu.VMEM),
    )(cols)


def solution(mesh):
    placed = (
        P(("dom", "grp"), None, None, None),
        P(("dom", "grp"), None, None),
        P(("dom", "grp"), None, None, None),
        P(("dom", "grp"), None, None, None),
        P(("dom", "grp"), None, None),
        P(("dom", "grp"), None, None),
        P(("dom", "grp"), None),
        P(("dom", "grp"), None, None),
        P(("dom", "grp"), None, None, None),
        P(("dom", "grp"), None, None, None),
        P(("dom", "grp"), None, None),
    )
    n_grp = mesh.shape["grp"]
    n_parts = mesh.shape["dom"] * n_grp
    return jax.shard_map(
        functools.partial(body, n_parts=n_parts, n_grp=n_grp),
        mesh=mesh,
        in_specs=placed,
        out_specs=P(("dom", "grp"), None, None, None),
        check_vma=False,
    )
```

```python
import functools

import jax
import jax.numpy as jnp
from jax import lax
from jax.experimental import pallas as pl
from jax.experimental.pallas import tpu as pltpu
from jax.sharding import PartitionSpec as P

CYCLES = 2
PRE = 2
POST = 2
CSWEEPS = 4

OMEGA = 0.8
HIGHEST = lax.Precision.HIGHEST
MESH = pl.DeviceIdType.MESH
LANES = 128
F32 = jnp.float32
BF16 = jnp.bfloat16


def mm(a, b):
    return jnp.dot(a, b, precision=HIGHEST, preferred_element_type=F32)


def select(onehot2, x):
    hi = x.astype(BF16)
    lo = (x - hi.astype(F32)).astype(BF16)
    return jnp.dot(onehot2, jnp.concatenate([hi, lo], 0), preferred_element_type=F32)


def doubled(onehot):
    return jnp.concatenate([onehot, onehot], 1)


def vcycle_kernel(
    n_parts,
    n_grp,
    reach,
    width,
    rhs_hbm,
    absorption_hbm,
    vertical_hbm,
    horizontal_hbm,
    weights_hbm,
    nb_hbm,
    si_hbm,
    agg_hbm,
    cnb_hbm,
    cvert_hbm,
    chor_hbm,
    out_hbm,
    rhs_v,
    absorption_v,
    vertical_v,
    horizontal_v,
    weights_v,
    nb_v,
    si_v,
    agg_v,
    cnb_v,
    cvert_v,
    chor_v,
    out_v,
    load_sem,
    mt_local,
    mt_ghost,
    ghost,
    sendbuf,
    cext,
    send_sem,
    recv_sem,
    csend_sem,
    crecv_sem,
):
    me = lax.axis_index("dom") * n_grp + lax.axis_index("grp")
    offsets = list(range(1, reach + 1)) + [-d for d in range(1, reach + 1)]
    n_slots = len(offsets)
    by_distance = sorted(range(n_slots), key=lambda s: (abs(offsets[s]) != 2, abs(offsets[s]) == reach, abs(offsets[s]), offsets[s] < 0))
    tracers, layers, columns = rhs_v.shape[1:]
    n_nb = nb_v.shape[0]
    c1 = cnb_v.shape[2]
    n_ch = chor_v.shape[1]
    halo = n_slots * width

    def valid(q):
        return jnp.logical_and(q >= 0, q < n_parts)

    def device(q):
        return (lax.div(q, n_grp), lax.rem(q, n_grp))

    loads = [
        pltpu.make_async_copy(src, dst, load_sem.at[i])
        for i, (src, dst) in enumerate(
            [
                (rhs_hbm, rhs_v),
                (absorption_hbm, absorption_v),
                (vertical_hbm, vertical_v),
                (horizontal_hbm, horizontal_v),
                (weights_hbm, weights_v),
                (nb_hbm, nb_v),
                (si_hbm, si_v),
                (agg_hbm, agg_v),
                (cnb_hbm, cnb_v),
                (cvert_hbm, cvert_v),
                (chor_hbm, chor_v),
            ]
        )
    ]
    for copy in loads:
        copy.start()

    ghost[...] = jnp.zeros_like(ghost)
    cext[...] = jnp.zeros_like(cext)

    barrier = pltpu.get_barrier_semaphore()
    for d in offsets:
        @pl.when(valid(me + d))
        def _():
            pl.semaphore_signal(barrier, 1, device_id=device(me + d), device_id_type=MESH)
    for copy in loads:
        copy.wait()

    lane = lax.broadcasted_iota(jnp.int32, (8, LANES), 1)
    probe = pltpu.roll(lane, 1, 1)
    expected = jnp.where(lane == 0, LANES - 1, lane - 1)
    forward = (probe == expected)[0:1, :]
    layer_lane = lax.broadcasted_iota(jnp.int32, (1, LANES), 1)
    live = layer_lane < layers

    def shifted(x):
        a = pltpu.roll(x, 1, 1)
        b = pltpu.roll(x, LANES - 1, 1)
        lower = jnp.where(forward, a, b)
        upper = jnp.where(forward, b, a)
        return lower, upper

    pad_rows = jnp.zeros((LANES - layers, columns), F32)

    def to_cols(slab):
        return jnp.transpose(jnp.concatenate([slab, pad_rows], 0))

    ab = absorption_v[0]
    vr0 = vertical_v[0, 0]
    vr1 = vertical_v[0, 1]
    diag_rows = ab + jnp.abs(vr0) + jnp.abs(vr1)
    hsum = jnp.abs(horizontal_v[0, 0])
    for n in range(1, horizontal_v.shape[1]):
        hsum = hsum + jnp.abs(horizontal_v[0, n])
    diag_rows = diag_rows + hsum
    diag = jnp.where(live, to_cols(diag_rows), 1.0)
    inv_diag = 1.0 / diag
    rhs = jnp.concatenate([to_cols(rhs_v[0, t]) for t in range(tracers)], 1)
    st_blocks = []
    for s in range(n_slots):
        block = (lax.broadcasted_iota(jnp.int32, (columns, width), 0) == si_v[0, s:s + 1, :]).astype(F32)
        st_blocks.append(jnp.transpose(block))
    st = doubled(jnp.concatenate(st_blocks, 0).astype(BF16))
    ctx = {}

    def fine_setup():
        ctx["v0"] = jnp.where(layer_lane == 0, 0.0, to_cols(vr0))
        ctx["v1"] = jnp.where(layer_lane == layers - 1, 0.0, to_cols(vr1))
        ctx["h"] = [to_cols(horizontal_v[0, n]) for n in range(horizontal_v.shape[1])]
        k_iota = lax.broadcasted_iota(jnp.int32, (columns + halo, columns), 0)
        for n in range(n_nb):
            chosen = jnp.transpose((k_iota == nb_v[n]).astype(F32)).astype(BF16)
            rows = pl.ds(n * columns, columns)
            mt_local[rows, :] = doubled(chosen[:, :columns])
            mt_ghost[rows, :] = doubled(chosen[:, columns:])

    def coarse_setup():
        ctx["w"] = to_cols(weights_v[0])
        ctx["at"] = (lax.broadcasted_iota(jnp.int32, (c1, columns), 0) == agg_v[...]).astype(F32)
        a_full = jnp.transpose((lax.broadcasted_iota(jnp.int32, (LANES, columns), 0) == agg_v[...]).astype(F32))
        ctx["a"] = doubled(a_full[:, :c1].astype(BF16))
        coarse_rows = cext.shape[1]
        mct_blocks = []
        for n in range(n_ch):
            block = (lax.broadcasted_iota(jnp.int32, (coarse_rows, c1), 0) == cnb_v[n]).astype(F32)
            mct_blocks.append(jnp.transpose(block))
        ctx["mct"] = doubled(jnp.concatenate(mct_blocks, 0).astype(BF16))
        widen = (
            lax.broadcasted_iota(jnp.int32, (layers, LANES), 0) == lax.broadcasted_iota(jnp.int32, (layers, LANES), 1)
        ).astype(F32)

        def coarse_cols(slab):
            return mm(slab, widen)

        cvr0 = cvert_v[0, 0]
        cvr1 = cvert_v[0, 1]
        cdiag_rows = 0.5 + jnp.abs(cvr0) + jnp.abs(cvr1)
        csum = jnp.abs(chor_v[0, 0])
        for n in range(1, n_ch):
            csum = csum + jnp.abs(chor_v[0, n])
        cdiag = jnp.where(live, coarse_cols(cdiag_rows + csum), 1.0)
        ctx["cdiag"] = cdiag
        ctx["inv_cdiag"] = 1.0 / cdiag
        ctx["cv0"] = jnp.where(layer_lane == 0, 0.0, coarse_cols(cvr0))
        ctx["cv1"] = jnp.where(layer_lane == layers - 1, 0.0, coarse_cols(cvr1))
        ctx["ch"] = [coarse_cols(chor_v[0, n]) for n in range(n_ch)]

    setup_hooks = [fine_setup, coarse_setup]

    def halves(x):
        return [x[:, t * LANES:(t + 1) * LANES] for t in range(x.shape[1] // LANES)]

    def fine_copy(slot, s):
        rows = pl.ds(s * width, width)
        return pltpu.make_async_remote_copy(
            src_ref=sendbuf.at[rows],
            dst_ref=ghost.at[slot, rows],
            send_sem=send_sem.at[s],
            recv_sem=recv_sem.at[slot, s],
            device_id=device(me + offsets[s]),
            device_id_type=MESH,
        )

    fine_round = [0]
    pending = {"fine": None, "coarse": None}

    def finish_sends(kind, copy_of):
        slot = pending[kind]
        if slot is None:
            return
        pending[kind] = None
        for s in range(n_slots):
            @pl.when(valid(me + offsets[s]))
            def _():
                copy_of(slot, s).wait_send()

    def fine_apply(field):
        slot = fine_round[0] % 2
        fine_round[0] += 1
        finish_sends("fine", fine_copy)
        sendbuf[...] = select(st, field)
        for s in by_distance:
            @pl.when(valid(me + offsets[s]))
            def _():
                fine_copy(slot, s).start()
        if setup_hooks:
            setup_hooks.pop(0)()
        v0, v1, h = ctx["v0"], ctx["v1"], ctx["h"]
        local = select(mt_local[...], field)
        bases = []
        for t, part in enumerate(halves(field)):
            lower, upper = shifted(part)
            total = diag * part + v0 * lower + v1 * upper
            for n in range(n_nb):
                total = total + h[n] * local[n * columns:(n + 1) * columns, t * LANES:(t + 1) * LANES]
            bases.append(total)
        pending["fine"] = slot
        for s in range(n_slots):
            @pl.when(valid(me - offsets[s]))
            def _():
                fine_copy(slot, s).wait_recv()
        received = ghost[slot]
        hi = received.astype(BF16)
        stacked = jnp.concatenate([hi, (received - hi.astype(F32)).astype(BF16)], 0)
        totals = list(bases)
        for n in range(n_nb):
            branch = jnp.dot(mt_ghost[pl.ds(n * columns, columns), :], stacked, preferred_element_type=F32)
            for t in range(len(totals)):
                totals[t] = totals[t] + h[n] * branch[:, t * LANES:(t + 1) * LANES]
        return jnp.concatenate(totals, 1)

    def coarse_copy(slot, k):
        d = offsets[k]
        return pltpu.make_async_remote_copy(
            src_ref=cext.at[slot, pl.ds(reach * c1, c1)],
            dst_ref=cext.at[slot, pl.ds((reach - d) * c1, c1)],
            send_sem=csend_sem.at[k],
            recv_sem=crecv_sem.at[slot, k],
            device_id=device(me + d),
            device_id_type=MESH,
        )

    coarse_round = [0]

    def coarse_apply(corr):
        slot = coarse_round[0] % 2
        coarse_round[0] += 1
        finish_sends("coarse", coarse_copy)
        cext[slot, pl.ds(reach * c1, c1), :] = corr
        cdiag, cv0, cv1, ch, mct = ctx["cdiag"], ctx["cv0"], ctx["cv1"], ctx["ch"], ctx["mct"]
        for k in by_distance:
            @pl.when(valid(me + offsets[k]))
            def _():
                coarse_copy(slot, k).start()
        bases = []
        for part in halves(corr):
            lower, upper = shifted(part)
            bases.append(cdiag * part + cv0 * lower + cv1 * upper)
        pending["coarse"] = slot
        for k in range(n_slots):
            @pl.when(valid(me - offsets[k]))
            def _():
                coarse_copy(slot, k).wait_recv()
        gathered = select(mct, cext[slot])
        totals = []
        for t, total in enumerate(bases):
            for n in range(n_ch):
                total = total + ch[n] * gathered[n * c1:(n + 1) * c1, t * LANES:(t + 1) * LANES]
            totals.append(total)
        return jnp.concatenate(totals, 1)

    peers = sum(valid(me + d).astype(jnp.int32) for d in offsets)
    pl.semaphore_wait(barrier, peers)

    def per_half(x, coeff, op):
        return jnp.concatenate([op(part, coeff) for part in halves(x)], 1)

    solution = per_half(OMEGA * rhs, inv_diag, lambda x, c: x * c)
    for cycle_index in range(CYCLES):
        for sweep_index in range(PRE):
            if cycle_index == 0 and sweep_index == 0:
                continue
            step = OMEGA * (rhs - fine_apply(solution))
            solution = solution + per_half(step, inv_diag, lambda x, c: x * c)
        residual = rhs - fine_apply(solution)
        weighted = per_half(residual, ctx["w"], lambda x, c: x * c)
        coarse_source = mm(ctx["at"], weighted)
        correction = per_half(OMEGA * coarse_source, ctx["inv_cdiag"], lambda x, c: x * c)
        for coarse_sweep_index in range(CSWEEPS - 1):
            step = OMEGA * (coarse_source - coarse_apply(correction))
            correction = correction + per_half(step, ctx["inv_cdiag"], lambda x, c: x * c)
        lifted = select(ctx["a"], correction)
        solution = solution + per_half(lifted, ctx["w"], lambda x, c: x * c)
        for sweep_index in range(POST):
            step = OMEGA * (rhs - fine_apply(solution))
            solution = solution + per_half(step, inv_diag, lambda x, c: x * c)
    finish_sends("fine", fine_copy)
    finish_sends("coarse", coarse_copy)
    for t, part in enumerate(halves(solution)):
        out_v[0, t] = jnp.transpose(part)[:layers]
    store = pltpu.make_async_copy(out_v, out_hbm, load_sem.at[len(loads)])
    store.start()
    store.wait()


def body(
    right_side,
    absorption,
    vertical,
    horizontal,
    neighbours,
    send_index,
    aggregate,
    weights,
    coarse_vertical,
    coarse_horizontal,
    coarse_neighbours,
    *,
    n_parts,
    n_grp,
):
    _, tracers, layers, columns = right_side.shape
    reach = send_index.shape[1] // 2
    width = send_index.shape[2]
    c1 = coarse_neighbours.shape[2]
    n_slots = 2 * reach

    args = (
        right_side,
        absorption,
        vertical,
        horizontal,
        weights,
        jnp.swapaxes(neighbours, 0, 1),
        send_index,
        aggregate,
        jnp.swapaxes(coarse_neighbours, 0, 1),
        jnp.swapaxes(coarse_vertical, 2, 3),
        jnp.swapaxes(coarse_horizontal, 2, 3),
    )
    ext_rows = columns + n_slots * width
    coarse_rows = ext_rows
    scratch = [pltpu.VMEM(x.shape, x.dtype) for x in args] + [
        pltpu.VMEM(right_side.shape, F32),
        pltpu.SemaphoreType.DMA((len(args) + 1,)),
        pltpu.VMEM((neighbours.shape[1] * columns, 2 * columns), BF16),
        pltpu.VMEM((neighbours.shape[1] * columns, 2 * n_slots * width), BF16),
        pltpu.VMEM((2, n_slots * width, tracers * LANES), F32),
        pltpu.VMEM((n_slots * width, tracers * LANES), F32),
        pltpu.VMEM((2, coarse_rows, tracers * LANES), F32),
        pltpu.SemaphoreType.DMA((n_slots,)),
        pltpu.SemaphoreType.DMA((2, n_slots)),
        pltpu.SemaphoreType.DMA((n_slots,)),
        pltpu.SemaphoreType.DMA((2, n_slots)),
    ]
    return pl.pallas_call(
        functools.partial(vcycle_kernel, n_parts, n_grp, reach, width),
        out_shape=jax.ShapeDtypeStruct(right_side.shape, F32),
        in_specs=[pl.BlockSpec(memory_space=pl.ANY)] * len(args),
        out_specs=pl.BlockSpec(memory_space=pl.ANY),
        scratch_shapes=scratch,
        compiler_params=pltpu.CompilerParams(collective_id=0, has_side_effects=True),
    )(*args)


def solution(mesh):
    placed = (
        P(("dom", "grp"), None, None, None),
        P(("dom", "grp"), None, None),
        P(("dom", "grp"), None, None, None),
        P(("dom", "grp"), None, None, None),
        P(("dom", "grp"), None, None),
        P(("dom", "grp"), None, None),
        P(("dom", "grp"), None),
        P(("dom", "grp"), None, None),
        P(("dom", "grp"), None, None, None),
        P(("dom", "grp"), None, None, None),
        P(("dom", "grp"), None, None),
    )
    n_grp = mesh.shape["grp"]
    n_parts = mesh.shape["dom"] * n_grp
    return jax.shard_map(
        functools.partial(body, n_parts=n_parts, n_grp=n_grp),
        mesh=mesh,
        in_specs=placed,
        out_specs=P(("dom", "grp"), None, None, None),
        check_vma=False,
    )
```

```python
import functools

import jax
import jax.numpy as jnp
from jax import lax
from jax.experimental import pallas as pl
from jax.experimental.pallas import tpu as pltpu
from jax.sharding import PartitionSpec as P

CYCLES = 2
PRE = 2
POST = 2
CSWEEPS = 4

OMEGA = 0.8
HIGHEST = lax.Precision.HIGHEST
MESH = pl.DeviceIdType.MESH
LANES = 128
F32 = jnp.float32
BF16 = jnp.bfloat16


def mm(a, b):
    return jnp.dot(a, b, precision=HIGHEST, preferred_element_type=F32)


def select(onehot2, x):
    hi = x.astype(BF16)
    lo = (x - hi.astype(F32)).astype(BF16)
    return jnp.dot(onehot2, jnp.concatenate([hi, lo], 0), preferred_element_type=F32)


def doubled(onehot):
    return jnp.concatenate([onehot, onehot], 1)


def vcycle_kernel(
    n_parts,
    n_grp,
    reach,
    width,
    rhs_hbm,
    absorption_hbm,
    vertical_hbm,
    horizontal_hbm,
    weights_hbm,
    nb_hbm,
    si_hbm,
    agg_hbm,
    cnb_hbm,
    cvert_hbm,
    chor_hbm,
    out_hbm,
    rhs_v,
    absorption_v,
    vertical_v,
    horizontal_v,
    weights_v,
    nb_v,
    si_v,
    agg_v,
    cnb_v,
    cvert_v,
    chor_v,
    out_v,
    load_sem,
    mt_local,
    mt_ghost,
    ghost,
    sendbuf,
    cext,
    send_sem,
    recv_sem,
    csend_sem,
    crecv_sem,
):
    me = lax.axis_index("dom") * n_grp + lax.axis_index("grp")
    offsets = list(range(1, reach + 1)) + [-d for d in range(1, reach + 1)]
    n_slots = len(offsets)
    by_distance = sorted(range(n_slots), key=lambda s: (abs(offsets[s]) != 2, abs(offsets[s]) == reach, abs(offsets[s]), offsets[s] < 0))
    tracers, layers, columns = rhs_v.shape[1:]
    n_nb = nb_v.shape[0]
    c1 = cnb_v.shape[2]
    n_ch = chor_v.shape[1]
    halo = n_slots * width

    def valid(q):
        return jnp.logical_and(q >= 0, q < n_parts)

    def device(q):
        return (lax.div(q, n_grp), lax.rem(q, n_grp))

    loads = [
        pltpu.make_async_copy(src, dst, load_sem.at[i])
        for i, (src, dst) in enumerate(
            [
                (rhs_hbm, rhs_v),
                (absorption_hbm, absorption_v),
                (vertical_hbm, vertical_v),
                (horizontal_hbm, horizontal_v),
                (weights_hbm, weights_v),
                (nb_hbm, nb_v),
                (si_hbm, si_v),
                (agg_hbm, agg_v),
                (cnb_hbm, cnb_v),
                (cvert_hbm, cvert_v),
                (chor_hbm, chor_v),
            ]
        )
    ]
    for copy in loads:
        copy.start()

    ghost[...] = jnp.zeros_like(ghost)
    cext[...] = jnp.zeros_like(cext)

    barrier = pltpu.get_barrier_semaphore()
    for d in offsets:
        @pl.when(valid(me + d))
        def _():
            pl.semaphore_signal(barrier, 1, device_id=device(me + d), device_id_type=MESH)
    for copy in loads:
        copy.wait()

    lane = lax.broadcasted_iota(jnp.int32, (8, LANES), 1)
    probe = pltpu.roll(lane, 1, 1)
    expected = jnp.where(lane == 0, LANES - 1, lane - 1)
    forward = (probe == expected)[0:1, :]
    layer_lane = lax.broadcasted_iota(jnp.int32, (1, LANES), 1)
    live = layer_lane < layers

    def shifted(x):
        a = pltpu.roll(x, 1, 1)
        b = pltpu.roll(x, LANES - 1, 1)
        lower = jnp.where(forward, a, b)
        upper = jnp.where(forward, b, a)
        return lower, upper

    pad_rows = jnp.zeros((LANES - layers, columns), F32)

    def to_cols(slab):
        return jnp.transpose(jnp.concatenate([slab, pad_rows], 0))

    ab = absorption_v[0]
    vr0 = vertical_v[0, 0]
    vr1 = vertical_v[0, 1]
    diag_rows = ab + jnp.abs(vr0) + jnp.abs(vr1)
    hsum = jnp.abs(horizontal_v[0, 0])
    for n in range(1, horizontal_v.shape[1]):
        hsum = hsum + jnp.abs(horizontal_v[0, n])
    diag_rows = diag_rows + hsum
    diag = jnp.where(live, to_cols(diag_rows), 1.0)
    inv_diag = 1.0 / diag
    rhs = jnp.concatenate([to_cols(rhs_v[0, t]) for t in range(tracers)], 1)
    st_blocks = []
    for s in range(n_slots):
        block = (lax.broadcasted_iota(jnp.int32, (columns, width), 0) == si_v[0, s:s + 1, :]).astype(F32)
        st_blocks.append(jnp.transpose(block))
    st = doubled(jnp.concatenate(st_blocks, 0).astype(BF16))
    ctx = {}

    def fine_setup():
        ctx["v0"] = jnp.where(layer_lane == 0, 0.0, to_cols(vr0))
        ctx["v1"] = jnp.where(layer_lane == layers - 1, 0.0, to_cols(vr1))
        ctx["h"] = [to_cols(horizontal_v[0, n]) for n in range(horizontal_v.shape[1])]
        k_iota = lax.broadcasted_iota(jnp.int32, (columns + halo, columns), 0)
        for n in range(n_nb):
            chosen = jnp.transpose((k_iota == nb_v[n]).astype(F32)).astype(BF16)
            rows = pl.ds(n * columns, columns)
            mt_local[rows, :] = doubled(chosen[:, :columns])
            mt_ghost[rows, :] = doubled(chosen[:, columns:])

    def coarse_setup():
        ctx["w"] = to_cols(weights_v[0])
        ctx["at"] = (lax.broadcasted_iota(jnp.int32, (c1, columns), 0) == agg_v[...]).astype(F32)
        a_full = jnp.transpose((lax.broadcasted_iota(jnp.int32, (LANES, columns), 0) == agg_v[...]).astype(F32))
        ctx["a"] = doubled(a_full[:, :c1].astype(BF16))
        coarse_rows = cext.shape[1]
        mct_blocks = []
        for n in range(n_ch):
            block = (lax.broadcasted_iota(jnp.int32, (coarse_rows, c1), 0) == cnb_v[n]).astype(F32)
            mct_blocks.append(jnp.transpose(block))
        ctx["mct"] = doubled(jnp.concatenate(mct_blocks, 0).astype(BF16))
        widen = (
            lax.broadcasted_iota(jnp.int32, (layers, LANES), 0) == lax.broadcasted_iota(jnp.int32, (layers, LANES), 1)
        ).astype(F32)

        def coarse_cols(slab):
            return mm(slab, widen)

        cvr0 = cvert_v[0, 0]
        cvr1 = cvert_v[0, 1]
        cdiag_rows = 0.5 + jnp.abs(cvr0) + jnp.abs(cvr1)
        csum = jnp.abs(chor_v[0, 0])
        for n in range(1, n_ch):
            csum = csum + jnp.abs(chor_v[0, n])
        cdiag = jnp.where(live, coarse_cols(cdiag_rows + csum), 1.0)
        ctx["cdiag"] = cdiag
        ctx["inv_cdiag"] = 1.0 / cdiag
        ctx["cv0"] = jnp.where(layer_lane == 0, 0.0, coarse_cols(cvr0))
        ctx["cv1"] = jnp.where(layer_lane == layers - 1, 0.0, coarse_cols(cvr1))
        ctx["ch"] = [coarse_cols(chor_v[0, n]) for n in range(n_ch)]

    setup_hooks = [fine_setup, coarse_setup]

    def halves(x):
        return [x[:, t * LANES:(t + 1) * LANES] for t in range(x.shape[1] // LANES)]

    def fine_copy(slot, s):
        rows = pl.ds(s * width, width)
        return pltpu.make_async_remote_copy(
            src_ref=sendbuf.at[slot, rows],
            dst_ref=ghost.at[slot, rows],
            send_sem=send_sem.at[slot, s],
            recv_sem=recv_sem.at[slot, s],
            device_id=device(me + offsets[s]),
            device_id_type=MESH,
        )

    fine_round = [0]
    pending = {("fine", 0): False, ("fine", 1): False, ("coarse", 0): False, ("coarse", 1): False}

    def finish_sends(kind, copy_of, slot):
        if not pending[(kind, slot)]:
            return
        pending[(kind, slot)] = False
        for s in range(n_slots):
            @pl.when(valid(me + offsets[s]))
            def _():
                copy_of(slot, s).wait_send()

    def fine_apply(field):
        slot = fine_round[0] % 2
        fine_round[0] += 1
        finish_sends("fine", fine_copy, slot)
        sendbuf[slot] = select(st, field)
        for s in by_distance:
            @pl.when(valid(me + offsets[s]))
            def _():
                fine_copy(slot, s).start()
        if setup_hooks:
            setup_hooks.pop(0)()
        v0, v1, h = ctx["v0"], ctx["v1"], ctx["h"]
        local = select(mt_local[...], field)
        bases = []
        for t, part in enumerate(halves(field)):
            lower, upper = shifted(part)
            total = diag * part + v0 * lower + v1 * upper
            for n in range(n_nb):
                total = total + h[n] * local[n * columns:(n + 1) * columns, t * LANES:(t + 1) * LANES]
            bases.append(total)
        pending[("fine", slot)] = True
        for s in range(n_slots):
            @pl.when(valid(me - offsets[s]))
            def _():
                fine_copy(slot, s).wait_recv()
        gathered = select(mt_ghost[...], ghost[slot])
        totals = []
        for t, total in enumerate(bases):
            for n in range(n_nb):
                total = total + h[n] * gathered[n * columns:(n + 1) * columns, t * LANES:(t + 1) * LANES]
            totals.append(total)
        return jnp.concatenate(totals, 1)

    def coarse_copy(slot, k):
        d = offsets[k]
        return pltpu.make_async_remote_copy(
            src_ref=cext.at[slot, pl.ds(reach * c1, c1)],
            dst_ref=cext.at[slot, pl.ds((reach - d) * c1, c1)],
            send_sem=csend_sem.at[slot, k],
            recv_sem=crecv_sem.at[slot, k],
            device_id=device(me + d),
            device_id_type=MESH,
        )

    coarse_round = [0]

    def coarse_apply(corr):
        slot = coarse_round[0] % 2
        coarse_round[0] += 1
        finish_sends("coarse", coarse_copy, slot)
        cext[slot, pl.ds(reach * c1, c1), :] = corr
        cdiag, cv0, cv1, ch, mct = ctx["cdiag"], ctx["cv0"], ctx["cv1"], ctx["ch"], ctx["mct"]
        for k in by_distance:
            @pl.when(valid(me + offsets[k]))
            def _():
                coarse_copy(slot, k).start()
        bases = []
        for part in halves(corr):
            lower, upper = shifted(part)
            bases.append(cdiag * part + cv0 * lower + cv1 * upper)
        pending[("coarse", slot)] = True
        for k in range(n_slots):
            @pl.when(valid(me - offsets[k]))
            def _():
                coarse_copy(slot, k).wait_recv()
        gathered = select(mct, cext[slot])
        totals = []
        for t, total in enumerate(bases):
            for n in range(n_ch):
                total = total + ch[n] * gathered[n * c1:(n + 1) * c1, t * LANES:(t + 1) * LANES]
            totals.append(total)
        return jnp.concatenate(totals, 1)

    peers = sum(valid(me + d).astype(jnp.int32) for d in offsets)
    pl.semaphore_wait(barrier, peers)

    def per_half(x, coeff, op):
        return jnp.concatenate([op(part, coeff) for part in halves(x)], 1)

    solution = per_half(OMEGA * rhs, inv_diag, lambda x, c: x * c)
    for cycle_index in range(CYCLES):
        for sweep_index in range(PRE):
            if cycle_index == 0 and sweep_index == 0:
                continue
            step = OMEGA * (rhs - fine_apply(solution))
            solution = solution + per_half(step, inv_diag, lambda x, c: x * c)
        residual = rhs - fine_apply(solution)
        weighted = per_half(residual, ctx["w"], lambda x, c: x * c)
        coarse_source = mm(ctx["at"], weighted)
        correction = per_half(OMEGA * coarse_source, ctx["inv_cdiag"], lambda x, c: x * c)
        for coarse_sweep_index in range(CSWEEPS - 1):
            step = OMEGA * (coarse_source - coarse_apply(correction))
            correction = correction + per_half(step, ctx["inv_cdiag"], lambda x, c: x * c)
        lifted = select(ctx["a"], correction)
        solution = solution + per_half(lifted, ctx["w"], lambda x, c: x * c)
        for sweep_index in range(POST):
            step = OMEGA * (rhs - fine_apply(solution))
            solution = solution + per_half(step, inv_diag, lambda x, c: x * c)
    for slot in range(2):
        finish_sends("fine", fine_copy, slot)
        finish_sends("coarse", coarse_copy, slot)
    for t, part in enumerate(halves(solution)):
        out_v[0, t] = jnp.transpose(part)[:layers]
    store = pltpu.make_async_copy(out_v, out_hbm, load_sem.at[len(loads)])
    store.start()
    store.wait()


def body(
    right_side,
    absorption,
    vertical,
    horizontal,
    neighbours,
    send_index,
    aggregate,
    weights,
    coarse_vertical,
    coarse_horizontal,
    coarse_neighbours,
    *,
    n_parts,
    n_grp,
):
    _, tracers, layers, columns = right_side.shape
    reach = send_index.shape[1] // 2
    width = send_index.shape[2]
    c1 = coarse_neighbours.shape[2]
    n_slots = 2 * reach

    args = (
        right_side,
        absorption,
        vertical,
        horizontal,
        weights,
        jnp.swapaxes(neighbours, 0, 1),
        send_index,
        aggregate,
        jnp.swapaxes(coarse_neighbours, 0, 1),
        jnp.swapaxes(coarse_vertical, 2, 3),
        jnp.swapaxes(coarse_horizontal, 2, 3),
    )
    ext_rows = columns + n_slots * width
    coarse_rows = ext_rows
    scratch = [pltpu.VMEM(x.shape, x.dtype) for x in args] + [
        pltpu.VMEM(right_side.shape, F32),
        pltpu.SemaphoreType.DMA((len(args) + 1,)),
        pltpu.VMEM((neighbours.shape[1] * columns, 2 * columns), BF16),
        pltpu.VMEM((neighbours.shape[1] * columns, 2 * n_slots * width), BF16),
        pltpu.VMEM((2, n_slots * width, tracers * LANES), F32),
        pltpu.VMEM((2, n_slots * width, tracers * LANES), F32),
        pltpu.VMEM((2, coarse_rows, tracers * LANES), F32),
        pltpu.SemaphoreType.DMA((2, n_slots)),
        pltpu.SemaphoreType.DMA((2, n_slots)),
        pltpu.SemaphoreType.DMA((2, n_slots)),
        pltpu.SemaphoreType.DMA((2, n_slots)),
    ]
    return pl.pallas_call(
        functools.partial(vcycle_kernel, n_parts, n_grp, reach, width),
        out_shape=jax.ShapeDtypeStruct(right_side.shape, F32),
        in_specs=[pl.BlockSpec(memory_space=pl.ANY)] * len(args),
        out_specs=pl.BlockSpec(memory_space=pl.ANY),
        scratch_shapes=scratch,
        compiler_params=pltpu.CompilerParams(collective_id=0, has_side_effects=True),
    )(*args)


def solution(mesh):
    placed = (
        P(("dom", "grp"), None, None, None),
        P(("dom", "grp"), None, None),
        P(("dom", "grp"), None, None, None),
        P(("dom", "grp"), None, None, None),
        P(("dom", "grp"), None, None),
        P(("dom", "grp"), None, None),
        P(("dom", "grp"), None),
        P(("dom", "grp"), None, None),
        P(("dom", "grp"), None, None, None),
        P(("dom", "grp"), None, None, None),
        P(("dom", "grp"), None, None),
    )
    n_grp = mesh.shape["grp"]
    n_parts = mesh.shape["dom"] * n_grp
    return jax.shard_map(
        functools.partial(body, n_parts=n_parts, n_grp=n_grp),
        mesh=mesh,
        in_specs=placed,
        out_specs=P(("dom", "grp"), None, None, None),
        check_vma=False,
    )
```

```python
import functools

import jax
import jax.numpy as jnp
from jax import lax
from jax.experimental import pallas as pl
from jax.experimental.pallas import tpu as pltpu
from jax.sharding import PartitionSpec as P

CYCLES = 2
PRE = 2
POST = 2
CSWEEPS = 4

OMEGA = 0.8
HIGHEST = lax.Precision.HIGHEST
MESH = pl.DeviceIdType.MESH
LANES = 128
F32 = jnp.float32
BF16 = jnp.bfloat16


def mm(a, b):
    return jnp.dot(a, b, precision=HIGHEST, preferred_element_type=F32)


def select(onehot2, x):
    hi = x.astype(BF16)
    lo = (x - hi.astype(F32)).astype(BF16)
    return jnp.dot(onehot2, jnp.concatenate([hi, lo], 0), preferred_element_type=F32)


def doubled(onehot):
    return jnp.concatenate([onehot, onehot], 1)


def vcycle_kernel(
    n_parts,
    n_grp,
    reach,
    width,
    rhs_hbm,
    absorption_hbm,
    vertical_hbm,
    horizontal_hbm,
    weights_hbm,
    nb_hbm,
    si_hbm,
    agg_hbm,
    cnb_hbm,
    cvert_hbm,
    chor_hbm,
    out_hbm,
    rhs_v,
    absorption_v,
    vertical_v,
    horizontal_v,
    weights_v,
    nb_v,
    si_v,
    agg_v,
    cnb_v,
    cvert_v,
    chor_v,
    out_v,
    load_sem,
    mt_local,
    mt_ghost,
    ghost,
    sendbuf,
    cext,
    send_sem,
    recv_sem,
    csend_sem,
    crecv_sem,
):
    me = lax.axis_index("dom") * n_grp + lax.axis_index("grp")
    offsets = list(range(1, reach + 1)) + [-d for d in range(1, reach + 1)]
    n_slots = len(offsets)
    by_distance = sorted(range(n_slots), key=lambda s: (abs(offsets[s]) != 2, abs(offsets[s]) == reach, abs(offsets[s]), offsets[s] < 0))
    tracers, layers, columns = rhs_v.shape[1:]
    n_nb = nb_v.shape[0]
    c1 = cnb_v.shape[2]
    n_ch = chor_v.shape[1]
    halo = n_slots * width

    def valid(q):
        return jnp.logical_and(q >= 0, q < n_parts)

    def device(q):
        return (lax.div(q, n_grp), lax.rem(q, n_grp))

    loads = [
        pltpu.make_async_copy(src, dst, load_sem.at[i])
        for i, (src, dst) in enumerate(
            [
                (rhs_hbm, rhs_v),
                (absorption_hbm, absorption_v),
                (vertical_hbm, vertical_v),
                (horizontal_hbm, horizontal_v),
                (weights_hbm, weights_v),
                (nb_hbm, nb_v),
                (si_hbm, si_v),
                (agg_hbm, agg_v),
                (cnb_hbm, cnb_v),
                (cvert_hbm, cvert_v),
                (chor_hbm, chor_v),
            ]
        )
    ]
    for copy in loads:
        copy.start()

    ghost[...] = jnp.zeros_like(ghost)
    cext[...] = jnp.zeros_like(cext)

    barrier = pltpu.get_barrier_semaphore()
    for d in offsets:
        @pl.when(valid(me + d))
        def _():
            pl.semaphore_signal(barrier, 1, device_id=device(me + d), device_id_type=MESH)
    for copy in loads:
        copy.wait()

    lane = lax.broadcasted_iota(jnp.int32, (8, LANES), 1)
    probe = pltpu.roll(lane, 1, 1)
    expected = jnp.where(lane == 0, LANES - 1, lane - 1)
    forward = (probe == expected)[0:1, :]
    layer_lane = lax.broadcasted_iota(jnp.int32, (1, LANES), 1)
    live = layer_lane < layers

    def shifted(x):
        a = pltpu.roll(x, 1, 1)
        b = pltpu.roll(x, LANES - 1, 1)
        lower = jnp.where(forward, a, b)
        upper = jnp.where(forward, b, a)
        return lower, upper

    pad_rows = jnp.zeros((LANES - layers, columns), F32)

    def to_cols(slab):
        return jnp.transpose(jnp.concatenate([slab, pad_rows], 0))

    ab = absorption_v[0]
    vr0 = vertical_v[0, 0]
    vr1 = vertical_v[0, 1]
    diag_rows = ab + jnp.abs(vr0) + jnp.abs(vr1)
    hsum = jnp.abs(horizontal_v[0, 0])
    for n in range(1, horizontal_v.shape[1]):
        hsum = hsum + jnp.abs(horizontal_v[0, n])
    diag_rows = diag_rows + hsum
    diag = jnp.where(live, to_cols(diag_rows), 1.0)
    inv_diag = 1.0 / diag
    rhs = jnp.concatenate([to_cols(rhs_v[0, t]) for t in range(tracers)], 1)
    st_blocks = []
    for s in range(n_slots):
        block = (lax.broadcasted_iota(jnp.int32, (columns, width), 0) == si_v[0, s:s + 1, :]).astype(F32)
        st_blocks.append(jnp.transpose(block))
    st = doubled(jnp.concatenate(st_blocks, 0).astype(BF16))
    ctx = {}

    def fine_setup():
        ctx["v0"] = jnp.where(layer_lane == 0, 0.0, to_cols(vr0))
        ctx["v1"] = jnp.where(layer_lane == layers - 1, 0.0, to_cols(vr1))
        ctx["h"] = [to_cols(horizontal_v[0, n]) for n in range(horizontal_v.shape[1])]
        k_iota = lax.broadcasted_iota(jnp.int32, (columns + halo, columns), 0)
        for n in range(n_nb):
            chosen = jnp.transpose((k_iota == nb_v[n]).astype(F32)).astype(BF16)
            rows = pl.ds(n * columns, columns)
            mt_local[rows, :] = doubled(chosen[:, :columns])
            mt_ghost[rows, :] = doubled(chosen[:, columns:])

    def coarse_setup():
        ctx["w"] = to_cols(weights_v[0])
        ctx["at"] = (lax.broadcasted_iota(jnp.int32, (c1, columns), 0) == agg_v[...]).astype(F32)
        a_full = jnp.transpose((lax.broadcasted_iota(jnp.int32, (LANES, columns), 0) == agg_v[...]).astype(F32))
        ctx["a"] = doubled(a_full[:, :c1].astype(BF16))
        coarse_rows = cext.shape[1]
        mct_blocks = []
        for n in range(n_ch):
            block = (lax.broadcasted_iota(jnp.int32, (coarse_rows, c1), 0) == cnb_v[n]).astype(F32)
            mct_blocks.append(jnp.transpose(block))
        ctx["mct"] = doubled(jnp.concatenate(mct_blocks, 0).astype(BF16))
        widen = (
            lax.broadcasted_iota(jnp.int32, (layers, LANES), 0) == lax.broadcasted_iota(jnp.int32, (layers, LANES), 1)
        ).astype(F32)

        def coarse_cols(slab):
            return mm(slab, widen)

        cvr0 = cvert_v[0, 0]
        cvr1 = cvert_v[0, 1]
        cdiag_rows = 0.5 + jnp.abs(cvr0) + jnp.abs(cvr1)
        csum = jnp.abs(chor_v[0, 0])
        for n in range(1, n_ch):
            csum = csum + jnp.abs(chor_v[0, n])
        cdiag = jnp.where(live, coarse_cols(cdiag_rows + csum), 1.0)
        ctx["cdiag"] = cdiag
        ctx["inv_cdiag"] = 1.0 / cdiag
        ctx["cv0"] = jnp.where(layer_lane == 0, 0.0, coarse_cols(cvr0))
        ctx["cv1"] = jnp.where(layer_lane == layers - 1, 0.0, coarse_cols(cvr1))
        ctx["ch"] = [coarse_cols(chor_v[0, n]) for n in range(n_ch)]

    setup_hooks = [fine_setup, coarse_setup]

    def halves(x):
        return [x[:, t * LANES:(t + 1) * LANES] for t in range(x.shape[1] // LANES)]

    def fine_copy(slot, s):
        rows = pl.ds(s * width, width)
        return pltpu.make_async_remote_copy(
            src_ref=sendbuf.at[rows],
            dst_ref=ghost.at[slot, rows],
            send_sem=send_sem.at[s],
            recv_sem=recv_sem.at[slot, s],
            device_id=device(me + offsets[s]),
            device_id_type=MESH,
        )

    fine_round = [0]
    pending = {"fine": None, "coarse": None}

    def finish_sends(kind, copy_of):
        slot = pending[kind]
        if slot is None:
            return
        pending[kind] = None
        for s in range(n_slots):
            @pl.when(valid(me + offsets[s]))
            def _():
                copy_of(slot, s).wait_send()

    def fine_apply(field):
        slot = fine_round[0] % 2
        fine_round[0] += 1
        finish_sends("fine", fine_copy)
        hi = field.astype(BF16)
        stacked = jnp.concatenate([hi, (field - hi.astype(F32)).astype(BF16)], 0)
        for group in (by_distance[:2], by_distance[2:]):
            for s in group:
                rows = pl.ds(s * width, width)
                sendbuf[rows, :] = jnp.dot(st[s * width:(s + 1) * width], stacked, preferred_element_type=F32)
            for s in group:
                @pl.when(valid(me + offsets[s]))
                def _():
                    fine_copy(slot, s).start()
        if setup_hooks:
            setup_hooks.pop(0)()
        v0, v1, h = ctx["v0"], ctx["v1"], ctx["h"]
        local = select(mt_local[...], field)
        bases = []
        for t, part in enumerate(halves(field)):
            lower, upper = shifted(part)
            total = diag * part + v0 * lower + v1 * upper
            for n in range(n_nb):
                total = total + h[n] * local[n * columns:(n + 1) * columns, t * LANES:(t + 1) * LANES]
            bases.append(total)
        pending["fine"] = slot
        for s in range(n_slots):
            @pl.when(valid(me - offsets[s]))
            def _():
                fine_copy(slot, s).wait_recv()
        gathered = select(mt_ghost[...], ghost[slot])
        totals = []
        for t, total in enumerate(bases):
            for n in range(n_nb):
                total = total + h[n] * gathered[n * columns:(n + 1) * columns, t * LANES:(t + 1) * LANES]
            totals.append(total)
        return jnp.concatenate(totals, 1)

    def coarse_copy(slot, k):
        d = offsets[k]
        return pltpu.make_async_remote_copy(
            src_ref=cext.at[slot, pl.ds(reach * c1, c1)],
            dst_ref=cext.at[slot, pl.ds((reach - d) * c1, c1)],
            send_sem=csend_sem.at[k],
            recv_sem=crecv_sem.at[slot, k],
            device_id=device(me + d),
            device_id_type=MESH,
        )

    coarse_round = [0]

    def coarse_apply(corr):
        slot = coarse_round[0] % 2
        coarse_round[0] += 1
        finish_sends("coarse", coarse_copy)
        cext[slot, pl.ds(reach * c1, c1), :] = corr
        cdiag, cv0, cv1, ch, mct = ctx["cdiag"], ctx["cv0"], ctx["cv1"], ctx["ch"], ctx["mct"]
        for k in by_distance:
            @pl.when(valid(me + offsets[k]))
            def _():
                coarse_copy(slot, k).start()
        bases = []
        for part in halves(corr):
            lower, upper = shifted(part)
            bases.append(cdiag * part + cv0 * lower + cv1 * upper)
        pending["coarse"] = slot
        for k in range(n_slots):
            @pl.when(valid(me - offsets[k]))
            def _():
                coarse_copy(slot, k).wait_recv()
        gathered = select(mct, cext[slot])
        totals = []
        for t, total in enumerate(bases):
            for n in range(n_ch):
                total = total + ch[n] * gathered[n * c1:(n + 1) * c1, t * LANES:(t + 1) * LANES]
            totals.append(total)
        return jnp.concatenate(totals, 1)

    peers = sum(valid(me + d).astype(jnp.int32) for d in offsets)
    pl.semaphore_wait(barrier, peers)

    def per_half(x, coeff, op):
        return jnp.concatenate([op(part, coeff) for part in halves(x)], 1)

    solution = per_half(OMEGA * rhs, inv_diag, lambda x, c: x * c)
    for cycle_index in range(CYCLES):
        for sweep_index in range(PRE):
            if cycle_index == 0 and sweep_index == 0:
                continue
            step = OMEGA * (rhs - fine_apply(solution))
            solution = solution + per_half(step, inv_diag, lambda x, c: x * c)
        residual = rhs - fine_apply(solution)
        weighted = per_half(residual, ctx["w"], lambda x, c: x * c)
        coarse_source = mm(ctx["at"], weighted)
        correction = per_half(OMEGA * coarse_source, ctx["inv_cdiag"], lambda x, c: x * c)
        for coarse_sweep_index in range(CSWEEPS - 1):
            step = OMEGA * (coarse_source - coarse_apply(correction))
            correction = correction + per_half(step, ctx["inv_cdiag"], lambda x, c: x * c)
        lifted = select(ctx["a"], correction)
        solution = solution + per_half(lifted, ctx["w"], lambda x, c: x * c)
        for sweep_index in range(POST):
            step = OMEGA * (rhs - fine_apply(solution))
            solution = solution + per_half(step, inv_diag, lambda x, c: x * c)
    finish_sends("fine", fine_copy)
    finish_sends("coarse", coarse_copy)
    for t, part in enumerate(halves(solution)):
        out_v[0, t] = jnp.transpose(part)[:layers]
    store = pltpu.make_async_copy(out_v, out_hbm, load_sem.at[len(loads)])
    store.start()
    store.wait()


def body(
    right_side,
    absorption,
    vertical,
    horizontal,
    neighbours,
    send_index,
    aggregate,
    weights,
    coarse_vertical,
    coarse_horizontal,
    coarse_neighbours,
    *,
    n_parts,
    n_grp,
):
    _, tracers, layers, columns = right_side.shape
    reach = send_index.shape[1] // 2
    width = send_index.shape[2]
    c1 = coarse_neighbours.shape[2]
    n_slots = 2 * reach

    args = (
        right_side,
        absorption,
        vertical,
        horizontal,
        weights,
        jnp.swapaxes(neighbours, 0, 1),
        send_index,
        aggregate,
        jnp.swapaxes(coarse_neighbours, 0, 1),
        jnp.swapaxes(coarse_vertical, 2, 3),
        jnp.swapaxes(coarse_horizontal, 2, 3),
    )
    ext_rows = columns + n_slots * width
    coarse_rows = ext_rows
    scratch = [pltpu.VMEM(x.shape, x.dtype) for x in args] + [
        pltpu.VMEM(right_side.shape, F32),
        pltpu.SemaphoreType.DMA((len(args) + 1,)),
        pltpu.VMEM((neighbours.shape[1] * columns, 2 * columns), BF16),
        pltpu.VMEM((neighbours.shape[1] * columns, 2 * n_slots * width), BF16),
        pltpu.VMEM((2, n_slots * width, tracers * LANES), F32),
        pltpu.VMEM((n_slots * width, tracers * LANES), F32),
        pltpu.VMEM((2, coarse_rows, tracers * LANES), F32),
        pltpu.SemaphoreType.DMA((n_slots,)),
        pltpu.SemaphoreType.DMA((2, n_slots)),
        pltpu.SemaphoreType.DMA((n_slots,)),
        pltpu.SemaphoreType.DMA((2, n_slots)),
    ]
    return pl.pallas_call(
        functools.partial(vcycle_kernel, n_parts, n_grp, reach, width),
        out_shape=jax.ShapeDtypeStruct(right_side.shape, F32),
        in_specs=[pl.BlockSpec(memory_space=pl.ANY)] * len(args),
        out_specs=pl.BlockSpec(memory_space=pl.ANY),
        scratch_shapes=scratch,
        compiler_params=pltpu.CompilerParams(collective_id=0, has_side_effects=True),
    )(*args)


def solution(mesh):
    placed = (
        P(("dom", "grp"), None, None, None),
        P(("dom", "grp"), None, None),
        P(("dom", "grp"), None, None, None),
        P(("dom", "grp"), None, None, None),
        P(("dom", "grp"), None, None),
        P(("dom", "grp"), None, None),
        P(("dom", "grp"), None),
        P(("dom", "grp"), None, None),
        P(("dom", "grp"), None, None, None),
        P(("dom", "grp"), None, None, None),
        P(("dom", "grp"), None, None),
    )
    n_grp = mesh.shape["grp"]
    n_parts = mesh.shape["dom"] * n_grp
    return jax.shard_map(
        functools.partial(body, n_parts=n_parts, n_grp=n_grp),
        mesh=mesh,
        in_specs=placed,
        out_specs=P(("dom", "grp"), None, None, None),
        check_vma=False,
    )
```

```python
import functools

import jax
import jax.numpy as jnp
from jax import lax
from jax.experimental import pallas as pl
from jax.experimental.pallas import tpu as pltpu
from jax.sharding import PartitionSpec as P

CYCLES = 2
PRE = 2
POST = 2
CSWEEPS = 4

OMEGA = 0.8
HIGHEST = lax.Precision.HIGHEST
MESH = pl.DeviceIdType.MESH
LANES = 128
F32 = jnp.float32
BF16 = jnp.bfloat16


def mm(a, b):
    return jnp.dot(a, b, precision=HIGHEST, preferred_element_type=F32)


def select(onehot2, x):
    hi = x.astype(BF16)
    lo = (x - hi.astype(F32)).astype(BF16)
    return jnp.dot(onehot2, jnp.concatenate([hi, lo], 0), preferred_element_type=F32)


def doubled(onehot):
    return jnp.concatenate([onehot, onehot], 1)


def vcycle_kernel(
    n_parts,
    n_grp,
    reach,
    width,
    rhs_hbm,
    absorption_hbm,
    vertical_hbm,
    horizontal_hbm,
    weights_hbm,
    nb_hbm,
    si_hbm,
    agg_hbm,
    cnb_hbm,
    cvert_hbm,
    chor_hbm,
    out_hbm,
    rhs_v,
    absorption_v,
    vertical_v,
    horizontal_v,
    weights_v,
    nb_v,
    si_v,
    agg_v,
    cnb_v,
    cvert_v,
    chor_v,
    out_v,
    load_sem,
    mt_local,
    mt_ghost,
    ghost,
    sendbuf,
    cext,
    send_sem,
    recv_sem,
    csend_sem,
    crecv_sem,
):
    me = lax.axis_index("dom") * n_grp + lax.axis_index("grp")
    offsets = list(range(1, reach + 1)) + [-d for d in range(1, reach + 1)]
    n_slots = len(offsets)
    by_distance = sorted(range(n_slots), key=lambda s: (abs(offsets[s]) != 2, abs(offsets[s]) == reach, abs(offsets[s]), offsets[s] < 0))
    tracers, layers, columns = rhs_v.shape[1:]
    n_nb = nb_v.shape[0]
    c1 = cnb_v.shape[2]
    n_ch = chor_v.shape[1]
    halo = n_slots * width

    def valid(q):
        return jnp.logical_and(q >= 0, q < n_parts)

    def device(q):
        return (lax.div(q, n_grp), lax.rem(q, n_grp))

    loads = [
        pltpu.make_async_copy(src, dst, load_sem.at[i])
        for i, (src, dst) in enumerate(
            [
                (rhs_hbm, rhs_v),
                (absorption_hbm, absorption_v),
                (vertical_hbm, vertical_v),
                (horizontal_hbm, horizontal_v),
                (weights_hbm, weights_v),
                (nb_hbm, nb_v),
                (si_hbm, si_v),
                (agg_hbm, agg_v),
                (cnb_hbm, cnb_v),
                (cvert_hbm, cvert_v),
                (chor_hbm, chor_v),
            ]
        )
    ]
    for copy in loads:
        copy.start()

    ghost[...] = jnp.zeros_like(ghost)
    cext[...] = jnp.zeros_like(cext)

    barrier = pltpu.get_barrier_semaphore()
    for d in offsets:
        @pl.when(valid(me + d))
        def _():
            pl.semaphore_signal(barrier, 1, device_id=device(me + d), device_id_type=MESH)
    for copy in loads:
        copy.wait()

    lane = lax.broadcasted_iota(jnp.int32, (8, LANES), 1)
    probe = pltpu.roll(lane, 1, 1)
    expected = jnp.where(lane == 0, LANES - 1, lane - 1)
    forward = (probe == expected)[0:1, :]
    layer_lane = lax.broadcasted_iota(jnp.int32, (1, LANES), 1)
    live = layer_lane < layers

    def shifted(x):
        a = pltpu.roll(x, 1, 1)
        b = pltpu.roll(x, LANES - 1, 1)
        lower = jnp.where(forward, a, b)
        upper = jnp.where(forward, b, a)
        return lower, upper

    pad_rows = jnp.zeros((LANES - layers, columns), F32)

    def to_cols(slab):
        return jnp.transpose(jnp.concatenate([slab, pad_rows], 0))

    ab = absorption_v[0]
    vr0 = vertical_v[0, 0]
    vr1 = vertical_v[0, 1]
    diag_rows = ab + jnp.abs(vr0) + jnp.abs(vr1)
    hsum = jnp.abs(horizontal_v[0, 0])
    for n in range(1, horizontal_v.shape[1]):
        hsum = hsum + jnp.abs(horizontal_v[0, n])
    diag_rows = diag_rows + hsum
    diag = jnp.where(live, to_cols(diag_rows), 1.0)
    inv_diag = 1.0 / diag
    rhs = jnp.concatenate([to_cols(rhs_v[0, t]) for t in range(tracers)], 1)
    st_blocks = []
    for s in range(n_slots):
        block = (lax.broadcasted_iota(jnp.int32, (columns, width), 0) == si_v[0, s:s + 1, :]).astype(F32)
        st_blocks.append(jnp.transpose(block))
    st = doubled(jnp.concatenate(st_blocks, 0).astype(BF16))
    ctx = {}

    def fine_setup():
        ctx["v0"] = jnp.where(layer_lane == 0, 0.0, to_cols(vr0))
        ctx["v1"] = jnp.where(layer_lane == layers - 1, 0.0, to_cols(vr1))
        ctx["h"] = [to_cols(horizontal_v[0, n]) for n in range(horizontal_v.shape[1])]
        k_iota = lax.broadcasted_iota(jnp.int32, (columns + halo, columns), 0)
        for n in range(n_nb):
            chosen = jnp.transpose((k_iota == nb_v[n]).astype(F32)).astype(BF16)
            rows = pl.ds(n * columns, columns)
            mt_local[rows, :] = doubled(chosen[:, :columns])
            mt_ghost[rows, :] = doubled(chosen[:, columns:])

    def coarse_setup():
        ctx["w"] = to_cols(weights_v[0])
        ctx["at"] = (lax.broadcasted_iota(jnp.int32, (c1, columns), 0) == agg_v[...]).astype(F32)
        a_full = jnp.transpose((lax.broadcasted_iota(jnp.int32, (LANES, columns), 0) == agg_v[...]).astype(F32))
        ctx["a"] = doubled(a_full[:, :c1].astype(BF16))
        coarse_rows = cext.shape[1]
        mct_blocks = []
        for n in range(n_ch):
            block = (lax.broadcasted_iota(jnp.int32, (coarse_rows, c1), 0) == cnb_v[n]).astype(F32)
            mct_blocks.append(jnp.transpose(block))
        ctx["mct"] = doubled(jnp.concatenate(mct_blocks, 0).astype(BF16))
        widen = (
            lax.broadcasted_iota(jnp.int32, (layers, LANES), 0) == lax.broadcasted_iota(jnp.int32, (layers, LANES), 1)
        ).astype(F32)

        def coarse_cols(slab):
            return mm(slab, widen)

        cvr0 = cvert_v[0, 0]
        cvr1 = cvert_v[0, 1]
        cdiag_rows = 0.5 + jnp.abs(cvr0) + jnp.abs(cvr1)
        csum = jnp.abs(chor_v[0, 0])
        for n in range(1, n_ch):
            csum = csum + jnp.abs(chor_v[0, n])
        cdiag = jnp.where(live, coarse_cols(cdiag_rows + csum), 1.0)
        ctx["cdiag"] = cdiag
        ctx["inv_cdiag"] = 1.0 / cdiag
        ctx["cv0"] = jnp.where(layer_lane == 0, 0.0, coarse_cols(cvr0))
        ctx["cv1"] = jnp.where(layer_lane == layers - 1, 0.0, coarse_cols(cvr1))
        ctx["ch"] = [coarse_cols(chor_v[0, n]) for n in range(n_ch)]

    setup_hooks = [fine_setup, coarse_setup]

    def halves(x):
        return [x[:, t * LANES:(t + 1) * LANES] for t in range(x.shape[1] // LANES)]

    def fine_copy(slot, s):
        rows = pl.ds(s * width, width)
        return pltpu.make_async_remote_copy(
            src_ref=sendbuf.at[rows],
            dst_ref=ghost.at[slot, rows],
            send_sem=send_sem.at[s],
            recv_sem=recv_sem.at[slot, s],
            device_id=device(me + offsets[s]),
            device_id_type=MESH,
        )

    fine_round = [0]
    pending = {"fine": None, "coarse": None}

    def finish_sends(kind, copy_of):
        slot = pending[kind]
        if slot is None:
            return
        pending[kind] = None
        for s in range(n_slots):
            @pl.when(valid(me + offsets[s]))
            def _():
                copy_of(slot, s).wait_send()

    def fine_apply(field):
        first = fine_round[0] == 0
        slot = fine_round[0] % 2
        fine_round[0] += 1
        finish_sends("fine", fine_copy)
        hi = field.astype(BF16)
        stacked = jnp.concatenate([hi, (field - hi.astype(F32)).astype(BF16)], 0)
        for group in (by_distance,) if first else (by_distance[:2], by_distance[2:]):
            for s in group:
                rows = pl.ds(s * width, width)
                sendbuf[rows, :] = jnp.dot(st[s * width:(s + 1) * width], stacked, preferred_element_type=F32)
            if first:
                pl.semaphore_wait(barrier, peers)
            for s in group:
                @pl.when(valid(me + offsets[s]))
                def _():
                    fine_copy(slot, s).start()
        if setup_hooks:
            setup_hooks.pop(0)()
        v0, v1, h = ctx["v0"], ctx["v1"], ctx["h"]
        local = select(mt_local[...], field)
        bases = []
        for t, part in enumerate(halves(field)):
            lower, upper = shifted(part)
            total = diag * part + v0 * lower + v1 * upper
            for n in range(n_nb):
                total = total + h[n] * local[n * columns:(n + 1) * columns, t * LANES:(t + 1) * LANES]
            bases.append(total)
        pending["fine"] = slot
        for s in range(n_slots):
            @pl.when(valid(me - offsets[s]))
            def _():
                fine_copy(slot, s).wait_recv()
        gathered = select(mt_ghost[...], ghost[slot])
        totals = []
        for t, total in enumerate(bases):
            for n in range(n_nb):
                total = total + h[n] * gathered[n * columns:(n + 1) * columns, t * LANES:(t + 1) * LANES]
            totals.append(total)
        return jnp.concatenate(totals, 1)

    def coarse_copy(slot, k):
        d = offsets[k]
        return pltpu.make_async_remote_copy(
            src_ref=cext.at[slot, pl.ds(reach * c1, c1)],
            dst_ref=cext.at[slot, pl.ds((reach - d) * c1, c1)],
            send_sem=csend_sem.at[k],
            recv_sem=crecv_sem.at[slot, k],
            device_id=device(me + d),
            device_id_type=MESH,
        )

    coarse_round = [0]

    def coarse_apply(corr):
        slot = coarse_round[0] % 2
        coarse_round[0] += 1
        finish_sends("coarse", coarse_copy)
        cext[slot, pl.ds(reach * c1, c1), :] = corr
        cdiag, cv0, cv1, ch, mct = ctx["cdiag"], ctx["cv0"], ctx["cv1"], ctx["ch"], ctx["mct"]
        for k in by_distance:
            @pl.when(valid(me + offsets[k]))
            def _():
                coarse_copy(slot, k).start()
        bases = []
        for part in halves(corr):
            lower, upper = shifted(part)
            bases.append(cdiag * part + cv0 * lower + cv1 * upper)
        pending["coarse"] = slot
        for k in range(n_slots):
            @pl.when(valid(me - offsets[k]))
            def _():
                coarse_copy(slot, k).wait_recv()
        gathered = select(mct, cext[slot])
        totals = []
        for t, total in enumerate(bases):
            for n in range(n_ch):
                total = total + ch[n] * gathered[n * c1:(n + 1) * c1, t * LANES:(t + 1) * LANES]
            totals.append(total)
        return jnp.concatenate(totals, 1)

    peers = sum(valid(me + d).astype(jnp.int32) for d in offsets)

    def per_half(x, coeff, op):
        return jnp.concatenate([op(part, coeff) for part in halves(x)], 1)

    solution = per_half(OMEGA * rhs, inv_diag, lambda x, c: x * c)
    for cycle_index in range(CYCLES):
        for sweep_index in range(PRE):
            if cycle_index == 0 and sweep_index == 0:
                continue
            step = OMEGA * (rhs - fine_apply(solution))
            solution = solution + per_half(step, inv_diag, lambda x, c: x * c)
        residual = rhs - fine_apply(solution)
        weighted = per_half(residual, ctx["w"], lambda x, c: x * c)
        coarse_source = mm(ctx["at"], weighted)
        correction = per_half(OMEGA * coarse_source, ctx["inv_cdiag"], lambda x, c: x * c)
        for coarse_sweep_index in range(CSWEEPS - 1):
            step = OMEGA * (coarse_source - coarse_apply(correction))
            correction = correction + per_half(step, ctx["inv_cdiag"], lambda x, c: x * c)
        lifted = select(ctx["a"], correction)
        solution = solution + per_half(lifted, ctx["w"], lambda x, c: x * c)
        for sweep_index in range(POST):
            step = OMEGA * (rhs - fine_apply(solution))
            solution = solution + per_half(step, inv_diag, lambda x, c: x * c)
    finish_sends("fine", fine_copy)
    finish_sends("coarse", coarse_copy)
    for t, part in enumerate(halves(solution)):
        out_v[0, t] = jnp.transpose(part)[:layers]
    store = pltpu.make_async_copy(out_v, out_hbm, load_sem.at[len(loads)])
    store.start()
    store.wait()


def body(
    right_side,
    absorption,
    vertical,
    horizontal,
    neighbours,
    send_index,
    aggregate,
    weights,
    coarse_vertical,
    coarse_horizontal,
    coarse_neighbours,
    *,
    n_parts,
    n_grp,
):
    _, tracers, layers, columns = right_side.shape
    reach = send_index.shape[1] // 2
    width = send_index.shape[2]
    c1 = coarse_neighbours.shape[2]
    n_slots = 2 * reach

    args = (
        right_side,
        absorption,
        vertical,
        horizontal,
        weights,
        jnp.swapaxes(neighbours, 0, 1),
        send_index,
        aggregate,
        jnp.swapaxes(coarse_neighbours, 0, 1),
        jnp.swapaxes(coarse_vertical, 2, 3),
        jnp.swapaxes(coarse_horizontal, 2, 3),
    )
    ext_rows = columns + n_slots * width
    coarse_rows = ext_rows
    scratch = [pltpu.VMEM(x.shape, x.dtype) for x in args] + [
        pltpu.VMEM(right_side.shape, F32),
        pltpu.SemaphoreType.DMA((len(args) + 1,)),
        pltpu.VMEM((neighbours.shape[1] * columns, 2 * columns), BF16),
        pltpu.VMEM((neighbours.shape[1] * columns, 2 * n_slots * width), BF16),
        pltpu.VMEM((2, n_slots * width, tracers * LANES), F32),
        pltpu.VMEM((n_slots * width, tracers * LANES), F32),
        pltpu.VMEM((2, coarse_rows, tracers * LANES), F32),
        pltpu.SemaphoreType.DMA((n_slots,)),
        pltpu.SemaphoreType.DMA((2, n_slots)),
        pltpu.SemaphoreType.DMA((n_slots,)),
        pltpu.SemaphoreType.DMA((2, n_slots)),
    ]
    return pl.pallas_call(
        functools.partial(vcycle_kernel, n_parts, n_grp, reach, width),
        out_shape=jax.ShapeDtypeStruct(right_side.shape, F32),
        in_specs=[pl.BlockSpec(memory_space=pl.ANY)] * len(args),
        out_specs=pl.BlockSpec(memory_space=pl.ANY),
        scratch_shapes=scratch,
        compiler_params=pltpu.CompilerParams(collective_id=0, has_side_effects=True),
    )(*args)


def solution(mesh):
    placed = (
        P(("dom", "grp"), None, None, None),
        P(("dom", "grp"), None, None),
        P(("dom", "grp"), None, None, None),
        P(("dom", "grp"), None, None, None),
        P(("dom", "grp"), None, None),
        P(("dom", "grp"), None, None),
        P(("dom", "grp"), None),
        P(("dom", "grp"), None, None),
        P(("dom", "grp"), None, None, None),
        P(("dom", "grp"), None, None, None),
        P(("dom", "grp"), None, None),
    )
    n_grp = mesh.shape["grp"]
    n_parts = mesh.shape["dom"] * n_grp
    return jax.shard_map(
        functools.partial(body, n_parts=n_parts, n_grp=n_grp),
        mesh=mesh,
        in_specs=placed,
        out_specs=P(("dom", "grp"), None, None, None),
        check_vma=False,
    )
```

```python
import functools

import jax
import jax.numpy as jnp
from jax import lax
from jax.experimental import pallas as pl
from jax.experimental.pallas import tpu as pltpu
from jax.sharding import PartitionSpec as P

CYCLES = 2
PRE = 2
POST = 2
CSWEEPS = 4

OMEGA = 0.8
HIGHEST = lax.Precision.HIGHEST
MESH = pl.DeviceIdType.MESH
LANES = 128
F32 = jnp.float32
BF16 = jnp.bfloat16


def mm(a, b):
    return jnp.dot(a, b, precision=HIGHEST, preferred_element_type=F32)


def select(onehot2, x):
    hi = x.astype(BF16)
    lo = (x - hi.astype(F32)).astype(BF16)
    return jnp.dot(onehot2, jnp.concatenate([hi, lo], 0), preferred_element_type=F32)


def doubled(onehot):
    return jnp.concatenate([onehot, onehot], 1)


def vcycle_kernel(
    n_parts,
    n_grp,
    reach,
    width,
    rhs_hbm,
    absorption_hbm,
    vertical_hbm,
    horizontal_hbm,
    weights_hbm,
    nb_hbm,
    si_hbm,
    agg_hbm,
    cnb_hbm,
    cvert_hbm,
    chor_hbm,
    out_hbm,
    rhs_v,
    absorption_v,
    vertical_v,
    horizontal_v,
    weights_v,
    nb_v,
    si_v,
    agg_v,
    cnb_v,
    cvert_v,
    chor_v,
    out_v,
    load_sem,
    mt_local,
    mt_ghost,
    ghost,
    sendbuf,
    cext,
    send_sem,
    recv_sem,
    csend_sem,
    crecv_sem,
):
    me = lax.axis_index("dom") * n_grp + lax.axis_index("grp")
    offsets = list(range(1, reach + 1)) + [-d for d in range(1, reach + 1)]
    n_slots = len(offsets)
    by_distance = sorted(range(n_slots), key=lambda s: (abs(offsets[s]) != 2, abs(offsets[s]) == reach, abs(offsets[s]), offsets[s] < 0))
    tracers, layers, columns = rhs_v.shape[1:]
    n_nb = nb_v.shape[0]
    c1 = cnb_v.shape[2]
    n_ch = chor_v.shape[1]
    halo = n_slots * width

    def valid(q):
        return jnp.logical_and(q >= 0, q < n_parts)

    def device(q):
        return (lax.div(q, n_grp), lax.rem(q, n_grp))

    loads = [
        pltpu.make_async_copy(src, dst, load_sem.at[i])
        for i, (src, dst) in enumerate(
            [
                (rhs_hbm, rhs_v),
                (absorption_hbm, absorption_v),
                (vertical_hbm, vertical_v),
                (horizontal_hbm, horizontal_v),
                (weights_hbm, weights_v),
                (nb_hbm, nb_v),
                (si_hbm, si_v),
                (agg_hbm, agg_v),
                (cnb_hbm, cnb_v),
                (cvert_hbm, cvert_v),
                (chor_hbm, chor_v),
            ]
        )
    ]
    for copy in loads:
        copy.start()

    ghost[...] = jnp.zeros_like(ghost)
    cext[...] = jnp.zeros_like(cext)

    barrier = pltpu.get_barrier_semaphore()
    for d in offsets:
        @pl.when(valid(me + d))
        def _():
            pl.semaphore_signal(barrier, 1, device_id=device(me + d), device_id_type=MESH)
    for copy in loads:
        copy.wait()

    lane = lax.broadcasted_iota(jnp.int32, (8, LANES), 1)
    probe = pltpu.roll(lane, 1, 1)
    expected = jnp.where(lane == 0, LANES - 1, lane - 1)
    forward = (probe == expected)[0:1, :]
    layer_lane = lax.broadcasted_iota(jnp.int32, (1, LANES), 1)
    live = layer_lane < layers

    def shifted(x):
        a = pltpu.roll(x, 1, 1)
        b = pltpu.roll(x, LANES - 1, 1)
        lower = jnp.where(forward, a, b)
        upper = jnp.where(forward, b, a)
        return lower, upper

    pad_rows = jnp.zeros((LANES - layers, columns), F32)

    def to_cols(slab):
        return jnp.transpose(jnp.concatenate([slab, pad_rows], 0))

    ab = absorption_v[0]
    vr0 = vertical_v[0, 0]
    vr1 = vertical_v[0, 1]
    diag_rows = ab + jnp.abs(vr0) + jnp.abs(vr1)
    hsum = jnp.abs(horizontal_v[0, 0])
    for n in range(1, horizontal_v.shape[1]):
        hsum = hsum + jnp.abs(horizontal_v[0, n])
    diag_rows = diag_rows + hsum
    diag = jnp.where(live, to_cols(diag_rows), 1.0)
    inv_diag = 1.0 / diag
    rhs = jnp.concatenate([to_cols(rhs_v[0, t]) for t in range(tracers)], 1)
    st_blocks = []
    for s in range(n_slots):
        block = (lax.broadcasted_iota(jnp.int32, (columns, width), 0) == si_v[0, s:s + 1, :]).astype(F32)
        st_blocks.append(jnp.transpose(block))
    st = doubled(jnp.concatenate(st_blocks, 0).astype(BF16))
    ctx = {}

    def fine_setup():
        ctx["v0"] = jnp.where(layer_lane == 0, 0.0, to_cols(vr0))
        ctx["v1"] = jnp.where(layer_lane == layers - 1, 0.0, to_cols(vr1))
        ctx["h"] = [to_cols(horizontal_v[0, n]) for n in range(horizontal_v.shape[1])]
        k_iota = lax.broadcasted_iota(jnp.int32, (columns + halo, columns), 0)
        for n in range(n_nb):
            chosen = jnp.transpose((k_iota == nb_v[n]).astype(F32)).astype(BF16)
            rows = pl.ds(n * columns, columns)
            mt_local[rows, :] = doubled(chosen[:, :columns])
            mt_ghost[rows, :] = doubled(chosen[:, columns:])

    def coarse_setup():
        ctx["w"] = to_cols(weights_v[0])
        ctx["at"] = (lax.broadcasted_iota(jnp.int32, (c1, columns), 0) == agg_v[...]).astype(F32)
        a_full = jnp.transpose((lax.broadcasted_iota(jnp.int32, (LANES, columns), 0) == agg_v[...]).astype(F32))
        ctx["a"] = doubled(a_full[:, :c1].astype(BF16))
        coarse_rows = cext.shape[1]
        mct_blocks = []
        for n in range(n_ch):
            block = (lax.broadcasted_iota(jnp.int32, (coarse_rows, c1), 0) == cnb_v[n]).astype(F32)
            mct_blocks.append(jnp.transpose(block))
        ctx["mct"] = doubled(jnp.concatenate(mct_blocks, 0).astype(BF16))
        widen = (
            lax.broadcasted_iota(jnp.int32, (layers, LANES), 0) == lax.broadcasted_iota(jnp.int32, (layers, LANES), 1)
        ).astype(F32)

        def coarse_cols(slab):
            return mm(slab, widen)

        cvr0 = cvert_v[0, 0]
        cvr1 = cvert_v[0, 1]
        cdiag_rows = 0.5 + jnp.abs(cvr0) + jnp.abs(cvr1)
        csum = jnp.abs(chor_v[0, 0])
        for n in range(1, n_ch):
            csum = csum + jnp.abs(chor_v[0, n])
        cdiag = jnp.where(live, coarse_cols(cdiag_rows + csum), 1.0)
        ctx["cdiag"] = cdiag
        ctx["inv_cdiag"] = 1.0 / cdiag
        ctx["cv0"] = jnp.where(layer_lane == 0, 0.0, coarse_cols(cvr0))
        ctx["cv1"] = jnp.where(layer_lane == layers - 1, 0.0, coarse_cols(cvr1))
        ctx["ch"] = [coarse_cols(chor_v[0, n]) for n in range(n_ch)]

    setup_hooks = [fine_setup, coarse_setup]

    def halves(x):
        return [x[:, t * LANES:(t + 1) * LANES] for t in range(x.shape[1] // LANES)]

    def fine_copy(slot, s):
        rows = pl.ds(s * width, width)
        return pltpu.make_async_remote_copy(
            src_ref=sendbuf.at[rows],
            dst_ref=ghost.at[slot, rows],
            send_sem=send_sem.at[s],
            recv_sem=recv_sem.at[slot, s],
            device_id=device(me + offsets[s]),
            device_id_type=MESH,
        )

    fine_round = [0]
    pending = {"fine": None, "coarse": None}

    def finish_sends(kind, copy_of):
        slot = pending[kind]
        if slot is None:
            return
        pending[kind] = None
        for s in range(n_slots):
            @pl.when(valid(me + offsets[s]))
            def _():
                copy_of(slot, s).wait_send()

    def fine_apply(field):
        first = fine_round[0] == 0
        slot = fine_round[0] % 2
        fine_round[0] += 1
        finish_sends("fine", fine_copy)
        hi = field.astype(BF16)
        stacked = jnp.concatenate([hi, (field - hi.astype(F32)).astype(BF16)], 0)
        for group in (by_distance,) if first else (by_distance[:2], by_distance[2:]):
            for s in group:
                rows = pl.ds(s * width, width)
                sendbuf[rows, :] = jnp.dot(st[s * width:(s + 1) * width], stacked, preferred_element_type=F32)
            if first:
                pl.semaphore_wait(barrier, peers)
            for s in group:
                @pl.when(valid(me + offsets[s]))
                def _():
                    fine_copy(slot, s).start()
        if setup_hooks:
            setup_hooks.pop(0)()
        v0, v1, h = ctx["v0"], ctx["v1"], ctx["h"]
        local = jnp.dot(mt_local[...], stacked, preferred_element_type=F32)
        bases = []
        for t, part in enumerate(halves(field)):
            lower, upper = shifted(part)
            total = diag * part + v0 * lower + v1 * upper
            for n in range(n_nb):
                total = total + h[n] * local[n * columns:(n + 1) * columns, t * LANES:(t + 1) * LANES]
            bases.append(total)
        pending["fine"] = slot
        for s in range(n_slots):
            @pl.when(valid(me - offsets[s]))
            def _():
                fine_copy(slot, s).wait_recv()
        gathered = select(mt_ghost[...], ghost[slot])
        totals = []
        for t, total in enumerate(bases):
            for n in range(n_nb):
                total = total + h[n] * gathered[n * columns:(n + 1) * columns, t * LANES:(t + 1) * LANES]
            totals.append(total)
        return jnp.concatenate(totals, 1)

    def coarse_copy(slot, k):
        d = offsets[k]
        return pltpu.make_async_remote_copy(
            src_ref=cext.at[slot, pl.ds(reach * c1, c1)],
            dst_ref=cext.at[slot, pl.ds((reach - d) * c1, c1)],
            send_sem=csend_sem.at[k],
            recv_sem=crecv_sem.at[slot, k],
            device_id=device(me + d),
            device_id_type=MESH,
        )

    coarse_round = [0]

    def coarse_apply(corr):
        slot = coarse_round[0] % 2
        coarse_round[0] += 1
        finish_sends("coarse", coarse_copy)
        cext[slot, pl.ds(reach * c1, c1), :] = corr
        cdiag, cv0, cv1, ch, mct = ctx["cdiag"], ctx["cv0"], ctx["cv1"], ctx["ch"], ctx["mct"]
        for k in by_distance:
            @pl.when(valid(me + offsets[k]))
            def _():
                coarse_copy(slot, k).start()
        bases = []
        for part in halves(corr):
            lower, upper = shifted(part)
            bases.append(cdiag * part + cv0 * lower + cv1 * upper)
        pending["coarse"] = slot
        for k in range(n_slots):
            @pl.when(valid(me - offsets[k]))
            def _():
                coarse_copy(slot, k).wait_recv()
        gathered = select(mct, cext[slot])
        totals = []
        for t, total in enumerate(bases):
            for n in range(n_ch):
                total = total + ch[n] * gathered[n * c1:(n + 1) * c1, t * LANES:(t + 1) * LANES]
            totals.append(total)
        return jnp.concatenate(totals, 1)

    peers = sum(valid(me + d).astype(jnp.int32) for d in offsets)

    def per_half(x, coeff, op):
        return jnp.concatenate([op(part, coeff) for part in halves(x)], 1)

    solution = per_half(OMEGA * rhs, inv_diag, lambda x, c: x * c)
    for cycle_index in range(CYCLES):
        for sweep_index in range(PRE):
            if cycle_index == 0 and sweep_index == 0:
                continue
            step = OMEGA * (rhs - fine_apply(solution))
            solution = solution + per_half(step, inv_diag, lambda x, c: x * c)
        residual = rhs - fine_apply(solution)
        weighted = per_half(residual, ctx["w"], lambda x, c: x * c)
        coarse_source = mm(ctx["at"], weighted)
        correction = per_half(OMEGA * coarse_source, ctx["inv_cdiag"], lambda x, c: x * c)
        for coarse_sweep_index in range(CSWEEPS - 1):
            step = OMEGA * (coarse_source - coarse_apply(correction))
            correction = correction + per_half(step, ctx["inv_cdiag"], lambda x, c: x * c)
        lifted = select(ctx["a"], correction)
        solution = solution + per_half(lifted, ctx["w"], lambda x, c: x * c)
        for sweep_index in range(POST):
            step = OMEGA * (rhs - fine_apply(solution))
            solution = solution + per_half(step, inv_diag, lambda x, c: x * c)
    finish_sends("fine", fine_copy)
    finish_sends("coarse", coarse_copy)
    for t, part in enumerate(halves(solution)):
        out_v[0, t] = jnp.transpose(part)[:layers]
    store = pltpu.make_async_copy(out_v, out_hbm, load_sem.at[len(loads)])
    store.start()
    store.wait()


def body(
    right_side,
    absorption,
    vertical,
    horizontal,
    neighbours,
    send_index,
    aggregate,
    weights,
    coarse_vertical,
    coarse_horizontal,
    coarse_neighbours,
    *,
    n_parts,
    n_grp,
):
    _, tracers, layers, columns = right_side.shape
    reach = send_index.shape[1] // 2
    width = send_index.shape[2]
    c1 = coarse_neighbours.shape[2]
    n_slots = 2 * reach

    args = (
        right_side,
        absorption,
        vertical,
        horizontal,
        weights,
        jnp.swapaxes(neighbours, 0, 1),
        send_index,
        aggregate,
        jnp.swapaxes(coarse_neighbours, 0, 1),
        jnp.swapaxes(coarse_vertical, 2, 3),
        jnp.swapaxes(coarse_horizontal, 2, 3),
    )
    ext_rows = columns + n_slots * width
    coarse_rows = ext_rows
    scratch = [pltpu.VMEM(x.shape, x.dtype) for x in args] + [
        pltpu.VMEM(right_side.shape, F32),
        pltpu.SemaphoreType.DMA((len(args) + 1,)),
        pltpu.VMEM((neighbours.shape[1] * columns, 2 * columns), BF16),
        pltpu.VMEM((neighbours.shape[1] * columns, 2 * n_slots * width), BF16),
        pltpu.VMEM((2, n_slots * width, tracers * LANES), F32),
        pltpu.VMEM((n_slots * width, tracers * LANES), F32),
        pltpu.VMEM((2, coarse_rows, tracers * LANES), F32),
        pltpu.SemaphoreType.DMA((n_slots,)),
        pltpu.SemaphoreType.DMA((2, n_slots)),
        pltpu.SemaphoreType.DMA((n_slots,)),
        pltpu.SemaphoreType.DMA((2, n_slots)),
    ]
    return pl.pallas_call(
        functools.partial(vcycle_kernel, n_parts, n_grp, reach, width),
        out_shape=jax.ShapeDtypeStruct(right_side.shape, F32),
        in_specs=[pl.BlockSpec(memory_space=pl.ANY)] * len(args),
        out_specs=pl.BlockSpec(memory_space=pl.ANY),
        scratch_shapes=scratch,
        compiler_params=pltpu.CompilerParams(collective_id=0, has_side_effects=True),
    )(*args)


def solution(mesh):
    placed = (
        P(("dom", "grp"), None, None, None),
        P(("dom", "grp"), None, None),
        P(("dom", "grp"), None, None, None),
        P(("dom", "grp"), None, None, None),
        P(("dom", "grp"), None, None),
        P(("dom", "grp"), None, None),
        P(("dom", "grp"), None),
        P(("dom", "grp"), None, None),
        P(("dom", "grp"), None, None, None),
        P(("dom", "grp"), None, None, None),
        P(("dom", "grp"), None, None),
    )
    n_grp = mesh.shape["grp"]
    n_parts = mesh.shape["dom"] * n_grp
    return jax.shard_map(
        functools.partial(body, n_parts=n_parts, n_grp=n_grp),
        mesh=mesh,
        in_specs=placed,
        out_specs=P(("dom", "grp"), None, None, None),
        check_vma=False,
    )
```
